128 devices in a mesh: row: 4 (over x), col: 32 (over z, y, core).
Axes of the slice: x: 4, y: 4, z: 4, core: 2. Of those that a mesh axis runs over, the one named last changes fastest.
Arguments:
- state: float32 [3, 32, 256, 256], P(None, 'row', 'col'), may hold values from -4 to 4
- acc_diag: float32 [3, 32, 256, 256], P(None, 'row', 'col'), may hold values from 1 to 2
- porosity: float32 [32, 256, 256], P('row', 'col'), may hold values from 0.1 to 0.3
- mobility: float32 [3, 32, 256, 256], P(None, 'row', 'col'), may hold values from 0.3 to 1.5
- trans_x: float32 [32, 256, 256], P('row', 'col'), may hold values from 0.5 to 2
- trans_y: float32 [32, 256, 256], P('row', 'col'), may hold values from 0.5 to 2
- trans_z: float32 [32, 256, 256], P('row', 'col'), may hold values from 0.05 to 0.5
- perf_cell: int32 [4, 32768], P('row', 'col'), may hold values from 0 to 16383
- perf_owner: int32 [4, 32768], P('row', 'col'), may hold values from 0 to 31, as said below
- perf_well: int32 [4, 32768], P('row', 'col'), may hold values from 0 to 15
- perf_index: float32 [4, 32768], P('row', 'col'), may hold values from 1 to 10
- perf_head: float32 [4, 32768], P('row', 'col'), may hold values from -3 to 3
- well_stiff: float32 [4, 512], P('row', 'col'), may hold values from 0.5 to 4
- well_drive: float32 [4, 512], P('row', 'col'), may hold values from -120 to 120
- coarse_inverse: float32 [128, 128], P('row'), may hold values from -1 to 2
Outputs:
- new_state: float32 [3, 32, 256, 256], P(None, 'row', 'col')
- residual: float32 [3, 32, 256, 256], P(None, 'row', 'col')
The draws below stay inside these ranges and needn't reach their ends.
Inputs may be any that keep to these rules, and one draw needn't show every extreme that they name: `perf_owner`: no device names one owner more than 64 times; in each row of devices one owner is named exactly 64 times by every device of the row.
All inputs are finite; a program needn't handle non-finite values.
Results may differ from the reference program's by a relative error of at most 0.0003.
Values sent between devices are 32-bit elements; how exact they have to be, the bound alone decides.
No kernel may reach another device: no remote copies, remote signals or barrier semaphores. Data moves between devices by JAX's collectives and lax.ppermute only.
A program may use at most 128 MiB of HBM per device.

```python
import math
import jax
import jax.numpy as jnp
from jax import lax

CX = 8
CY = 8
LZ = 256
WELLS_DEV = 16
NEWTON = 2
KRYLOV = 2
CAP = 64
PERF_DEV = 1024
WELLS = 2048
COARSE = 128
NX = 32
NY = 256
N_ROW = 4
N_COL = 32


def owner_list(device_key, special):
    others = jnp.arange((N_COL - 1) * CAP, dtype=jnp.int32) // CAP
    others = others + (others >= special).astype(jnp.int32)
    mixed = jax.random.permutation(jax.random.fold_in(device_key, 1), others)[:PERF_DEV - CAP]
    listed = jnp.concatenate([jnp.full((CAP,), special, jnp.int32), mixed])
    return jax.random.permutation(jax.random.fold_in(device_key, 2), listed)


def draw_perf_owner(key, part):
    specials = jax.random.randint(jax.random.fold_in(key, 5), (N_ROW, 1), 0, N_COL)
    specials = jnp.broadcast_to(specials, (N_ROW, N_COL)).reshape(-1).astype(jnp.int32)
    keys = jax.random.split(jax.random.fold_in(key, 9), N_ROW * N_COL)
    lists = jax.vmap(owner_list)(keys, specials)
    return lists.reshape(N_ROW, N_COL * PERF_DEV).astype(jnp.int32)


def draw_coarse_inverse(key, part):
    spread = jax.random.truncated_normal(jax.random.fold_in(key, 3), -4.0, 4.0, (COARSE, COARSE), jnp.float32)
    diagonal = jax.random.uniform(jax.random.fold_in(key, 4), (COARSE,), jnp.float32, 0.5, 1.5)
    return spread * (0.6 / math.sqrt(COARSE)) + jnp.diag(diagonal)


def plant(values, key, low, top_value):
    longest = values.shape.index(max(values.shape))
    spots = []
    for shift in (0, 1):
        where = [jax.random.randint(jax.random.fold_in(key, axis), (), 0, length) for axis, length in enumerate(values.shape)]
        where[longest] = (where[longest] + shift) % values.shape[longest]
        spots.append(tuple(where))
    return values.at[spots[0]].set(low).at[spots[1]].set(top_value)


def shard_levels(stream_key, extent, cuts, least, largest):
    loudness = 1.0
    for dim, parts in cuts:
        draws = jax.random.uniform(jax.random.fold_in(jax.random.fold_in(stream_key, 6), dim), (parts,), jnp.float32, least / len(cuts), largest / len(cuts))
        loudness = loudness * jnp.repeat(jnp.exp(draws), extent[dim] // parts).reshape((-1,) + (1,) * (len(extent) - 1 - dim))
    return loudness


def gaussian(own_key, dims, deviation, most, shards=(), kind=jnp.bfloat16):
    values = deviation * jax.random.normal(own_key, dims, jnp.float32)
    if shards:
        values = values * shard_levels(own_key, dims, shards, -0.22, 0.18)
    return jnp.clip(values, -most, most).astype(kind)


def setup_inputs(seed: int = 0) -> dict:
    streams_of = jax.random.split(jax.random.key(seed), 16)
    return {
        "state": gaussian(streams_of[0], (3, NX, NY, LZ), 1.0, 4.0, ((1, 4), (2, 32)), jnp.float32),
        "acc_diag": jnp.clip(1.0 + 1.0 * jax.random.uniform(streams_of[1], (3, NX, NY, LZ), jnp.float32) ** shard_levels(streams_of[1], (3, NX, NY, LZ), ((1, 4), (2, 32)), -0.2, 0.2), 1.0, 2.0),
        "porosity": jnp.clip(0.1 + 0.20000001043081284 * jax.random.uniform(streams_of[2], (NX, NY, LZ), jnp.float32) ** shard_levels(streams_of[2], (NX, NY, LZ), ((0, 4), (1, 32)), -0.2, 0.2), 0.1, 0.3),
        "mobility": jnp.clip(jnp.exp(math.log(1.5) - 1.60943787 * jax.random.uniform(streams_of[3], (3, NX, NY, LZ), jnp.float32) ** shard_levels(streams_of[3], (3, NX, NY, LZ), ((1, 4), (2, 32)), -0.2, 0.2)), 0.3, 1.5),
        "trans_x": jnp.clip(jnp.exp(math.log(2.0) - 1.3862944 * jax.random.uniform(streams_of[4], (NX, NY, LZ), jnp.float32) ** shard_levels(streams_of[4], (NX, NY, LZ), ((0, 4), (1, 32)), -0.2, 0.2)), 0.5, 2.0),
        "trans_y": jnp.clip(jnp.exp(math.log(2.0) - 1.3862944 * jax.random.uniform(streams_of[5], (NX, NY, LZ), jnp.float32) ** shard_levels(streams_of[5], (NX, NY, LZ), ((0, 4), (1, 32)), -0.2, 0.2)), 0.5, 2.0),
        "trans_z": jnp.clip(jnp.exp(math.log(0.5) - 2.3025851 * jax.random.uniform(streams_of[6], (NX, NY, LZ), jnp.float32) ** shard_levels(streams_of[6], (NX, NY, LZ), ((0, 4), (1, 32)), -0.2, 0.2)), 0.05, 0.5),
        "perf_cell": plant(jax.random.randint(streams_of[7], (N_ROW, N_COL * PERF_DEV), 0, CX * CY * LZ), jax.random.fold_in(streams_of[7], 1), 0, (CX * CY * LZ) - 1).astype(jnp.int32),
        "perf_owner": draw_perf_owner(jax.random.fold_in(streams_of[15], 71), 0),
        "perf_well": plant(jax.random.randint(streams_of[9], (N_ROW, N_COL * PERF_DEV), 0, WELLS_DEV), jax.random.fold_in(streams_of[9], 1), 0, WELLS_DEV - 1).astype(jnp.int32),
        "perf_index": jnp.clip(jnp.exp(math.log(10.0) - 2.3025851 * jax.random.uniform(streams_of[10], (N_ROW, N_COL * PERF_DEV), jnp.float32) ** shard_levels(streams_of[10], (N_ROW, N_COL * PERF_DEV), ((0, 4), (1, 32)), -0.2, 0.2)), 1.0, 10.0),
        "perf_head": gaussian(streams_of[11], (N_ROW, N_COL * PERF_DEV), 0.5, 3.0, ((0, 4), (1, 32)), jnp.float32),
        "well_stiff": jnp.clip(jnp.exp(math.log(4.0) - 2.0794415 * jax.random.uniform(streams_of[12], (N_ROW, N_COL * WELLS_DEV), jnp.float32) ** shard_levels(streams_of[12], (N_ROW, N_COL * WELLS_DEV), ((0, 4), (1, 32)), -0.2, 0.2)), 0.5, 4.0),
        "well_drive": gaussian(streams_of[13], (N_ROW, N_COL * WELLS_DEV), 20.0, 120.0, ((0, 4), (1, 32)), jnp.float32),
        "coarse_inverse": draw_coarse_inverse(jax.random.fold_in(streams_of[15], 71), 0),
    }


EXACT = lax.Precision.HIGHEST
COUPLING = ((0.0, 0.3, 0.2), (0.25, 0.0, 0.15), (0.2, 0.1, 0.0))

def smooth(x):
    return x + 0.5 * jnp.tanh(x)

def slope(x):
    bent = jnp.tanh(x)
    return 1.5 - 0.5 * bent * bent

def accumulate(state, acc_diag, porosity):
    shaped = smooth(state)
    result = []
    for k in range(3):
        total = acc_diag[k] * shaped[k]
        for j in range(3):
            if COUPLING[k][j] != 0.0:
                total = total + porosity * COUPLING[k][j] * shaped[j]
        result.append(total)
    return jnp.stack(result)

def mass_jacobian(slopes, acc_diag, porosity, vector):
    result = []
    for k in range(3):
        total = acc_diag[k] * slopes[k] * vector[k]
        for j in range(3):
            if COUPLING[k][j] != 0.0:
                total = total + porosity * COUPLING[k][j] * slopes[j] * vector[j]
        result.append(total)
    return jnp.stack(result)

def block_inverse(slopes, acc_diag, porosity, column):
    m = []
    for k in range(3):
        line = []
        for j in range(3):
            entry = porosity * COUPLING[k][j] * slopes[j]
            if j == k:
                entry = entry + acc_diag[k] * slopes[k]
            if j == 0:
                entry = entry + column[k]
            line.append(entry)
        m.append(line)
    cofactor = [[m[1][1] * m[2][2] - m[1][2] * m[2][1], m[1][2] * m[2][0] - m[1][0] * m[2][2], m[1][0] * m[2][1] - m[1][1] * m[2][0]], [m[0][2] * m[2][1] - m[0][1] * m[2][2], m[0][0] * m[2][2] - m[0][2] * m[2][0], m[0][1] * m[2][0] - m[0][0] * m[2][1]], [m[0][1] * m[1][2] - m[0][2] * m[1][1], m[0][2] * m[1][0] - m[0][0] * m[1][2], m[0][0] * m[1][1] - m[0][1] * m[1][0]]]
    determinant = m[0][0] * cofactor[0][0] + m[0][1] * cofactor[0][1] + m[0][2] * cofactor[0][2]
    reciprocal = 1.0 / determinant
    return [[cofactor[j][k] * reciprocal for j in range(3)] for k in range(3)]

def apply_inverse(inverse, vector):
    return jnp.stack([inverse[k][0] * vector[0] + inverse[k][1] * vector[1] + inverse[k][2] * vector[2] for k in range(3)])

def least_squares(hessenberg, beta):
    size = hessenberg.shape[1]
    gram = jnp.dot(hessenberg.T, hessenberg, precision=EXACT)
    target = beta * hessenberg[0]
    lower = {}
    for i in range(size):
        for j in range(i + 1):
            total = gram[i, j]
            for k in range(j):
                total = total - lower[i, k] * lower[j, k]
            lower[i, j] = jnp.sqrt(total) if i == j else total / lower[j, j]
    forward = []
    for i in range(size):
        total = target[i]
        for k in range(i):
            total = total - lower[i, k] * forward[k]
        forward.append(total / lower[i, i])
    backward = [None] * size
    for i in reversed(range(size)):
        total = forward[i]
        for k in range(i + 1, size):
            total = total - lower[k, i] * backward[k]
        backward[i] = total / lower[i, i]
    return backward

def shift_next(x, axis):
    rest = lax.slice_in_dim(x, 1, x.shape[axis], axis=axis)
    return jnp.concatenate([rest, jnp.zeros_like(lax.slice_in_dim(x, 0, 1, axis=axis))], axis)

def shift_prev(x, axis):
    rest = lax.slice_in_dim(x, 0, x.shape[axis] - 1, axis=axis)
    return jnp.concatenate([jnp.zeros_like(lax.slice_in_dim(x, 0, 1, axis=axis)), rest], axis)

def plus_faces(mobility, trans, axis):
    coef = trans * 0.5 * (mobility + shift_next(mobility, axis + 1))
    place = lax.broadcasted_iota(jnp.int32, trans.shape, axis)
    return jnp.where(place < trans.shape[axis] - 1, coef, 0.0)

def flux(field, faces):
    total = None
    for axis in range(3):
        plus = faces[axis]
        minus = shift_prev(plus, axis + 1)
        term = plus * (field - shift_next(field, axis)) + minus * (field - shift_prev(field, axis))
        total = term if total is None else total + term
    return total

def perforations(perf_cell, perf_owner, perf_well):
    local = perf_cell.reshape(N_ROW, N_COL, PERF_DEV)
    row_of = lax.broadcasted_iota(jnp.int32, local.shape, 0)
    col_of = lax.broadcasted_iota(jnp.int32, local.shape, 1)
    first = local // (CY * LZ)
    second = local // LZ % CY
    third = local % LZ
    cells = ((row_of * CX + first) * NY + col_of * CY + second) * LZ + third
    wells = (row_of * N_COL + perf_owner.reshape(local.shape)) * WELLS_DEV + perf_well.reshape(local.shape)
    return (cells.reshape(-1).astype(jnp.int32), wells.reshape(-1).astype(jnp.int32))

def reference(state, acc_diag, porosity, mobility, trans_x, trans_y, trans_z, perf_cell, perf_owner, perf_well, perf_index, perf_head, well_stiff, well_drive, coarse_inverse):
    cells, wells = perforations(perf_cell, perf_owner, perf_well)
    faces = [plus_faces(mobility, trans_x, 0), plus_faces(mobility, trans_y, 1), plus_faces(mobility, trans_z, 2)]
    column = None
    for axis in range(3):
        term = faces[axis] + shift_prev(faces[axis], axis + 1)
        column = term if column is None else column + term
    phase_index = perf_index.reshape(-1) * mobility.reshape(3, -1)[:, cells]
    total_index = phase_index[0] + phase_index[1] + phase_index[2]
    divisor = jax.ops.segment_sum(total_index, wells, num_segments=WELLS) + well_stiff.reshape(-1)
    head = perf_head.reshape(-1)
    drive = well_drive.reshape(-1)
    zero_head = jnp.zeros_like(head)
    zero_drive = jnp.zeros_like(drive)
    cell_count = NX * NY * LZ

    def to_cells(rates):
        return jnp.zeros((3, cell_count), jnp.float32).at[:, cells].add(rates).reshape(3, NX, NY, LZ)
    well_column = to_cells(phase_index)
    stored = accumulate(state, acc_diag, porosity)

    def well_rates(pressure, shift, push):
        base = pressure.reshape(-1)[cells] - shift
        bhp = (jax.ops.segment_sum(total_index * base, wells, num_segments=WELLS) + push) / divisor
        return to_cells(phase_index * (base - bhp[wells]))

    def residual(current):
        return accumulate(current, acc_diag, porosity) - stored + flux(current[0], faces) + well_rates(current[0], head, drive)

    def jacobian(slopes, vector):
        return mass_jacobian(slopes, acc_diag, porosity, vector) + flux(vector[0], faces) + well_rates(vector[0], zero_head, zero_drive)

    def precondition(slopes, inverse, vector):
        pressure_sum = vector[0] + vector[1] + vector[2]
        means = pressure_sum.reshape(N_ROW, CX, N_COL, CY, LZ).mean(axis=(1, 3, 4))
        ordered = means.T.reshape(-1)
        solved = jnp.dot(coarse_inverse, ordered, precision=EXACT)
        values = solved.reshape(N_COL, N_ROW).T
        field = jnp.broadcast_to(values[:, None, :, None, None], (N_ROW, CX, N_COL, CY, LZ)).reshape(NX, NY, LZ)
        zeros = jnp.zeros_like(field)
        coarse = jnp.stack([field, zeros, zeros])
        remain = vector - jacobian(slopes, coarse)
        return coarse + apply_inverse(inverse, remain)
    current = state
    for outer in range(NEWTON):
        slopes = slope(current)
        inverse = block_inverse(slopes, acc_diag, porosity, column + well_column)
        right_side = -residual(current)
        beta = jnp.sqrt(jnp.sum(right_side * right_side))
        basis = [right_side / beta]
        directions = []
        hessenberg = jnp.zeros((KRYLOV + 1, KRYLOV), jnp.float32)
        for j in range(KRYLOV):
            direction = precondition(slopes, inverse, basis[j])
            directions.append(direction)
            image = jacobian(slopes, direction)
            projections = jnp.stack([jnp.sum(image * basis[i]) for i in range(j + 1)])
            for i in range(j + 1):
                image = image - projections[i] * basis[i]
            norm_next = jnp.sqrt(jnp.sum(image * image))
            hessenberg = hessenberg.at[:j + 1, j].set(projections).at[j + 1, j].set(norm_next)
            if j + 1 < KRYLOV:
                basis.append(image / norm_next)
        weights = least_squares(hessenberg, beta)
        for j in range(KRYLOV):
            current = current + weights[j] * directions[j]
    return (current, residual(current))
```

```python
import jax
import jax.numpy as jnp
from jax import lax
from jax.experimental import pallas as pl
from jax.experimental.pallas import tpu as pltpu
from jax.sharding import PartitionSpec as P

NEWTON = 2
WELLS_DEV = 16
EXACT = lax.Precision.HIGHEST
COUPLING = ((0.0, 0.3, 0.2), (0.25, 0.0, 0.15), (0.2, 0.1, 0.0))
ROWS = 4
COLS = 32
DEVS = ROWS * COLS
CELLS = 8 * 8 * 256
F32 = jnp.float32
BF16 = jnp.bfloat16
PARAMS = pltpu.CompilerParams(vmem_limit_bytes=24 << 20)


def call(body, outs, *args, scratch=()):
    return pl.pallas_call(
        body,
        out_shape=[jax.ShapeDtypeStruct(s, t) for s, t in outs],
        scratch_shapes=list(scratch),
        compiler_params=PARAMS,
    )(*args)


def iota(shape, dim):
    return lax.broadcasted_iota(jnp.int32, shape, dim)


def split(value):
    high = value.astype(BF16)
    low = (value - high.astype(F32)).astype(BF16)
    return jnp.concatenate([high, low], 0)


def joined(pair):
    half = pair.shape[0] // 2
    return pair[:half] + pair[half:]


def nn(a, b):
    return lax.dot_general(a, b, (((1,), (0,)), ((), ())), preferred_element_type=F32)


def nt(a, b):
    return lax.dot_general(a, b, (((1,), (1,)), ((), ())), preferred_element_type=F32)


def to_wells(field, layer, place, index, low_mark, high_mark):
    picked = joined(nn(split(field), layer))
    value = index * jnp.sum(picked * place, 0, keepdims=True)
    return joined(nt(split(high_mark * value), low_mark))


def to_cells(per_well, layer, place, index, low_mark, high_mark):
    spread = joined(nn(split(per_well), low_mark))
    value = index * jnp.sum(spread * high_mark, 0, keepdims=True)
    return joined(nt(split(place * value), layer))


def write_plane(ref, base, plane):
    ref[base : base + 8, :] = plane[:, :128]
    ref[base + 8 : base + 16, :] = plane[:, 128:]


def read_plane(ref, base):
    return jnp.concatenate([ref[base : base + 8, :], ref[base + 8 : base + 16, :]], 1)


def pack_body(state, mobility, trans_x, trans_y, coarse, up_x, down_x, up_y, down_y):
    for k in range(3):
        write_plane(up_x, 16 * k, mobility[k, 7])
        write_plane(down_x, 16 * k, mobility[k, 0])
        write_plane(up_y, 16 * k, mobility[k, :, 7, :])
        write_plane(down_y, 16 * k, mobility[k, :, 0, :])
    write_plane(up_x, 48, state[0, 7])
    write_plane(down_x, 48, state[0, 0])
    write_plane(up_y, 48, state[0, :, 7, :])
    write_plane(down_y, 48, state[0, :, 0, :])
    write_plane(up_x, 64, trans_x[7])
    write_plane(up_y, 64, trans_y[:, 7, :])
    up_x[80:112, :] = coarse[...]
    down_x[64:96, :] = coarse[...]


def perforation_body(
    spot,
    state,
    mobility,
    cell,
    owner,
    well,
    index,
    head,
    stiff,
    drive,
    layer,
    place,
    low_mark,
    high_mark,
    fields,
    outgoing,
):
    count = cell.shape[1]
    layer[...] = jnp.where(iota((256, count), 0) == (cell[...] & 255), 1.0, 0.0).astype(BF16)
    place[...] = jnp.where(iota((64, count), 0) == (cell[...] >> 8), 1.0, 0.0)
    label = owner[...] * WELLS_DEV + well[...]
    low_mark[...] = jnp.where(iota((128, count), 0) == (label & 127), 1.0, 0.0).astype(BF16)
    high_mark[...] = jnp.where(iota((8, count), 0) == (label >> 7), 1.0, 0.0)
    both = jnp.concatenate([place[...] * index[...], place[...] * (index[...] * head[...])], 0)
    fields[...] = joined(nt(split(both), layer[...])).reshape(2, 64, 256)
    total = (mobility[0] + mobility[1] + mobility[2]).reshape(64, 256)
    pressure = total * state[0].reshape(64, 256)
    pair = split(jnp.concatenate([total, pressure], 0))
    picked = joined(nn(pair, layer[...])) * jnp.concatenate([place[...], place[...]], 0)
    base = index[...] * jnp.sum(picked[:64], 0, keepdims=True)
    terms = index[...] * jnp.sum(picked[64:], 0, keepdims=True) - base * head[...]
    mark = high_mark[...]
    sums = joined(nt(split(jnp.concatenate([mark * base, mark * terms], 0)), low_mark[...]))
    me = spot[1]
    tile = jnp.where(iota((WELLS_DEV, 128), 1) % WELLS_DEV == iota((WELLS_DEV, 128), 0), 1.0, 0.0)
    lines = jnp.concatenate([stiff[...], drive[...], jnp.zeros((6, WELLS_DEV), F32)], 0)
    lines = jnp.dot(lines, tile, precision=EXACT, preferred_element_type=F32)
    mine = (iota((8, 128), 1) // WELLS_DEV == me % 8) & (iota((8, 128), 0) % 4 == me // 8)
    upper = iota((8, 128), 0) < 4
    extra = jnp.where(mine, jnp.where(upper, lines[1:2], lines[0:1]), 0.0)
    second = jnp.where(upper, sums[8:], 0.0) + extra
    for other in range(COLS):
        outgoing[other, 0:8, :] = sums[:8]
        outgoing[other, 8:16, :] = second


def neighbours(planes, x, x_low, x_high, y_low, y_high):
    plane = planes[x]
    line = iota((8, 256), 0)
    return (
        planes[x + 1] if x < 7 else x_high,
        planes[x - 1] if x > 0 else x_low,
        jnp.where(line == 7, y_high[x : x + 1], pltpu.roll(plane, 7, 0)),
        jnp.where(line == 0, y_low[x : x + 1], pltpu.roll(plane, 1, 0)),
        pltpu.roll(plane, 255, 1),
        pltpu.roll(plane, 1, 1),
    )


def gathered(faces, k, x, around):
    total = faces[0, k, x] * around[0]
    for side in range(1, 6):
        total = total + faces[side, k, x] * around[side]
    return total


def coupled(acc_diag, porosity, k, x, terms):
    total = acc_diag[k, x] * terms[k]
    mixed = None
    for j in range(3):
        if COUPLING[k][j] != 0.0:
            part = COUPLING[k][j] * terms[j]
            mixed = part if mixed is None else mixed + part
    return total + porosity[x] * mixed


def invert(slopes, acc_diag, porosity, diagonal, x, inverse):
    m = []
    for k in range(3):
        line = []
        for j in range(3):
            if j == k:
                entry = acc_diag[k, x] * slopes[k]
            else:
                entry = porosity[x] * COUPLING[k][j] * slopes[j]
            if j == 0:
                entry = entry + diagonal[k, x]
            line.append(entry)
        m.append(line)
    cofactor = [
        [
            m[1][1] * m[2][2] - m[1][2] * m[2][1],
            m[1][2] * m[2][0] - m[1][0] * m[2][2],
            m[1][0] * m[2][1] - m[1][1] * m[2][0],
        ],
        [
            m[0][2] * m[2][1] - m[0][1] * m[2][2],
            m[0][0] * m[2][2] - m[0][2] * m[2][0],
            m[0][1] * m[2][0] - m[0][0] * m[2][1],
        ],
        [
            m[0][1] * m[1][2] - m[0][2] * m[1][1],
            m[0][2] * m[1][0] - m[0][0] * m[1][2],
            m[0][0] * m[1][1] - m[0][1] * m[1][0],
        ],
    ]
    determinant = m[0][0] * cofactor[0][0] + m[0][1] * cofactor[0][1] + m[0][2] * cofactor[0][2]
    reciprocal = 1.0 / determinant
    for k in range(3):
        for j in range(3):
            inverse[k, j, x] = cofactor[j][k] * reciprocal


def total_of(plane):
    return jnp.sum(jnp.sum(plane, 1, keepdims=True), 0, keepdims=True)


def broadcast_rows(outgoing, mean, dots=()):
    lane = iota((1, 128), 1)
    row = jnp.broadcast_to(mean, (1, 128))
    for n, dot in enumerate(dots):
        row = jnp.where(lane == 127 - n, dot, row)
    outgoing[...] = jnp.broadcast_to(row, (DEVS, 128))


def start_body(
    spot,
    state,
    acc_diag,
    porosity,
    mobility,
    trans_x,
    trans_y,
    trans_z,
    from_low_x,
    from_high_x,
    far,
    coarse,
    from_low_y,
    from_high_y,
    arrived,
    fields,
    layer,
    place,
    low_mark,
    high_mark,
    index,
    faces,
    diagonal,
    inverse,
    right,
    divisor,
    solve,
    outgoing,
    whole,
):
    row = spot[0]
    col = spot[1]
    for shift, source in ((0, coarse), (1, from_low_x.at[80:112]), (2, far), (3, from_high_x.at[64:96])):
        start = pl.multiple_of(((row - shift + 4) % 4) * 32, 32)
        whole[pl.ds(start, 32), :] = source[...]
    order = iota((DEVS, DEVS), 0)
    pick = jnp.where(iota((DEVS, DEVS), 1) == (order % COLS) * ROWS + order // COLS, 1.0, 0.0)
    part = jnp.dot(pick, whole[...], precision=EXACT, preferred_element_type=F32)
    solve[...] = lax.dot_general(
        part, pick, (((1,), (1,)), ((), ())), precision=EXACT, preferred_element_type=F32
    )
    totals = jnp.zeros((8, 128), F32)
    others = jnp.zeros((8, 128), F32)
    for other in range(COLS):
        totals = totals + arrived[other, 0:8, :]
        others = others + arrived[other, 8:16, :]
    upper = iota((8, 128), 0) < 4
    div = jnp.where(upper, totals + pltpu.roll(others, 4, 0), 1.0)
    divisor[...] = div
    hole = jnp.where(upper, others, 0.0) / div
    back = to_cells(hole, layer[...], place[...], index[...], low_mark[...], high_mark[...])
    low_x = jnp.where(row > 0, 1.0, 0.0)
    high_x = jnp.where(row < ROWS - 1, 1.0, 0.0)
    low_y = jnp.where(col > 0, 1.0, 0.0)
    high_y = jnp.where(col < COLS - 1, 1.0, 0.0)
    lane = iota((8, 256), 1)
    line = iota((8, 256), 0)
    t_low_x = read_plane(from_low_x, 64) * low_x
    t_low_y = read_plane(from_low_y, 64) * low_y
    for k in range(3):
        m_low_x = read_plane(from_low_x, 16 * k)
        m_high_x = read_plane(from_high_x, 16 * k)
        m_low_y = read_plane(from_low_y, 16 * k)
        m_high_y = read_plane(from_high_y, 16 * k)
        previous = t_low_x * 0.5 * (m_low_x + mobility[k, 0])
        planes = [mobility[k, x] for x in range(8)]
        for x in range(8):
            here = planes[x]
            around = neighbours(planes, x, m_low_x, m_high_x, m_low_y, m_high_y)
            tx = trans_x[x] if x < 7 else trans_x[x] * high_x
            ahead = tx * 0.5 * (here + around[0])
            faces[0, k, x] = ahead
            faces[1, k, x] = previous
            total = ahead + previous
            previous = ahead
            ty = jnp.where(line == 7, trans_y[x] * high_y, trans_y[x])
            ahead_y = ty * 0.5 * (here + around[2])
            entering = t_low_y[x : x + 1] * 0.5 * (m_low_y[x : x + 1] + here[0:1])
            behind_y = jnp.where(line == 0, entering, pltpu.roll(ahead_y, 1, 0))
            faces[2, k, x] = ahead_y
            faces[3, k, x] = behind_y
            total = total + (ahead_y + behind_y)
            ahead_z = jnp.where(lane < 255, trans_z[x] * 0.5 * (here + around[4]), 0.0)
            behind_z = pltpu.roll(ahead_z, 1, 1)
            faces[4, k, x] = ahead_z
            faces[5, k, x] = behind_z
            diagonal[k, x] = total + (ahead_z + behind_z) + here * fields[0, x * 8 : x * 8 + 8, :]
    halo = (
        read_plane(from_low_x, 48),
        read_plane(from_high_x, 48),
        read_plane(from_low_y, 48),
        read_plane(from_high_y, 48),
    )
    planes = [state[0, x] for x in range(8)]
    mean = jnp.zeros((8, 256), F32)
    for x in range(8):
        around = neighbours(planes, x, *halo)
        source = fields[1, x * 8 : x * 8 + 8, :] + back[x * 8 : x * 8 + 8]
        for k in range(3):
            value = (
                gathered(faces, k, x, around) + mobility[k, x] * source - diagonal[k, x] * planes[x]
            )
            right[k, x] = value
            mean = mean + value
        slopes = []
        for k in range(3):
            bent = jnp.tanh(state[k, x])
            slopes.append(1.5 - 0.5 * bent * bent)
        invert(slopes, acc_diag, porosity, diagonal, x, inverse)
    broadcast_rows(outgoing, total_of(mean) * (1.0 / CELLS))


def direction_parts(
    spot,
    coarse_x,
    basis,
    mobility,
    faces,
    inverse,
    divisor,
    arrived,
    layer,
    place,
    low_mark,
    high_mark,
    index,
    direction,
    to_high,
    to_low,
    outgoing,
    swept,
):
    row = spot[0]
    col = spot[1]
    me = row * COLS + col

    def entry(place_of):
        return coarse_x[pl.ds(place_of, 1), :]

    def wide(value):
        return jnp.broadcast_to(jnp.concatenate([value, value], 1), (8, 256))

    own = wide(entry(me))
    x_high = wide(entry(jnp.minimum(row + 1, ROWS - 1) * COLS + col))
    x_low = wide(entry(jnp.maximum(row - 1, 0) * COLS + col))
    y_high = wide(entry(row * COLS + jnp.minimum(col + 1, COLS - 1)))
    y_low = wide(entry(row * COLS + jnp.maximum(col - 1, 0)))
    sums = jnp.zeros((8, 128), F32)
    for other in range(COLS):
        sums = sums + entry(row * COLS + other) * arrived[other, 0:8, :]
    back = to_cells(
        sums / divisor[...], layer[...], place[...], index[...], low_mark[...], high_mark[...]
    )
    line = iota((8, 256), 0)
    up_y = jnp.where(line == 7, y_high, own)
    down_y = jnp.where(line == 0, y_low, own)
    kept = []
    weighted = []
    for x in range(8):
        around = (
            own if x < 7 else x_high,
            own if x > 0 else x_low,
            up_y,
            down_y,
            own,
            own,
        )
        vector = [
            basis(k, x)
            + gathered(faces, k, x, around)
            + mobility[k, x] * back[x * 8 : x * 8 + 8]
            for k in range(3)
        ]
        for k in range(3):
            value = (
                inverse[k, 0, x] * vector[0]
                + inverse[k, 1, x] * vector[1]
                + inverse[k, 2, x] * vector[2]
            )
            direction[k, x] = value
            if k == 0:
                kept.append(value - own)
        weighted.append(kept[x] * (mobility[0, x] + mobility[1, x] + mobility[2, x]))
    for x in range(8):
        swept[x] = kept[x]
    field = jnp.concatenate(weighted, 0)
    local = to_wells(field, layer[...], place[...], index[...], low_mark[...], high_mark[...])
    to_high[...] = kept[7]
    to_low[...] = kept[0]
    last = swept[:, 7, :]
    first = swept[:, 0, :]
    for other in range(COLS):
        outgoing[other, 0:8, :] = local
        send = jnp.where(other < col, first, last)
        outgoing[other, 8:16, :] = send[:, :128]
        outgoing[other, 16:24, :] = send[:, 128:]


def coarse_solve(solve, received, coarse_x):
    means = jnp.broadcast_to(received, (DEVS, 128))
    coarse_x[...] = jnp.dot(solve[...], means, precision=EXACT, preferred_element_type=F32)


def first_body(spot, solve, received, right, *rest):
    *rest, coarse_x = rest
    coarse_solve(solve, received[:, 0:1], coarse_x)
    direction_parts(spot, coarse_x, lambda k, x: right[k, x], *rest)


def second_body(spot, solve, received, met, right, image, *rest):
    *rest, basis, coarse_x = rest
    sums = jnp.sum(met[...], 0, keepdims=True)
    scale = sums[:, 127:128] / sums[:, 126:127]
    coarse_solve(solve, met[:, 0:1] - scale * received[:, 0:1], coarse_x)
    for k in range(3):
        for x in range(8):
            basis[k, x] = image[k, x] - scale * right[k, x]
    direction_parts(spot, coarse_x, lambda k, x: basis[k, x], *rest)


def image_planes(
    spot,
    basis,
    swept,
    from_low,
    from_high,
    came,
    mobility,
    faces,
    divisor,
    layer,
    place,
    low_mark,
    high_mark,
    index,
):
    col = spot[1]
    sums = jnp.zeros((8, 128), F32)
    for other in range(COLS):
        sums = sums + came[other, 0:8, :]
    back = to_cells(
        sums / divisor[...], layer[...], place[...], index[...], low_mark[...], high_mark[...]
    )
    below = jnp.maximum(col - 1, 0)
    above = jnp.minimum(col + 1, COLS - 1)
    y_low = jnp.concatenate([came[below, 8:16, :], came[below, 16:24, :]], 1)
    y_high = jnp.concatenate([came[above, 8:16, :], came[above, 16:24, :]], 1)
    planes = [swept[x] for x in range(8)]
    for x in range(8):
        around = neighbours(planes, x, from_low[...], from_high[...], y_low, y_high)
        for k in range(3):
            yield (
                k,
                x,
                basis[k, x]
                - gathered(faces, k, x, around)
                - mobility[k, x] * back[x * 8 : x * 8 + 8],
            )


def first_image_body(spot, right, *rest):
    *rest, image, outgoing = rest
    mean = jnp.zeros((8, 256), F32)
    along = jnp.zeros((8, 256), F32)
    square = jnp.zeros((8, 256), F32)
    for k, x, value in image_planes(spot, right, *rest):
        image[k, x] = value
        mean = mean + value
        along = along + value * right[k, x]
        square = square + right[k, x] * right[k, x]
    broadcast_rows(outgoing, total_of(mean) * (1.0 / CELLS), (total_of(along), total_of(square)))


def second_image_body(spot, right, first_image, basis, *rest):
    *rest, image, outgoing = rest
    totals = [jnp.zeros((8, 256), F32) for _ in range(5)]
    for k, x, value in image_planes(spot, basis, *rest):
        image[k, x] = value
        one = first_image[k, x]
        goal = right[k, x]
        for n, term in enumerate((one * one, one * value, value * value, one * goal, value * goal)):
            totals[n] = totals[n] + term
    broadcast_rows(outgoing, jnp.zeros((1, 1), F32), [total_of(t) for t in totals])


def update_body(last, *refs):
    (
        met,
        current,
        acc_diag,
        porosity,
        diagonal,
        right,
        first_image,
        second_image,
        first_direction,
        second_direction,
        *outs,
    ) = refs
    sums = jnp.sum(met[...], 0, keepdims=True)
    g00, g01, g11, t0, t1 = [sums[:, 127 - n : 128 - n] for n in range(5)]
    l00 = jnp.sqrt(g00)
    l10 = g01 / l00
    l11 = jnp.sqrt(g11 - l10 * l10)
    f0 = t0 / l00
    f1 = (t1 - l10 * f0) / l11
    y1 = f1 / l11
    y0 = (f0 - l10 * y1) / l00
    if last:
        fresh, residual = outs
    else:
        fresh, residual, inverse, outgoing = outs
    mean = jnp.zeros((8, 256), F32)
    for x in range(8):
        remainder = []
        slopes = []
        for k in range(3):
            old = current[k, x]
            step = y0 * first_direction[k, x] + y1 * second_direction[k, x]
            new = old + step
            fresh[k, x] = new
            before = jnp.tanh(old)
            after = jnp.tanh(new)
            remainder.append(0.5 * ((after - before) - (1.0 - before * before) * step))
            slopes.append(1.5 - 0.5 * after * after)
        for k in range(3):
            value = (
                right[k, x]
                - y0 * first_image[k, x]
                - y1 * second_image[k, x]
                - coupled(acc_diag, porosity, k, x, remainder)
            )
            residual[k, x] = -value if last else value
            mean = mean + value
        if not last:
            invert(slopes, acc_diag, porosity, diagonal, x, inverse)
    if not last:
        broadcast_rows(outgoing, total_of(mean) * (1.0 / CELLS))


def per_device(
    state,
    acc_diag,
    porosity,
    mobility,
    trans_x,
    trans_y,
    trans_z,
    perf_cell,
    perf_owner,
    perf_well,
    perf_index,
    perf_head,
    well_stiff,
    well_drive,
    coarse_inverse,
):
    spot = jnp.stack([lax.axis_index("row"), lax.axis_index("col")]).astype(jnp.int32)
    field = (8, 8, 256)
    triple = (3, *field)

    def ring(value, axis, count, shift):
        return lax.ppermute(value, axis, [(i, (i + shift) % count) for i in range(count)])

    def run(body, outs, *args, scratch=()):
        specs = [pl.BlockSpec(memory_space=pltpu.SMEM)]
        specs += [pl.BlockSpec(memory_space=pltpu.VMEM)] * (len(args) - 1)
        return pl.pallas_call(
            body,
            out_shape=[jax.ShapeDtypeStruct(s, t) for s, t in outs],
            in_specs=specs,
            out_specs=[pl.BlockSpec(memory_space=pltpu.VMEM)] * len(outs),
            scratch_shapes=list(scratch),
            compiler_params=PARAMS,
        )(*args)

    up_x, down_x, up_y, down_y = call(
        pack_body,
        [((112, 128), F32), ((96, 128), F32), ((80, 128), F32), ((64, 128), F32)],
        state,
        mobility,
        trans_x,
        trans_y,
        coarse_inverse,
    )
    from_low_x = ring(up_x, "row", ROWS, 1)
    from_high_x = ring(down_x, "row", ROWS, -1)
    far = ring(coarse_inverse, "row", ROWS, 2)
    from_low_y = ring(up_y, "col", COLS, 1)
    from_high_y = ring(down_y, "col", COLS, -1)
    count = perf_cell.shape[1]
    layer, place, low_mark, high_mark, fields, outgoing = run(
        perforation_body,
        [
            ((256, count), BF16),
            ((64, count), F32),
            ((128, count), BF16),
            ((8, count), F32),
            ((2, 64, 256), F32),
            ((COLS, 16, 128), F32),
        ],
        spot,
        state,
        mobility,
        perf_cell,
        perf_owner,
        perf_well,
        perf_index,
        perf_head,
        well_stiff,
        well_drive,
    )
    marks = (layer, place, low_mark, high_mark, perf_index)

    def swap_cols(value):
        return lax.all_to_all(value, "col", 0, 0, tiled=True)

    def swap_all(value):
        return lax.all_to_all(value, ("row", "col"), 0, 0, tiled=True)

    arrived = swap_cols(outgoing)
    faces, diagonal, inverse, right, divisor, solve, outgoing = run(
        start_body,
        [
            ((6, *triple), F32),
            (triple, F32),
            ((3, *triple), F32),
            (triple, F32),
            ((8, 128), F32),
            ((DEVS, DEVS), F32),
            ((DEVS, 128), F32),
        ],
        spot,
        state,
        acc_diag,
        porosity,
        mobility,
        trans_x,
        trans_y,
        trans_z,
        from_low_x,
        from_high_x,
        far,
        coarse_inverse,
        from_low_y,
        from_high_y,
        arrived,
        fields,
        *marks,
        scratch=[pltpu.VMEM((DEVS, DEVS), F32)],
    )
    current = state
    plane = (8, 256)
    sends = [(triple, F32), (plane, F32), (plane, F32), ((COLS, 24, 128), F32), (field, F32)]
    coarse_x = pltpu.VMEM((DEVS, 128), F32)

    def exchange(to_high, to_low, outgoing):
        return (
            ring(to_high, "row", ROWS, 1),
            ring(to_low, "row", ROWS, -1),
            swap_cols(outgoing),
        )

    for outer in range(NEWTON):
        received = swap_all(outgoing)
        first_direction, to_high, to_low, outgoing, swept = run(
            first_body,
            sends,
            spot,
            solve,
            received,
            right,
            mobility,
            faces,
            inverse,
            divisor,
            arrived,
            *marks,
            scratch=[coarse_x],
        )
        first_image, outgoing = run(
            first_image_body,
            [(triple, F32), ((DEVS, 128), F32)],
            spot,
            right,
            swept,
            *exchange(to_high, to_low, outgoing),
            mobility,
            faces,
            divisor,
            *marks,
        )
        met = swap_all(outgoing)
        second_direction, to_high, to_low, outgoing, swept, basis = run(
            second_body,
            [*sends, (triple, F32)],
            spot,
            solve,
            received,
            met,
            right,
            first_image,
            mobility,
            faces,
            inverse,
            divisor,
            arrived,
            *marks,
            scratch=[coarse_x],
        )
        second_image, outgoing = run(
            second_image_body,
            [(triple, F32), ((DEVS, 128), F32)],
            spot,
            right,
            first_image,
            basis,
            swept,
            *exchange(to_high, to_low, outgoing),
            mobility,
            faces,
            divisor,
            *marks,
        )
        met = swap_all(outgoing)
        last = outer == NEWTON - 1
        outs = [(triple, F32), (triple, F32)]
        if not last:
            outs += [((3, *triple), F32), ((DEVS, 128), F32)]
        results = call(
            lambda *refs: update_body(last, *refs),
            outs,
            met,
            current,
            acc_diag,
            porosity,
            diagonal,
            right,
            first_image,
            second_image,
            first_direction,
            second_direction,
        )
        if last:
            return tuple(results)
        current, right, inverse, outgoing = results


def solution(mesh):
    in_specs = (
        P(None, "row", "col", None),
        P(None, "row", "col", None),
        P("row", "col", None),
        P(None, "row", "col", None),
        P("row", "col", None),
        P("row", "col", None),
        P("row", "col", None),
        P("row", "col"),
        P("row", "col"),
        P("row", "col"),
        P("row", "col"),
        P("row", "col"),
        P("row", "col"),
        P("row", "col"),
        P("row", None),
    )
    out_specs = (P(None, "row", "col", None), P(None, "row", "col", None))
    return jax.shard_map(
        per_device, mesh=mesh, in_specs=in_specs, out_specs=out_specs, check_vma=False
    )
```

```python
import jax
import jax.numpy as jnp
from jax import lax
from jax.experimental import pallas as pl
from jax.experimental.pallas import tpu as pltpu
from jax.sharding import PartitionSpec as P

NEWTON = 2
WELLS_DEV = 16
EXACT = lax.Precision.HIGHEST
COUPLING = ((0.0, 0.3, 0.2), (0.25, 0.0, 0.15), (0.2, 0.1, 0.0))
ROWS = 4
COLS = 32
DEVS = ROWS * COLS
CELLS = 8 * 8 * 256
F32 = jnp.float32
BF16 = jnp.bfloat16
ROOM = 24 << 20
FIRST_ROOM = 66_700_000
START_ROOM = 64_100_000


def iota(shape, dim):
    return lax.broadcasted_iota(jnp.int32, shape, dim)


def split(value):
    high = value.astype(BF16)
    low = (value - high.astype(F32)).astype(BF16)
    return jnp.concatenate([high, low], 0)


def joined(pair):
    half = pair.shape[0] // 2
    return pair[:half] + pair[half:]


def nn(a, b):
    return lax.dot_general(a, b, (((1,), (0,)), ((), ())), preferred_element_type=F32)


def nt(a, b):
    return lax.dot_general(a, b, (((1,), (1,)), ((), ())), preferred_element_type=F32)


def marks_of(cell, label):
    count = cell.shape[1]
    layer = jnp.where(iota((256, count), 0) == (cell[...] & 255), 1.0, 0.0).astype(BF16)
    place = jnp.where(iota((64, count), 0) == (cell[...] >> 8), 1.0, 0.0)
    low_mark = jnp.where(iota((128, count), 0) == (label[...] & 127), 1.0, 0.0).astype(BF16)
    high_mark = jnp.where(iota((8, count), 0) == (label[...] >> 7), 1.0, 0.0)
    return layer, place, low_mark, high_mark


def to_wells(field, index, marks):
    layer, place, low_mark, high_mark = marks
    picked = joined(nn(split(field), layer))
    value = index[...] * jnp.sum(picked * place, 0, keepdims=True)
    return joined(nt(split(high_mark * value), low_mark))


def to_cells(per_well, index, marks):
    layer, place, low_mark, high_mark = marks
    spread = joined(nn(split(per_well), low_mark))
    value = index[...] * jnp.sum(spread * high_mark, 0, keepdims=True)
    return joined(nt(split(place * value), layer))


def write_plane(ref, base, plane):
    ref[base : base + 8, :] = plane[:, :128]
    ref[base + 8 : base + 16, :] = plane[:, 128:]


def read_plane(ref, base):
    return jnp.concatenate([ref[base : base + 8, :], ref[base + 8 : base + 16, :]], 1)


def fetch(pairs, sems):
    copies = [
        pltpu.make_async_copy(source, target, sems.at[n]) for n, (source, target) in enumerate(pairs)
    ]
    for copy in copies:
        copy.start()
    return copies


def prepare_body(
    state,
    mobility,
    trans_x,
    trans_y,
    cell_in,
    owner_in,
    well_in,
    index_in,
    head_in,
    stiff_in,
    drive_in,
    up_x,
    down_x,
    up_y,
    down_y,
    cell,
    label,
    index,
    fields,
    sums,
    pressure,
    carried,
    along_x,
    along_y,
    owner,
    well,
    head,
    stiff,
    drive,
    sems,
):
    copies = fetch(
        (
            (cell_in, cell),
            (owner_in, owner),
            (well_in, well),
            (index_in, index),
            (head_in, head),
            (stiff_in, stiff),
            (drive_in, drive),
            (mobility, carried),
            (state.at[0], pressure),
            (trans_x.at[7], along_x),
            (trans_y, along_y),
        ),
        sems,
    )
    for copy in copies:
        copy.wait()
    label[...] = owner[...] * WELLS_DEV + well[...]
    layer, place, low_mark, high_mark = marks_of(cell, label)
    both = jnp.concatenate([place * index[...], place * (index[...] * head[...])], 0)
    fields[...] = joined(nt(split(both), layer)).reshape(2, 64, 256)
    for k in range(3):
        write_plane(up_x, 16 * k, carried[k, 7])
        write_plane(down_x, 16 * k, carried[k, 0])
        write_plane(up_y, 16 * k, carried[k, :, 7, :])
        write_plane(down_y, 16 * k, carried[k, :, 0, :])
    write_plane(up_x, 48, pressure[7])
    write_plane(down_x, 48, pressure[0])
    write_plane(up_y, 48, pressure[:, 7, :])
    write_plane(down_y, 48, pressure[:, 0, :])
    write_plane(up_x, 64, along_x[...])
    write_plane(up_y, 64, along_y[:, 7, :])
    total = (carried[0] + carried[1] + carried[2]).reshape(64, 256)
    pair = split(jnp.concatenate([total, total * pressure[...].reshape(64, 256)], 0))
    picked = joined(nn(pair, layer)) * jnp.concatenate([place, place], 0)
    base = index[...] * jnp.sum(picked[:64], 0, keepdims=True)
    terms = index[...] * jnp.sum(picked[64:], 0, keepdims=True) - base * head[...]
    local = joined(nt(split(jnp.concatenate([high_mark * base, high_mark * terms], 0)), low_mark))
    me = lax.axis_index("col")
    tile = jnp.where(iota((WELLS_DEV, 128), 1) % WELLS_DEV == iota((WELLS_DEV, 128), 0), 1.0, 0.0)
    lines = jnp.concatenate([stiff[...], drive[...], jnp.zeros((6, WELLS_DEV), F32)], 0)
    lines = jnp.dot(lines, tile, precision=EXACT, preferred_element_type=F32)
    mine = (iota((8, 128), 1) // WELLS_DEV == me % 8) & (iota((8, 128), 0) % 4 == me // 8)
    upper = iota((8, 128), 0) < 4
    extra = jnp.where(mine, jnp.where(upper, lines[1:2], lines[0:1]), 0.0)
    sums[0:8, :] = local[:8]
    sums[8:16, :] = jnp.where(upper, local[8:], 0.0) + extra


def neighbours(planes, x, x_low, x_high, y_low, y_high):
    plane = planes[x]
    line = iota((8, 256), 0)
    return (
        planes[x + 1] if x < 7 else x_high,
        planes[x - 1] if x > 0 else x_low,
        jnp.where(line == 7, y_high[x : x + 1], pltpu.roll(plane, 7, 0)),
        jnp.where(line == 0, y_low[x : x + 1], pltpu.roll(plane, 1, 0)),
        pltpu.roll(plane, 255, 1),
    )


def gathered(faces, k, x, plane, around):
    face_x, face_y, face_z = faces
    ahead = face_z[k, x]
    return (
        face_x[k, x + 1] * around[0]
        + face_x[k, x] * around[1]
        + (face_y[0, k, x] * around[2] + face_y[1, k, x] * around[3])
        + (ahead * around[4] + pltpu.roll(ahead * plane, 1, 1))
    )


def coupled(acc_diag, porosity, k, x, terms):
    total = acc_diag[k, x] * terms[k]
    mixed = None
    for j in range(3):
        if COUPLING[k][j] != 0.0:
            part = COUPLING[k][j] * terms[j]
            mixed = part if mixed is None else mixed + part
    return total + porosity[x] * mixed


def invert(slopes, acc_diag, porosity, diagonal, x, inverse):
    m = []
    for k in range(3):
        line = []
        for j in range(3):
            if j == k:
                entry = acc_diag[k, x] * slopes[k]
            else:
                entry = porosity[x] * COUPLING[k][j] * slopes[j]
            if j == 0:
                entry = entry + diagonal[k]
            line.append(entry)
        m.append(line)
    cofactor = [
        [
            m[1][1] * m[2][2] - m[1][2] * m[2][1],
            m[1][2] * m[2][0] - m[1][0] * m[2][2],
            m[1][0] * m[2][1] - m[1][1] * m[2][0],
        ],
        [
            m[0][2] * m[2][1] - m[0][1] * m[2][2],
            m[0][0] * m[2][2] - m[0][2] * m[2][0],
            m[0][1] * m[2][0] - m[0][0] * m[2][1],
        ],
        [
            m[0][1] * m[1][2] - m[0][2] * m[1][1],
            m[0][2] * m[1][0] - m[0][0] * m[1][2],
            m[0][0] * m[1][1] - m[0][1] * m[1][0],
        ],
    ]
    determinant = m[0][0] * cofactor[0][0] + m[0][1] * cofactor[0][1] + m[0][2] * cofactor[0][2]
    reciprocal = 1.0 / determinant
    for k in range(3):
        for j in range(3):
            inverse[k, j, x] = cofactor[j][k] * reciprocal


def total_of(plane):
    return jnp.sum(jnp.sum(plane, 1, keepdims=True), 0, keepdims=True)


def broadcast_rows(outgoing, mean, dots=()):
    lane = iota((1, 128), 1)
    row = jnp.broadcast_to(mean, (1, 128))
    for n, dot in enumerate(dots):
        row = jnp.where(lane == 127 - n, dot, row)
    outgoing[...] = jnp.broadcast_to(row, (DEVS, 128))


def start_body(
    state_in,
    acc_in,
    porosity_in,
    mobility_in,
    trans_x_in,
    trans_y_in,
    trans_z_in,
    from_low_x,
    from_high_x,
    from_low_y,
    from_high_y,
    fields,
    sums,
    face_x,
    face_y,
    face_z,
    inner,
    edges,
    inverse,
    right,
    outgoing,
    state,
    acc_diag,
    porosity,
    mobility,
    trans_x,
    trans_y,
    trans_z,
    diagonal,
    sems,
):
    copies = fetch(
        (
            (mobility_in, mobility),
            (trans_x_in, trans_x),
            (trans_y_in, trans_y),
            (trans_z_in, trans_z),
            (state_in, state),
            (acc_in, acc_diag),
            (porosity_in, porosity),
        ),
        sems,
    )
    row = lax.axis_index("row")
    col = lax.axis_index("col")
    low_x = jnp.where(row > 0, 1.0, 0.0)
    high_x = jnp.where(row < ROWS - 1, 1.0, 0.0)
    low_y = jnp.where(col > 0, 1.0, 0.0)
    high_y = jnp.where(col < COLS - 1, 1.0, 0.0)
    lane = iota((8, 256), 1)
    line = iota((8, 256), 0)
    t_low_x = read_plane(from_low_x, 64) * low_x
    t_low_y = read_plane(from_low_y, 64) * low_y
    for copy in copies[:4]:
        copy.wait()
    for k in range(3):
        m_low_x = read_plane(from_low_x, 16 * k)
        m_high_x = read_plane(from_high_x, 16 * k)
        m_low_y = read_plane(from_low_y, 16 * k)
        m_high_y = read_plane(from_high_y, 16 * k)
        previous = t_low_x * 0.5 * (m_low_x + mobility[k, 0])
        face_x[k, 0] = previous
        planes = [mobility[k, x] for x in range(8)]
        for x in range(8):
            here = planes[x]
            around = neighbours(planes, x, m_low_x, m_high_x, m_low_y, m_high_y)
            tx = trans_x[x] if x < 7 else trans_x[x] * high_x
            ahead = tx * 0.5 * (here + around[0])
            face_x[k, x + 1] = ahead
            total = ahead + previous
            previous = ahead
            ty = jnp.where(line == 7, trans_y[x] * high_y, trans_y[x])
            ahead_y = ty * 0.5 * (here + around[2])
            entering = t_low_y[x : x + 1] * 0.5 * (m_low_y[x : x + 1] + here[0:1])
            behind_y = jnp.where(line == 0, entering, pltpu.roll(ahead_y, 1, 0))
            face_y[0, k, x] = ahead_y
            face_y[1, k, x] = behind_y
            total = total + (ahead_y + behind_y)
            ahead_z = jnp.where(lane < 255, trans_z[x] * 0.5 * (here + around[4]), 0.0)
            face_z[k, x] = ahead_z
            total = total + (ahead_z + pltpu.roll(ahead_z, 1, 1))
            diagonal[k, x] = total + here * fields[0, x * 8 : x * 8 + 8, :]

    def summed(face, *place):
        return face[0, *place] + face[1, *place] + face[2, *place]

    edges[0] = summed(face_x, 8)
    edges[1] = summed(face_x, 0)
    edges[2] = face_y[0, 0, :, 7, :] + face_y[0, 1, :, 7, :] + face_y[0, 2, :, 7, :]
    edges[3] = face_y[1, 0, :, 0, :] + face_y[1, 1, :, 0, :] + face_y[1, 2, :, 0, :]
    halo = (
        read_plane(from_low_x, 48),
        read_plane(from_high_x, 48),
        read_plane(from_low_y, 48),
        read_plane(from_high_y, 48),
    )
    for copy in copies[4:]:
        copy.wait()
    planes = [state[0, x] for x in range(8)]
    whole = jnp.zeros((8, 256), F32)
    for x in range(8):
        up_z = summed(face_z, x)
        kept = up_z + pltpu.roll(up_z, 1, 1)
        kept = kept + jnp.where(line < 7, summed(face_y.at[0], x), 0.0)
        kept = kept + jnp.where(line > 0, summed(face_y.at[1], x), 0.0)
        if x < 7:
            kept = kept + summed(face_x, x + 1)
        if x > 0:
            kept = kept + summed(face_x, x)
        inner[x] = kept
        around = neighbours(planes, x, *halo)
        source = fields[1, x * 8 : x * 8 + 8, :]
        for k in range(3):
            value = (
                gathered((face_x, face_y, face_z), k, x, planes[x], around)
                + mobility[k, x] * source
                - diagonal[k, x] * planes[x]
            )
            right[k, x] = value
            whole = whole + value
        slopes = []
        for k in range(3):
            bent = jnp.tanh(state[k, x])
            slopes.append(1.5 - 0.5 * bent * bent)
        invert(slopes, acc_diag, porosity, [diagonal[k, x] for k in range(3)], x, inverse)
    first = jnp.where(
        (iota((8, 128), 0) == 4) & (iota((8, 128), 1) == 0), total_of(whole), sums[0:8, :]
    )
    second = sums[8:16, :]
    for other in range(COLS):
        outgoing[other, 0:8, :] = first
        outgoing[other, 8:16, :] = second


def shares(per_block, hole):
    share = per_block[0] * hole[0:1]
    for a in range(1, 4):
        share = share + per_block[a] * hole[a : a + 1]
    return jnp.sum(share, 1, keepdims=True)


def open_wells_body(arrived, coarse, divisor, per_block, hole, tile):
    totals = jnp.zeros((8, 128), F32)
    others = jnp.zeros((8, 128), F32)
    for other in range(COLS):
        totals = totals + arrived[other, 0:8, :]
        others = others + arrived[other, 8:16, :]
    blocks = [arrived[:, a, :] for a in range(4)]
    for a in range(4):
        per_block[a] = blocks[a]
    upper = iota((8, 128), 0) < 4
    div = jnp.where(upper, totals + pltpu.roll(others, 4, 0), 1.0)
    divisor[...] = div
    found = jnp.where(upper, others, 0.0) / div
    hole[...] = found
    share = shares(blocks, found) + arrived[:, 4, 0:1]
    tile[0:32, :] = jnp.where(iota((COLS, 128), 1) == 0, share * -1.0, 0.0)
    tile[32:64, :] = coarse[...]


def finish_right_body(partly, hole, mobility, cell, label, index, right):
    back = to_cells(hole[...], index, marks_of(cell, label))
    for x in range(8):
        for k in range(3):
            right[k, x] = partly[k, x] + mobility[k, x] * back[x * 8 : x * 8 + 8]


def find_direction(
    coarse_x,
    vector,
    mobility,
    face_x,
    face_y,
    face_z,
    inner,
    edges,
    inverse,
    divisor,
    per_block,
    cell,
    label,
    index,
    direction,
    to_high,
    to_low,
    outgoing,
    swept,
    for_wells,
    for_sides,
    sems,
):
    row = lax.axis_index("row")
    col = lax.axis_index("col")
    faces = (face_x, face_y, face_z)

    def wide(at_row, at_col):
        place = at_col * ROWS + at_row
        value = coarse_x[pl.ds(place, 1), :]
        return jnp.broadcast_to(jnp.concatenate([value, value], 1), (8, 256))

    own = wide(row, col)
    x_high = wide(jnp.minimum(row + 1, ROWS - 1), col)
    x_low = wide(jnp.maximum(row - 1, 0), col)
    y_high = wide(row, jnp.minimum(col + 1, COLS - 1))
    y_low = wide(row, jnp.maximum(col - 1, 0))
    weights = coarse_x[pl.ds(row, COLS, stride=ROWS), :]
    sums = [jnp.sum(weights * per_block[a], 0, keepdims=True) for a in range(4)]
    sums = jnp.concatenate([*sums, jnp.zeros((4, 128), F32)], 0)
    marks = marks_of(cell, label)
    back = to_cells(sums / divisor[...], index, marks)
    line = iota((8, 256), 0)
    up_y = jnp.where(line == 7, y_high, own)
    down_y = jnp.where(line == 0, y_low, own)
    weighted = []
    inside = jnp.zeros((8, 256), F32)
    for x in range(8):
        around = (own if x < 7 else x_high, own if x > 0 else x_low, up_y, down_y, own)
        terms = [
            vector[k, x] + gathered(faces, k, x, own, around) + mobility[k, x] * back[x * 8 : x * 8 + 8]
            for k in range(3)
        ]
        for k in range(3):
            value = (
                inverse[k, 0, x] * terms[0]
                + inverse[k, 1, x] * terms[1]
                + inverse[k, 2, x] * terms[2]
            )
            direction[k, x] = value
            if k == 0:
                kept = value - own
                swept[x] = kept
        inside = inside + kept * inner[x]
        weighted.append(kept * (mobility[0, x] + mobility[1, x] + mobility[2, x]))
    to_high[...] = swept[7]
    to_low[...] = swept[0]
    last = swept[:, 7, :]
    first = swept[:, 0, :]
    for other in range(COLS):
        send = jnp.where(other < col, first, last)
        for_sides[other, 0:8, :] = send[:, :128]
        for_sides[other, 8:16, :] = send[:, 128:]
    side_copy = pltpu.make_async_copy(for_sides, outgoing.at[:, 8:24, :], sems.at[0])
    side_copy.start()
    local = to_wells(jnp.concatenate(weighted, 0), index, marks)
    sides = (swept[7] * edges[0], swept[0] * edges[1], last * edges[2], first * edges[3])
    lane = iota((8, 128), 1)
    for n, term in enumerate((inside, *sides)):
        local = jnp.where((iota((8, 128), 0) == 4) & (lane == n), total_of(term), local)
    for other in range(COLS):
        for_wells[other] = local
    well_copy = pltpu.make_async_copy(for_wells, outgoing.at[:, 0:8, :], sems.at[1])
    well_copy.start()
    side_copy.wait()
    well_copy.wait()


def coarse_solve(solve, means, ordered, coarse_x):
    for r in range(ROWS):
        ordered[pl.ds(r, COLS, stride=ROWS), :] = means[r * COLS : (r + 1) * COLS, :]
    coarse_x[...] = jnp.dot(solve[...], ordered[...], precision=EXACT, preferred_element_type=F32)


def direction_body(solve, received, *rest):
    *rest, ordered, coarse_x = rest
    coarse_solve(solve, received, ordered, coarse_x)
    find_direction(coarse_x, *rest)


def place_rows(sources, target, base):
    for shift, source in enumerate(sources):
        start = pl.multiple_of(((lax.axis_index("row") - shift + ROWS) % ROWS) * COLS, COLS)
        target[pl.ds(start, COLS), :] = source[base : base + COLS, :]


def from_rows(solve, sources, rest, opening):
    *rest, ordered, coarse_x = rest
    place_rows(sources, coarse_x, 0)
    every = coarse_x[...]
    means = every[:, 0:1]
    if not opening:
        means = means + pltpu.roll(every, COLS, 0)[:, 1:2]
        means = means + pltpu.roll(every, DEVS - COLS, 0)[:, 2:3]
    means = jnp.broadcast_to(means * (-1.0 / CELLS), (DEVS, 128))
    coarse_solve(solve, means, ordered, coarse_x)
    find_direction(coarse_x, *rest)


def gathered_direction_body(solve, own, low, far, high, *rest):
    from_rows(solve, (own, low, far, high), rest, False)


def opening_direction_body(own, low, far, high, *rest):
    *rest, solve, for_wells, for_sides, sems, ordered, coarse_x = rest
    place_rows((own, low, far, high), solve, COLS)
    rest = (*rest, for_wells, for_sides, sems, ordered, coarse_x)
    from_rows(solve, (own, low, far, high), rest, True)


def sum_wells_body(came, divisor, per_block, hole, tile):
    sums = jnp.zeros((8, 128), F32)
    for other in range(COLS):
        sums = sums + came[other, 0:8, :]
    found = jnp.where(iota((8, 128), 0) < 4, sums, 0.0) / divisor[...]
    hole[...] = found
    if tile is not None:
        pieces = came[:, 4, :]
        share = shares(per_block, found) + pieces[:, 0:1]
        share = share + pltpu.roll(pieces, 1, 0)[:, 3:4] + pltpu.roll(pieces, COLS - 1, 0)[:, 4:5]
        tile[...] = jnp.where(iota((COLS, 128), 1) == 0, share, pieces)


def close_wells_body(came, divisor, per_block, from_low, from_high, hole, tile):
    sum_wells_body(came, divisor, per_block, hole, tile)


def coupling_planes(
    hole,
    swept,
    from_low,
    from_high,
    came,
    mobility,
    face_x,
    face_y,
    face_z,
    cell,
    label,
    index,
):
    col = lax.axis_index("col")
    faces = (face_x, face_y, face_z)
    back = to_cells(hole[...], index, marks_of(cell, label))
    below = jnp.maximum(col - 1, 0)
    above = jnp.minimum(col + 1, COLS - 1)
    y_low = jnp.concatenate([came[below, 8:16, :], came[below, 16:24, :]], 1)
    y_high = jnp.concatenate([came[above, 8:16, :], came[above, 16:24, :]], 1)
    planes = [swept[x] for x in range(8)]
    for x in range(8):
        around = neighbours(planes, x, from_low[...], from_high[...], y_low, y_high)
        for k in range(3):
            value = gathered(faces, k, x, planes[x], around)
            yield k, x, value + mobility[k, x] * back[x * 8 : x * 8 + 8]


def first_image_body(*rest):
    *rest, tied = rest
    for k, x, value in coupling_planes(*rest):
        tied[k, x] = -value


def second_image_body(divisor, right, tied, *rest):
    *rest, image, outgoing, hole = rest
    sum_wells_body(rest[3], divisor, None, hole, None)
    totals = [jnp.zeros((8, 256), F32) for _ in range(5)]
    for k, x, value in coupling_planes(hole, *rest):
        value = tied[k, x] - value
        image[k, x] = value
        goal = right[k, x]
        one = goal + tied[k, x]
        for n, term in enumerate((one * one, one * value, value * value, one * goal, value * goal)):
            totals[n] = totals[n] + term
    broadcast_rows(outgoing, jnp.zeros((1, 1), F32), [total_of(t) for t in totals])


def update_body(last, *refs):
    (
        met,
        current,
        acc_diag,
        porosity,
        right,
        tied,
        image,
        first_direction,
        second_direction,
        *outs,
    ) = refs
    sums = jnp.sum(met[...], 0, keepdims=True)
    g00, g01, g11, t0, t1 = [sums[:, 127 - n : 128 - n] for n in range(5)]
    l00 = jnp.sqrt(g00)
    l10 = g01 / l00
    l11 = jnp.sqrt(g11 - l10 * l10)
    f0 = t0 / l00
    f1 = (t1 - l10 * f0) / l11
    y1 = f1 / l11
    y0 = (f0 - l10 * y1) / l00
    if last:
        fresh, residual = outs
    else:
        mobility, face_x, face_y, face_z, fields, fresh, residual, inverse, outgoing = outs
    mean = jnp.zeros((8, 256), F32)
    for x in range(8):
        remainder = []
        slopes = []
        for k in range(3):
            old = current[k, x]
            step = y0 * first_direction[k, x] + y1 * second_direction[k, x]
            new = old + step
            fresh[k, x] = new
            before = jnp.tanh(old)
            after = jnp.tanh(new)
            remainder.append(0.5 * ((after - before) - (1.0 - before * before) * step))
            slopes.append(1.5 - 0.5 * after * after)
        for k in range(3):
            goal = right[k, x]
            value = (
                goal
                - y0 * (goal + tied[k, x])
                - y1 * image[k, x]
                - coupled(acc_diag, porosity, k, x, remainder)
            )
            residual[k, x] = -value if last else value
            mean = mean + value
        if not last:
            diagonal = []
            for k in range(3):
                total = face_x[k, x + 1] + face_x[k, x] + (face_y[0, k, x] + face_y[1, k, x])
                total = total + (face_z[k, x] + pltpu.roll(face_z[k, x], 1, 1))
                diagonal.append(total + mobility[k, x] * fields[0, x * 8 : x * 8 + 8, :])
            invert(slopes, acc_diag, porosity, diagonal, x, inverse)
    if not last:
        broadcast_rows(outgoing, total_of(mean) * (1.0 / CELLS))


def per_device(
    state,
    acc_diag,
    porosity,
    mobility,
    trans_x,
    trans_y,
    trans_z,
    perf_cell,
    perf_owner,
    perf_well,
    perf_index,
    perf_head,
    well_stiff,
    well_drive,
    coarse_inverse,
):
    field = (8, 8, 256)
    triple = (3, *field)
    plane = (8, 256)
    count = perf_cell.shape[1]

    def ring(value, axis, count, shift):
        return lax.ppermute(value, axis, [(i, (i + shift) % count) for i in range(count)])

    def swap_cols(value):
        return lax.all_to_all(value, "col", 0, 0, tiled=True)

    def swap_all(value):
        return lax.all_to_all(value, ("row", "col"), 0, 0, tiled=True)

    def exchange(to_high, to_low, outgoing):
        return (
            ring(to_high, "row", ROWS, 1),
            ring(to_low, "row", ROWS, -1),
            swap_cols(outgoing),
        )

    vmem = pl.BlockSpec(memory_space=pltpu.VMEM)
    hbm = pl.BlockSpec(memory_space=pltpu.HBM)

    def run(body, outs, *args, scratch=(), far=(), far_outs=(), room=ROOM):
        specs = [hbm if n in far else vmem for n in range(len(args))]
        return pl.pallas_call(
            body,
            out_shape=[jax.ShapeDtypeStruct(s, t) for s, t in outs],
            in_specs=specs,
            out_specs=[hbm if n in far_outs else vmem for n in range(len(outs))],
            scratch_shapes=list(scratch),
            compiler_params=pltpu.CompilerParams(vmem_limit_bytes=room),
        )(*args)

    def buffers(*values):
        return [pltpu.VMEM(value.shape, value.dtype) for value in values]

    line = (1, count)
    up_x, down_x, up_y, down_y, cell, label, index, fields, sums = run(
        prepare_body,
        [
            ((80, 128), F32),
            ((64, 128), F32),
            ((80, 128), F32),
            ((64, 128), F32),
            (line, jnp.int32),
            (line, jnp.int32),
            (line, F32),
            ((2, 64, 256), F32),
            ((16, 128), F32),
        ],
        state,
        mobility,
        trans_x,
        trans_y,
        perf_cell,
        perf_owner,
        perf_well,
        perf_index,
        perf_head,
        well_stiff,
        well_drive,
        scratch=[
            pltpu.VMEM(field, F32),
            pltpu.VMEM(triple, F32),
            pltpu.VMEM(plane, F32),
            pltpu.VMEM(field, F32),
            *buffers(perf_owner, perf_well, perf_head, well_stiff, well_drive),
            pltpu.SemaphoreType.DMA((11,)),
        ],
        far=range(0, 11),
        room=FIRST_ROOM,
    )
    marks = (cell, label, index)
    face_x, face_y, face_z, inner, edges, inverse, partly, outgoing = run(
        start_body,
        [
            ((3, 9, *plane), F32),
            ((2, *triple), F32),
            (triple, F32),
            (field, F32),
            ((4, *plane), F32),
            ((3, *triple), F32),
            (triple, F32),
            ((COLS, 16, 128), F32),
        ],
        state,
        acc_diag,
        porosity,
        mobility,
        trans_x,
        trans_y,
        trans_z,
        ring(up_x, "row", ROWS, 1),
        ring(down_x, "row", ROWS, -1),
        ring(up_y, "col", COLS, 1),
        ring(down_y, "col", COLS, -1),
        fields,
        sums,
        scratch=[
            *buffers(state, acc_diag, porosity, mobility, trans_x, trans_y, trans_z),
            pltpu.VMEM(triple, F32),
            pltpu.SemaphoreType.DMA((7,)),
        ],
        far=range(0, 7),
        room=START_ROOM,
    )
    faces = (face_x, face_y, face_z)
    well_tile = (8, 128)
    divisor, per_block, hole, tile = run(
        open_wells_body,
        [(well_tile, F32), ((4, COLS, 128), F32), (well_tile, F32), ((2 * COLS, 128), F32)],
        swap_cols(outgoing),
        coarse_inverse,
    )
    (right,) = run(finish_right_body, [(triple, F32)], partly, hole, mobility, *marks)
    current = state
    solve = None
    sends = [(triple, F32), (plane, F32), (plane, F32), ((COLS, 24, 128), F32), (field, F32)]
    send_scratch = [
        pltpu.VMEM((COLS, 8, 128), F32),
        pltpu.VMEM((COLS, 16, 128), F32),
        pltpu.SemaphoreType.DMA((2,)),
    ]
    coarse_scratch = [pltpu.VMEM((DEVS, 128), F32)] * 2

    def spread_rows(tile):
        return (tile, *(ring(tile, "row", ROWS, shift) for shift in (1, 2, 3)))

    for outer in range(NEWTON):
        static = (mobility, *faces, inner, edges, inverse, divisor, per_block, *marks)
        if outer == 0:
            first_direction, to_high, to_low, outgoing, swept, solve = run(
                opening_direction_body,
                [*sends, ((DEVS, DEVS), F32)],
                *spread_rows(tile),
                right,
                *static,
                scratch=[*send_scratch, *coarse_scratch],
                far_outs=(3,),
            )
        else:
            first_direction, to_high, to_low, outgoing, swept = run(
                direction_body,
                sends,
                solve,
                swap_all(outgoing),
                right,
                *static,
                scratch=[*send_scratch, *coarse_scratch],
                far_outs=(3,),
            )
        from_low, from_high, came = exchange(to_high, to_low, outgoing)
        hole, tile = run(
            close_wells_body,
            [(well_tile, F32), ((COLS, 128), F32)],
            came,
            divisor,
            per_block,
            from_low,
            from_high,
        )
        (tied,) = run(
            first_image_body,
            [(triple, F32)],
            hole,
            swept,
            from_low,
            from_high,
            came,
            mobility,
            *faces,
            *marks,
        )
        second_direction, to_high, to_low, outgoing, swept = run(
            gathered_direction_body,
            sends,
            solve,
            *spread_rows(tile),
            tied,
            *static,
            scratch=[*send_scratch, *coarse_scratch],
            far_outs=(3,),
        )
        image, outgoing = run(
            second_image_body,
            [(triple, F32), ((DEVS, 128), F32)],
            divisor,
            right,
            tied,
            swept,
            *exchange(to_high, to_low, outgoing),
            mobility,
            *faces,
            *marks,
            scratch=[pltpu.VMEM(well_tile, F32)],
        )
        met = swap_all(outgoing)
        last = outer == NEWTON - 1
        outs = [(triple, F32), (triple, F32)]
        extra = ()
        if not last:
            outs += [((3, *triple), F32), ((DEVS, 128), F32)]
            extra = (mobility, *faces, fields)
        results = run(
            lambda *refs: update_body(last, *refs),
            outs,
            met,
            current,
            acc_diag,
            porosity,
            right,
            tied,
            image,
            first_direction,
            second_direction,
            *extra,
        )
        if last:
            return tuple(results)
        current, right, inverse, outgoing = results


def solution(mesh):
    in_specs = (
        P(None, "row", "col", None),
        P(None, "row", "col", None),
        P("row", "col", None),
        P(None, "row", "col", None),
        P("row", "col", None),
        P("row", "col", None),
        P("row", "col", None),
        P("row", "col"),
        P("row", "col"),
        P("row", "col"),
        P("row", "col"),
        P("row", "col"),
        P("row", "col"),
        P("row", "col"),
        P("row", None),
    )
    out_specs = (P(None, "row", "col", None), P(None, "row", "col", None))
    return jax.shard_map(
        per_device, mesh=mesh, in_specs=in_specs, out_specs=out_specs, check_vma=False
    )
```

```python
import jax
import jax.numpy as jnp
from jax import lax
from jax.experimental import pallas as pl
from jax.experimental.pallas import tpu as pltpu
from jax.sharding import PartitionSpec as P

NEWTON = 2
WELLS_DEV = 16
EXACT = lax.Precision.HIGHEST
COUPLING = ((0.0, 0.3, 0.2), (0.25, 0.0, 0.15), (0.2, 0.1, 0.0))
ROWS = 4
COLS = 32
DEVS = ROWS * COLS
CELLS = 8 * 8 * 256
F32 = jnp.float32
BF16 = jnp.bfloat16
ROOM = 24_000_000
FIRST_ROOM = 66_700_000


def iota(shape, dim):
    return lax.broadcasted_iota(jnp.int32, shape, dim)


def split(value):
    high = value.astype(BF16)
    low = (value - high.astype(F32)).astype(BF16)
    return jnp.concatenate([high, low], 0)


def joined(pair):
    half = pair.shape[0] // 2
    return pair[:half] + pair[half:]


def nn(a, b):
    return lax.dot_general(a, b, (((1,), (0,)), ((), ())), preferred_element_type=F32)


def nt(a, b):
    return lax.dot_general(a, b, (((1,), (1,)), ((), ())), preferred_element_type=F32)


def marks_of(cell, label):
    count = cell.shape[1]
    layer = jnp.where(iota((256, count), 0) == (cell[...] & 255), 1.0, 0.0).astype(BF16)
    place = jnp.where(iota((64, count), 0) == (cell[...] >> 8), 1.0, 0.0)
    low_mark = jnp.where(iota((128, count), 0) == (label[...] & 127), 1.0, 0.0).astype(BF16)
    high_mark = jnp.where(iota((8, count), 0) == (label[...] >> 7), 1.0, 0.0)
    return layer, place, low_mark, high_mark


def to_wells(field, index, marks):
    layer, place, low_mark, high_mark = marks
    picked = joined(nn(split(field), layer))
    value = index[...] * jnp.sum(picked * place, 0, keepdims=True)
    return joined(nt(split(high_mark * value), low_mark))


def to_cells(per_well, index, marks):
    layer, place, low_mark, high_mark = marks
    spread = joined(nn(split(per_well), low_mark))
    value = index[...] * jnp.sum(spread * high_mark, 0, keepdims=True)
    return joined(nt(split(place * value), layer))


def write_plane(ref, base, plane):
    ref[base : base + 8, :] = plane[:, :128]
    ref[base + 8 : base + 16, :] = plane[:, 128:]


def read_plane(ref, base):
    return jnp.concatenate([ref[base : base + 8, :], ref[base + 8 : base + 16, :]], 1)


def fetch(pairs, sems):
    copies = [
        pltpu.make_async_copy(source, target, sems.at[n]) for n, (source, target) in enumerate(pairs)
    ]
    for copy in copies:
        copy.start()
    return copies


def pack_body(
    state,
    mobility,
    trans_x,
    trans_y,
    up_x,
    down_x,
    up_y,
    down_y,
    pressure,
    carried,
    along_x,
    along_y,
    sems,
):
    copies = fetch(
        (
            (mobility, carried),
            (state.at[0], pressure),
            (trans_x.at[7], along_x),
            (trans_y, along_y),
        ),
        sems,
    )
    for copy in copies:
        copy.wait()
    for k in range(3):
        write_plane(up_x, 16 * k, carried[k, 7])
        write_plane(down_x, 16 * k, carried[k, 0])
        write_plane(up_y, 16 * k, carried[k, :, 7, :])
        write_plane(down_y, 16 * k, carried[k, :, 0, :])
    write_plane(up_x, 48, pressure[7])
    write_plane(down_x, 48, pressure[0])
    write_plane(up_y, 48, pressure[:, 7, :])
    write_plane(down_y, 48, pressure[:, 0, :])
    write_plane(up_x, 64, along_x[...])
    write_plane(up_y, 64, along_y[:, 7, :])


def prepare_body(
    state,
    mobility,
    cell_in,
    owner_in,
    well_in,
    index_in,
    head_in,
    stiff_in,
    drive_in,
    cell,
    label,
    index,
    density,
    pulled,
    sums,
    pressure,
    carried,
    owner,
    well,
    head,
    stiff,
    drive,
    sems,
):
    copies = fetch(
        (
            (cell_in, cell),
            (owner_in, owner),
            (well_in, well),
            (index_in, index),
            (head_in, head),
            (stiff_in, stiff),
            (drive_in, drive),
            (mobility, carried),
            (state.at[0], pressure),
        ),
        sems,
    )
    for copy in copies:
        copy.wait()
    label[...] = owner[...] * WELLS_DEV + well[...]
    layer, place, low_mark, high_mark = marks_of(cell, label)
    both = jnp.concatenate([place * index[...], place * (index[...] * head[...])], 0)
    spread = joined(nt(split(both), layer))
    density[...] = spread[:64]
    pulled[...] = spread[64:]
    total = (carried[0] + carried[1] + carried[2]).reshape(64, 256)
    pair = split(jnp.concatenate([total, total * pressure[...].reshape(64, 256)], 0))
    picked = joined(nn(pair, layer)) * jnp.concatenate([place, place], 0)
    base = index[...] * jnp.sum(picked[:64], 0, keepdims=True)
    terms = index[...] * jnp.sum(picked[64:], 0, keepdims=True) - base * head[...]
    local = joined(nt(split(jnp.concatenate([high_mark * base, high_mark * terms], 0)), low_mark))
    me = lax.axis_index("col")
    tile = jnp.where(iota((WELLS_DEV, 128), 1) % WELLS_DEV == iota((WELLS_DEV, 128), 0), 1.0, 0.0)
    lines = jnp.concatenate([stiff[...], drive[...], jnp.zeros((6, WELLS_DEV), F32)], 0)
    lines = jnp.dot(lines, tile, precision=EXACT, preferred_element_type=F32)
    mine = (iota((8, 128), 1) // WELLS_DEV == me % 8) & (iota((8, 128), 0) % 4 == me // 8)
    upper = iota((8, 128), 0) < 4
    extra = jnp.where(mine, jnp.where(upper, lines[1:2], lines[0:1]), 0.0)
    corner = (iota((8, 128), 0) == 4) & (iota((8, 128), 1) == 0)
    sums[0:8, :] = jnp.where(corner, jnp.sum(terms, 1, keepdims=True) * -1.0, local[:8])
    sums[8:16, :] = jnp.where(upper, local[8:], 0.0) + extra


def inside_flags():
    row = lax.axis_index("row")
    col = lax.axis_index("col")
    return (
        jnp.where(row > 0, 1.0, 0.0),
        jnp.where(row < ROWS - 1, 1.0, 0.0),
        jnp.where(col > 0, 1.0, 0.0),
        jnp.where(col < COLS - 1, 1.0, 0.0),
    )


def border_body(
    up_x, down_x, up_y, down_y, from_low_x, from_high_x, from_low_y, from_high_y, sums, outgoing
):
    low_x, high_x, low_y, high_y = inside_flags()

    def crossing(lower, upper, inside):
        mobile = read_plane(lower, 0) + read_plane(upper, 0)
        for k in (1, 2):
            mobile = mobile + read_plane(lower, 16 * k) + read_plane(upper, 16 * k)
        rate = read_plane(lower, 64) * 0.5 * mobile
        return rate * (read_plane(lower, 48) - read_plane(upper, 48)) * inside

    net = crossing(up_x, from_high_x, high_x) - crossing(from_low_x, down_x, low_x)
    net = net + crossing(up_y, from_high_y, high_y) - crossing(from_low_y, down_y, low_y)
    corner = (iota((8, 128), 0) == 4) & (iota((8, 128), 1) == 0)
    first = sums[0:8, :] - jnp.where(corner, total_of(net), 0.0)
    second = sums[8:16, :]
    for other in range(COLS):
        outgoing[other, 0:8, :] = first
        outgoing[other, 8:16, :] = second


def neighbours(planes, x, x_low, x_high, y_low, y_high):
    plane = planes[x]
    line = iota((8, 256), 0)
    return (
        planes[x + 1] if x < 7 else x_high,
        planes[x - 1] if x > 0 else x_low,
        jnp.where(line == 7, y_high[x : x + 1], pltpu.roll(plane, 7, 0)),
        jnp.where(line == 0, y_low[x : x + 1], pltpu.roll(plane, 1, 0)),
        pltpu.roll(plane, 255, 1),
    )


def gathered(faces, k, x, plane, around):
    face_x, face_y, face_z = faces
    ahead = face_z[k, x]
    return (
        face_x[k, x + 1] * around[0]
        + face_x[k, x] * around[1]
        + (face_y[0, k, x] * around[2] + face_y[1, k, x] * around[3])
        + (ahead * around[4] + pltpu.roll(ahead * plane, 1, 1))
    )


def coupled(acc_diag, porosity, k, x, terms):
    total = acc_diag[k, x] * terms[k]
    mixed = None
    for j in range(3):
        if COUPLING[k][j] != 0.0:
            part = COUPLING[k][j] * terms[j]
            mixed = part if mixed is None else mixed + part
    return total + porosity[x] * mixed


def invert(slopes, acc_diag, porosity, diagonal, x, inverse):
    m = []
    for k in range(3):
        line = []
        for j in range(3):
            if j == k:
                entry = acc_diag[k, x] * slopes[k]
            else:
                entry = porosity[x] * COUPLING[k][j] * slopes[j]
            if j == 0:
                entry = entry + diagonal[k]
            line.append(entry)
        m.append(line)
    cofactor = [
        [
            m[1][1] * m[2][2] - m[1][2] * m[2][1],
            m[1][2] * m[2][0] - m[1][0] * m[2][2],
            m[1][0] * m[2][1] - m[1][1] * m[2][0],
        ],
        [
            m[0][2] * m[2][1] - m[0][1] * m[2][2],
            m[0][0] * m[2][2] - m[0][2] * m[2][0],
            m[0][1] * m[2][0] - m[0][0] * m[2][1],
        ],
        [
            m[0][1] * m[1][2] - m[0][2] * m[1][1],
            m[0][2] * m[1][0] - m[0][0] * m[1][2],
            m[0][0] * m[1][1] - m[0][1] * m[1][0],
        ],
    ]
    determinant = m[0][0] * cofactor[0][0] + m[0][1] * cofactor[0][1] + m[0][2] * cofactor[0][2]
    reciprocal = 1.0 / determinant
    for k in range(3):
        for j in range(3):
            inverse[k, j, x] = cofactor[j][k] * reciprocal


def total_of(plane):
    return jnp.sum(jnp.sum(plane, 1, keepdims=True), 0, keepdims=True)


def broadcast_rows(outgoing, mean, dots=()):
    lane = iota((1, 128), 1)
    row = jnp.broadcast_to(mean, (1, 128))
    for n, dot in enumerate(dots):
        row = jnp.where(lane == 127 - n, dot, row)
    outgoing[...] = jnp.broadcast_to(row, (DEVS, 128))


def start_body(
    state_in,
    acc_in,
    porosity_in,
    mobility_in,
    trans_x_in,
    trans_y_in,
    trans_z_in,
    from_low_x,
    from_high_x,
    from_low_y,
    from_high_y,
    density,
    pulled,
    hole,
    cell,
    label,
    index,
    face_x,
    face_y,
    face_z,
    inner,
    edges,
    inverse,
    right,
    state,
    acc_diag,
    porosity,
    mobility,
    trans_x,
    trans_y,
    trans_z,
    diagonal,
    sems,
):
    copies = fetch(
        (
            (mobility_in, mobility),
            (trans_x_in, trans_x),
            (trans_y_in, trans_y),
            (trans_z_in, trans_z),
            (state_in, state),
            (acc_in, acc_diag),
            (porosity_in, porosity),
        ),
        sems,
    )
    back = to_cells(hole[...], index, marks_of(cell, label))
    low_x, high_x, low_y, high_y = inside_flags()
    lane = iota((8, 256), 1)
    line = iota((8, 256), 0)
    t_low_x = read_plane(from_low_x, 64) * low_x
    t_low_y = read_plane(from_low_y, 64) * low_y
    for copy in copies[:4]:
        copy.wait()
    for k in range(3):
        m_low_x = read_plane(from_low_x, 16 * k)
        m_high_x = read_plane(from_high_x, 16 * k)
        m_low_y = read_plane(from_low_y, 16 * k)
        m_high_y = read_plane(from_high_y, 16 * k)
        previous = t_low_x * 0.5 * (m_low_x + mobility[k, 0])
        face_x[k, 0] = previous
        planes = [mobility[k, x] for x in range(8)]
        for x in range(8):
            here = planes[x]
            around = neighbours(planes, x, m_low_x, m_high_x, m_low_y, m_high_y)
            tx = trans_x[x] if x < 7 else trans_x[x] * high_x
            ahead = tx * 0.5 * (here + around[0])
            face_x[k, x + 1] = ahead
            total = ahead + previous
            previous = ahead
            ty = jnp.where(line == 7, trans_y[x] * high_y, trans_y[x])
            ahead_y = ty * 0.5 * (here + around[2])
            entering = t_low_y[x : x + 1] * 0.5 * (m_low_y[x : x + 1] + here[0:1])
            behind_y = jnp.where(line == 0, entering, pltpu.roll(ahead_y, 1, 0))
            face_y[0, k, x] = ahead_y
            face_y[1, k, x] = behind_y
            total = total + (ahead_y + behind_y)
            ahead_z = jnp.where(lane < 255, trans_z[x] * 0.5 * (here + around[4]), 0.0)
            face_z[k, x] = ahead_z
            total = total + (ahead_z + pltpu.roll(ahead_z, 1, 1))
            diagonal[k, x] = total + here * density[x * 8 : x * 8 + 8, :]

    def summed(face, *place):
        return face[0, *place] + face[1, *place] + face[2, *place]

    edges[0] = summed(face_x, 8)
    edges[1] = summed(face_x, 0)
    edges[2] = face_y[0, 0, :, 7, :] + face_y[0, 1, :, 7, :] + face_y[0, 2, :, 7, :]
    edges[3] = face_y[1, 0, :, 0, :] + face_y[1, 1, :, 0, :] + face_y[1, 2, :, 0, :]
    halo = (
        read_plane(from_low_x, 48),
        read_plane(from_high_x, 48),
        read_plane(from_low_y, 48),
        read_plane(from_high_y, 48),
    )
    for copy in copies[4:]:
        copy.wait()
    planes = [state[0, x] for x in range(8)]
    for x in range(8):
        up_z = summed(face_z, x)
        kept = up_z + pltpu.roll(up_z, 1, 1)
        kept = kept + jnp.where(line < 7, summed(face_y.at[0], x), 0.0)
        kept = kept + jnp.where(line > 0, summed(face_y.at[1], x), 0.0)
        if x < 7:
            kept = kept + summed(face_x, x + 1)
        if x > 0:
            kept = kept + summed(face_x, x)
        inner[x] = kept
        around = neighbours(planes, x, *halo)
        source = pulled[x * 8 : x * 8 + 8, :] + back[x * 8 : x * 8 + 8]
        for k in range(3):
            value = (
                gathered((face_x, face_y, face_z), k, x, planes[x], around)
                + mobility[k, x] * source
                - diagonal[k, x] * planes[x]
            )
            right[k, x] = value
        slopes = []
        for k in range(3):
            bent = jnp.tanh(state[k, x])
            slopes.append(1.5 - 0.5 * bent * bent)
        invert(slopes, acc_diag, porosity, [diagonal[k, x] for k in range(3)], x, inverse)


def shares(per_block, hole):
    share = per_block[0] * hole[0:1]
    for a in range(1, 4):
        share = share + per_block[a] * hole[a : a + 1]
    return jnp.sum(share, 1, keepdims=True)


def open_wells_body(arrived, coarse, divisor, per_block, hole, tile):
    totals = jnp.zeros((8, 128), F32)
    others = jnp.zeros((8, 128), F32)
    for other in range(COLS):
        totals = totals + arrived[other, 0:8, :]
        others = others + arrived[other, 8:16, :]
    blocks = [arrived[:, a, :] for a in range(4)]
    for a in range(4):
        per_block[a] = blocks[a]
    upper = iota((8, 128), 0) < 4
    div = jnp.where(upper, totals + pltpu.roll(others, 4, 0), 1.0)
    divisor[...] = div
    found = jnp.where(upper, others, 0.0) / div
    hole[...] = found
    share = shares(blocks, found) + arrived[:, 4, 0:1]
    tile[0:32, :] = jnp.where(iota((COLS, 128), 1) == 0, share * -1.0, 0.0)
    tile[32:64, :] = coarse[...]


def find_direction(
    coarse_x,
    vector,
    mobility,
    face_x,
    face_y,
    face_z,
    inner,
    edges,
    inverse,
    divisor,
    per_block,
    cell,
    label,
    index,
    direction_out,
    to_high,
    to_low,
    outgoing,
    swept,
    level,
    direction,
    for_wells,
    for_sides,
    sems,
):
    row = lax.axis_index("row")
    col = lax.axis_index("col")
    faces = (face_x, face_y, face_z)

    def wide(at_row, at_col):
        place = at_col * ROWS + at_row
        value = coarse_x[pl.ds(place, 1), :]
        return jnp.broadcast_to(jnp.concatenate([value, value], 1), (8, 256))

    own = wide(row, col)
    x_high = wide(jnp.minimum(row + 1, ROWS - 1), col)
    x_low = wide(jnp.maximum(row - 1, 0), col)
    y_high = wide(row, jnp.minimum(col + 1, COLS - 1))
    y_low = wide(row, jnp.maximum(col - 1, 0))
    level[...] = own[:, :128]
    weights = coarse_x[pl.ds(row, COLS, stride=ROWS), :]
    sums = [jnp.sum(weights * per_block[a], 0, keepdims=True) for a in range(4)]
    sums = jnp.concatenate([*sums, jnp.zeros((4, 128), F32)], 0)
    marks = marks_of(cell, label)
    back = to_cells(sums / divisor[...], index, marks)
    line = iota((8, 256), 0)
    up_y = jnp.where(line == 7, y_high, own)
    down_y = jnp.where(line == 0, y_low, own)
    weighted = []
    inside = jnp.zeros((8, 256), F32)
    for x in range(8):
        around = (own if x < 7 else x_high, own if x > 0 else x_low, up_y, down_y, own)
        terms = [
            vector[k, x] + gathered(faces, k, x, own, around) + mobility[k, x] * back[x * 8 : x * 8 + 8]
            for k in range(3)
        ]
        for k in range(3):
            value = (
                inverse[k, 0, x] * terms[0]
                + inverse[k, 1, x] * terms[1]
                + inverse[k, 2, x] * terms[2]
            )
            if k == 0:
                kept = value - own
                swept[x] = kept
            else:
                direction[k - 1, x] = value
        inside = inside + kept * inner[x]
        weighted.append(kept * (mobility[0, x] + mobility[1, x] + mobility[2, x]))
    to_high[...] = swept[7]
    to_low[...] = swept[0]
    last = swept[:, 7, :]
    first = swept[:, 0, :]
    for other in range(COLS):
        send = jnp.where(other < col, first, last)
        for_sides[other, 0:8, :] = send[:, :128]
        for_sides[other, 8:16, :] = send[:, 128:]
    side_copy = pltpu.make_async_copy(for_sides, outgoing.at[:, 8:24, :], sems.at[0])
    side_copy.start()
    direction_copy = pltpu.make_async_copy(direction, direction_out, sems.at[2])
    direction_copy.start()
    local = to_wells(jnp.concatenate(weighted, 0), index, marks)
    sides = (swept[7] * edges[0], swept[0] * edges[1], last * edges[2], first * edges[3])
    lane = iota((8, 128), 1)
    for n, term in enumerate((inside, *sides)):
        local = jnp.where((iota((8, 128), 0) == 4) & (lane == n), total_of(term), local)
    for other in range(COLS):
        for_wells[other] = local
    well_copy = pltpu.make_async_copy(for_wells, outgoing.at[:, 0:8, :], sems.at[1])
    well_copy.start()
    direction_copy.wait()
    side_copy.wait()
    well_copy.wait()


def coarse_solve(solve, means, ordered, coarse_x):
    for r in range(ROWS):
        ordered[pl.ds(r, COLS, stride=ROWS), :] = means[r * COLS : (r + 1) * COLS, :]
    coarse_x[...] = jnp.dot(solve[...], ordered[...], precision=EXACT, preferred_element_type=F32)


def direction_body(solve, received, *rest):
    *rest, ordered, coarse_x = rest
    coarse_solve(solve, received, ordered, coarse_x)
    find_direction(coarse_x, *rest)


def place_rows(sources, target, base):
    for shift, source in enumerate(sources):
        start = pl.multiple_of(((lax.axis_index("row") - shift + ROWS) % ROWS) * COLS, COLS)
        target[pl.ds(start, COLS), :] = source[base : base + COLS, :]


def from_rows(solve, sources, rest, opening):
    *rest, ordered, coarse_x = rest
    place_rows(sources, coarse_x, 0)
    every = coarse_x[...]
    means = every[:, 0:1]
    if not opening:
        means = means + pltpu.roll(every, COLS, 0)[:, 1:2]
        means = means + pltpu.roll(every, DEVS - COLS, 0)[:, 2:3]
    means = jnp.broadcast_to(means * (-1.0 / CELLS), (DEVS, 128))
    coarse_solve(solve, means, ordered, coarse_x)
    find_direction(coarse_x, *rest)


def gathered_direction_body(solve, own, low, far, high, *rest):
    from_rows(solve, (own, low, far, high), rest, False)


def opening_direction_body(own, low, far, high, *rest):
    *rest, solve, direction, for_wells, for_sides, sems, ordered, coarse_x = rest
    place_rows((own, low, far, high), solve, COLS)
    rest = (*rest, direction, for_wells, for_sides, sems, ordered, coarse_x)
    from_rows(solve, (own, low, far, high), rest, True)


def sum_wells_body(came, divisor, per_block, hole, tile):
    sums = jnp.zeros((8, 128), F32)
    for other in range(COLS):
        sums = sums + came[other, 0:8, :]
    found = jnp.where(iota((8, 128), 0) < 4, sums, 0.0) / divisor[...]
    hole[...] = found
    if tile is not None:
        pieces = came[:, 4, :]
        share = shares(per_block, found) + pieces[:, 0:1]
        share = share + pltpu.roll(pieces, 1, 0)[:, 3:4] + pltpu.roll(pieces, COLS - 1, 0)[:, 4:5]
        tile[...] = jnp.where(iota((COLS, 128), 1) == 0, share, pieces)


def close_wells_body(came, divisor, per_block, from_low, from_high, hole, tile):
    sum_wells_body(came, divisor, per_block, hole, tile)


def coupling_planes(
    hole,
    swept,
    from_low,
    from_high,
    came,
    mobility,
    face_x,
    face_y,
    face_z,
    cell,
    label,
    index,
):
    col = lax.axis_index("col")
    faces = (face_x, face_y, face_z)
    back = to_cells(hole[...], index, marks_of(cell, label))
    below = jnp.maximum(col - 1, 0)
    above = jnp.minimum(col + 1, COLS - 1)
    y_low = jnp.concatenate([came[below, 8:16, :], came[below, 16:24, :]], 1)
    y_high = jnp.concatenate([came[above, 8:16, :], came[above, 16:24, :]], 1)
    planes = [swept[x] for x in range(8)]
    for x in range(8):
        around = neighbours(planes, x, from_low[...], from_high[...], y_low, y_high)
        for k in range(3):
            value = gathered(faces, k, x, planes[x], around)
            yield k, x, value + mobility[k, x] * back[x * 8 : x * 8 + 8]


def first_image_body(*rest):
    *rest, tied = rest
    for k, x, value in coupling_planes(*rest):
        tied[k, x] = -value


def second_image_body(divisor, right, tied, *rest):
    *rest, image, outgoing, hole = rest
    sum_wells_body(rest[3], divisor, None, hole, None)
    totals = [jnp.zeros((8, 256), F32) for _ in range(5)]
    for k, x, value in coupling_planes(hole, *rest):
        value = tied[k, x] - value
        image[k, x] = value
        goal = right[k, x]
        one = goal + tied[k, x]
        for n, term in enumerate((one * one, one * value, value * value, one * goal, value * goal)):
            totals[n] = totals[n] + term
    broadcast_rows(outgoing, jnp.zeros((1, 1), F32), [total_of(t) for t in totals])


def update_body(last, *refs):
    (
        met,
        current,
        acc_diag,
        porosity,
        right,
        tied,
        image,
        first_swept,
        first_level,
        first_direction,
        second_swept,
        second_level,
        second_direction,
        *outs,
    ) = refs
    sums = jnp.sum(met[...], 0, keepdims=True)
    g00, g01, g11, t0, t1 = [sums[:, 127 - n : 128 - n] for n in range(5)]
    l00 = jnp.sqrt(g00)
    l10 = g01 / l00
    l11 = jnp.sqrt(g11 - l10 * l10)
    f0 = t0 / l00
    f1 = (t1 - l10 * f0) / l11
    y1 = f1 / l11
    y0 = (f0 - l10 * y1) / l00
    shift = y0 * first_level[0:1, 0:1] + y1 * second_level[0:1, 0:1]
    if last:
        fresh, residual = outs
    else:
        mobility, face_x, face_y, face_z, density, fresh, residual, inverse, outgoing = outs
    mean = jnp.zeros((8, 256), F32)
    for x in range(8):
        remainder = []
        slopes = []
        for k in range(3):
            old = current[k, x]
            if k == 0:
                step = y0 * first_swept[x] + y1 * second_swept[x] + shift
            else:
                step = y0 * first_direction[k - 1, x] + y1 * second_direction[k - 1, x]
            new = old + step
            fresh[k, x] = new
            before = jnp.tanh(old)
            after = jnp.tanh(new)
            remainder.append(0.5 * ((after - before) - (1.0 - before * before) * step))
            slopes.append(1.5 - 0.5 * after * after)
        for k in range(3):
            goal = right[k, x]
            value = (
                goal
                - y0 * (goal + tied[k, x])
                - y1 * image[k, x]
                - coupled(acc_diag, porosity, k, x, remainder)
            )
            residual[k, x] = -value if last else value
            mean = mean + value
        if not last:
            diagonal = []
            for k in range(3):
                total = face_x[k, x + 1] + face_x[k, x] + (face_y[0, k, x] + face_y[1, k, x])
                total = total + (face_z[k, x] + pltpu.roll(face_z[k, x], 1, 1))
                diagonal.append(total + mobility[k, x] * density[x * 8 : x * 8 + 8, :])
            invert(slopes, acc_diag, porosity, diagonal, x, inverse)
    if not last:
        broadcast_rows(outgoing, total_of(mean) * (1.0 / CELLS))


def per_device(
    state,
    acc_diag,
    porosity,
    mobility,
    trans_x,
    trans_y,
    trans_z,
    perf_cell,
    perf_owner,
    perf_well,
    perf_index,
    perf_head,
    well_stiff,
    well_drive,
    coarse_inverse,
):
    field = (8, 8, 256)
    triple = (3, *field)
    plane = (8, 256)
    count = perf_cell.shape[1]

    def ring(value, axis, count, shift):
        return lax.ppermute(value, axis, [(i, (i + shift) % count) for i in range(count)])

    def swap_cols(value):
        return lax.all_to_all(value, "col", 0, 0, tiled=True)

    def swap_all(value):
        return lax.all_to_all(value, ("row", "col"), 0, 0, tiled=True)

    def exchange(to_high, to_low, outgoing):
        return (
            ring(to_high, "row", ROWS, 1),
            ring(to_low, "row", ROWS, -1),
            swap_cols(outgoing),
        )

    vmem = pl.BlockSpec(memory_space=pltpu.VMEM)
    hbm = pl.BlockSpec(memory_space=pltpu.HBM)

    def run(body, outs, *args, scratch=(), far=(), far_outs=(), room=ROOM):
        specs = [hbm if n in far else vmem for n in range(len(args))]
        return pl.pallas_call(
            body,
            out_shape=[
                pltpu.HBM(s, t) if n in far_outs else jax.ShapeDtypeStruct(s, t)
                for n, (s, t) in enumerate(outs)
            ],
            in_specs=specs,
            out_specs=[hbm if n in far_outs else vmem for n in range(len(outs))],
            scratch_shapes=list(scratch),
            compiler_params=pltpu.CompilerParams(vmem_limit_bytes=room),
        )(
            *(
                pltpu.with_memory_space_constraint(arg, pltpu.HBM) if n in far else arg
                for n, arg in enumerate(args)
            )
        )

    def buffers(*values):
        return [pltpu.VMEM(value.shape, value.dtype) for value in values]

    line = (1, count)
    packs = run(
        pack_body,
        [((80, 128), F32), ((64, 128), F32), ((80, 128), F32), ((64, 128), F32)],
        state,
        mobility,
        trans_x,
        trans_y,
        scratch=[
            pltpu.VMEM(field, F32),
            pltpu.VMEM(triple, F32),
            pltpu.VMEM(plane, F32),
            pltpu.VMEM(field, F32),
            pltpu.SemaphoreType.DMA((4,)),
        ],
        far=range(4),
        room=FIRST_ROOM,
    )
    up_x, down_x, up_y, down_y = packs
    halos = (
        ring(up_x, "row", ROWS, 1),
        ring(down_x, "row", ROWS, -1),
        ring(up_y, "col", COLS, 1),
        ring(down_y, "col", COLS, -1),
    )
    cell, label, index, density, pulled, sums = run(
        prepare_body,
        [
            (line, jnp.int32),
            (line, jnp.int32),
            (line, F32),
            ((64, 256), F32),
            ((64, 256), F32),
            ((16, 128), F32),
        ],
        state,
        mobility,
        perf_cell,
        perf_owner,
        perf_well,
        perf_index,
        perf_head,
        well_stiff,
        well_drive,
        scratch=[
            pltpu.VMEM(field, F32),
            pltpu.VMEM(triple, F32),
            *buffers(perf_owner, perf_well, perf_head, well_stiff, well_drive),
            pltpu.SemaphoreType.DMA((9,)),
        ],
        far=range(9),
    )
    marks = (cell, label, index)
    (outgoing,) = run(border_body, [((COLS, 16, 128), F32)], *packs, *halos, sums)
    well_tile = (8, 128)
    divisor, per_block, hole, tile = run(
        open_wells_body,
        [(well_tile, F32), ((4, COLS, 128), F32), (well_tile, F32), ((2 * COLS, 128), F32)],
        swap_cols(outgoing),
        coarse_inverse,
    )
    face_x, face_y, face_z, inner, edges, inverse, right = run(
        start_body,
        [
            ((3, 9, *plane), F32),
            ((2, *triple), F32),
            (triple, F32),
            (field, F32),
            ((4, *plane), F32),
            ((3, *triple), F32),
            (triple, F32),
        ],
        state,
        acc_diag,
        porosity,
        mobility,
        trans_x,
        trans_y,
        trans_z,
        *halos,
        density,
        pulled,
        hole,
        *marks,
        scratch=[
            *buffers(state, acc_diag, porosity, mobility, trans_x, trans_y, trans_z),
            pltpu.VMEM(triple, F32),
            pltpu.SemaphoreType.DMA((7,)),
        ],
        far=range(7),
    )
    faces = (face_x, face_y, face_z)
    current = state
    solve = None
    sends = [((2, *field), F32), (plane, F32), (plane, F32), ((COLS, 24, 128), F32)]
    sends += [(field, F32), (well_tile, F32)]
    send_scratch = [
        pltpu.VMEM((2, *field), F32),
        pltpu.VMEM((COLS, 8, 128), F32),
        pltpu.VMEM((COLS, 16, 128), F32),
        pltpu.SemaphoreType.DMA((3,)),
    ]
    coarse_scratch = [pltpu.VMEM((DEVS, 128), F32)] * 2

    def spread_rows(tile):
        return (tile, *(ring(tile, "row", ROWS, shift) for shift in (1, 2, 3)))

    for outer in range(NEWTON):
        static = (mobility, *faces, inner, edges, inverse, divisor, per_block, *marks)
        if outer == 0:
            first_direction, to_high, to_low, outgoing, first_swept, first_level, solve = run(
                opening_direction_body,
                [*sends, ((DEVS, DEVS), F32)],
                *spread_rows(tile),
                right,
                *static,
                scratch=[*send_scratch, *coarse_scratch],
                far_outs=(0, 3),
            )
        else:
            first_direction, to_high, to_low, outgoing, first_swept, first_level = run(
                direction_body,
                sends,
                solve,
                swap_all(outgoing),
                right,
                *static,
                scratch=[*send_scratch, *coarse_scratch],
                far_outs=(0, 3),
            )
        from_low, from_high, came = exchange(to_high, to_low, outgoing)
        hole, tile = run(
            close_wells_body,
            [(well_tile, F32), ((COLS, 128), F32)],
            came,
            divisor,
            per_block,
            from_low,
            from_high,
        )
        (tied,) = run(
            first_image_body,
            [(triple, F32)],
            hole,
            first_swept,
            from_low,
            from_high,
            came,
            mobility,
            *faces,
            *marks,
        )
        second_direction, to_high, to_low, outgoing, second_swept, second_level = run(
            gathered_direction_body,
            sends,
            solve,
            *spread_rows(tile),
            tied,
            *static,
            scratch=[*send_scratch, *coarse_scratch],
            far_outs=(0, 3),
        )
        image, outgoing = run(
            second_image_body,
            [(triple, F32), ((DEVS, 128), F32)],
            divisor,
            right,
            tied,
            second_swept,
            *exchange(to_high, to_low, outgoing),
            mobility,
            *faces,
            *marks,
            scratch=[pltpu.VMEM(well_tile, F32)],
        )
        met = swap_all(outgoing)
        last = outer == NEWTON - 1
        outs = [(triple, F32), (triple, F32)]
        extra = ()
        if not last:
            outs += [((3, *triple), F32), ((DEVS, 128), F32)]
            extra = (mobility, *faces, density)
        results = run(
            lambda *refs: update_body(last, *refs),
            outs,
            met,
            current,
            acc_diag,
            porosity,
            right,
            tied,
            image,
            first_swept,
            first_level,
            first_direction,
            second_swept,
            second_level,
            second_direction,
            *extra,
        )
        if last:
            return tuple(results)
        current, right, inverse, outgoing = results


def solution(mesh):
    in_specs = (
        P(None, "row", "col", None),
        P(None, "row", "col", None),
        P("row", "col", None),
        P(None, "row", "col", None),
        P("row", "col", None),
        P("row", "col", None),
        P("row", "col", None),
        P("row", "col"),
        P("row", "col"),
        P("row", "col"),
        P("row", "col"),
        P("row", "col"),
        P("row", "col"),
        P("row", "col"),
        P("row", None),
    )
    out_specs = (P(None, "row", "col", None), P(None, "row", "col", None))
    return jax.shard_map(
        per_device, mesh=mesh, in_specs=in_specs, out_specs=out_specs, check_vma=False
    )
```

```python
import jax
import jax.numpy as jnp
from jax import lax
from jax.experimental import pallas as pl
from jax.experimental.pallas import tpu as pltpu
from jax.sharding import PartitionSpec as P

NEWTON = 2
WELLS_DEV = 16
EXACT = lax.Precision.HIGHEST
COUPLING = ((0.0, 0.3, 0.2), (0.25, 0.0, 0.15), (0.2, 0.1, 0.0))
ROWS = 4
COLS = 32
DEVS = ROWS * COLS
CELLS = 8 * 8 * 256
F32 = jnp.float32
BF16 = jnp.bfloat16
ROOM = 24_000_000
FIRST_ROOM = 66_700_000


def iota(shape, dim):
    return lax.broadcasted_iota(jnp.int32, shape, dim)


def split(value):
    high = value.astype(BF16)
    low = (value - high.astype(F32)).astype(BF16)
    return jnp.concatenate([high, low], 0)


def joined(pair):
    half = pair.shape[0] // 2
    return pair[:half] + pair[half:]


def nn(a, b):
    return lax.dot_general(a, b, (((1,), (0,)), ((), ())), preferred_element_type=F32)


def nt(a, b):
    return lax.dot_general(a, b, (((1,), (1,)), ((), ())), preferred_element_type=F32)


def one_hot(rows, key):
    key = key.astype(F32).astype(BF16)
    line = iota((rows, 128), 0).astype(F32).astype(BF16)
    one = jnp.ones((rows, 128), BF16)
    none = jnp.zeros((rows, 128), BF16)
    return jnp.concatenate(
        [
            jnp.where(line == key[:, start : start + 128], one, none)
            for start in range(0, key.shape[1], 128)
        ],
        1,
    )


def marks_of(cell, label):
    count = cell.shape[1]
    layer = one_hot(256, cell[...] & 255)
    place = jnp.where(iota((64, count), 0) == (cell[...] >> 8), 1.0, 0.0)
    low_mark = one_hot(128, label[...] & 127)
    high_mark = jnp.where(iota((8, count), 0) == (label[...] >> 7), 1.0, 0.0)
    return layer, place, low_mark, high_mark


def keep(marks, targets):
    for value, target in zip(marks, targets):
        target[...] = value


def to_wells(field, index, marks):
    layer, place, low_mark, high_mark = marks
    picked = joined(nn(split(field), layer))
    value = index[...] * jnp.sum(picked * place, 0, keepdims=True)
    return joined(nt(split(high_mark * value), low_mark))


def to_cells(per_well, index, marks):
    layer, place, low_mark, high_mark = marks
    spread = joined(nn(split(per_well), low_mark))
    value = index[...] * jnp.sum(spread * high_mark, 0, keepdims=True)
    return joined(nt(split(place * value), layer))


def write_plane(ref, base, plane):
    ref[base : base + 8, :] = plane[:, :128]
    ref[base + 8 : base + 16, :] = plane[:, 128:]


def read_plane(ref, base):
    return jnp.concatenate([ref[base : base + 8, :], ref[base + 8 : base + 16, :]], 1)


def fetch(pairs, sems):
    copies = [
        pltpu.make_async_copy(source, target, sems.at[n]) for n, (source, target) in enumerate(pairs)
    ]
    for copy in copies:
        copy.start()
    return copies


def pack_body(
    state,
    mobility,
    trans_x,
    trans_y,
    up_x,
    down_x,
    up_y,
    down_y,
    pressure,
    carried,
    along_x,
    along_y,
    sems,
):
    copies = fetch(
        (
            (mobility, carried),
            (state.at[0], pressure),
            (trans_x.at[7], along_x),
            (trans_y, along_y),
        ),
        sems,
    )
    for copy in copies:
        copy.wait()
    for k in range(3):
        write_plane(up_x, 16 * k, carried[k, 7])
        write_plane(down_x, 16 * k, carried[k, 0])
        write_plane(up_y, 16 * k, carried[k, :, 7, :])
        write_plane(down_y, 16 * k, carried[k, :, 0, :])
    write_plane(up_x, 48, pressure[7])
    write_plane(down_x, 48, pressure[0])
    write_plane(up_y, 48, pressure[:, 7, :])
    write_plane(down_y, 48, pressure[:, 0, :])
    write_plane(up_x, 64, along_x[...])
    write_plane(up_y, 64, along_y[:, 7, :])


def prepare_body(
    state,
    mobility,
    cell_in,
    owner_in,
    well_in,
    index_in,
    head_in,
    stiff_in,
    drive_in,
    cell,
    label,
    index,
    density,
    pulled,
    sums,
    pressure,
    carried,
    owner,
    well,
    head,
    stiff,
    drive,
    sems,
):
    copies = fetch(
        (
            (cell_in, cell),
            (owner_in, owner),
            (well_in, well),
            (index_in, index),
            (head_in, head),
            (stiff_in, stiff),
            (drive_in, drive),
            (mobility, carried),
            (state.at[0], pressure),
        ),
        sems,
    )
    for copy in copies:
        copy.wait()
    label[...] = owner[...] * WELLS_DEV + well[...]
    layer, place, low_mark, high_mark = marks_of(cell, label)
    both = jnp.concatenate([place * index[...], place * (index[...] * head[...])], 0)
    spread = joined(nt(split(both), layer))
    density[...] = spread[:64]
    pulled[...] = spread[64:]
    total = (carried[0] + carried[1] + carried[2]).reshape(64, 256)
    pair = split(jnp.concatenate([total, total * pressure[...].reshape(64, 256)], 0))
    picked = joined(nn(pair, layer)) * jnp.concatenate([place, place], 0)
    base = index[...] * jnp.sum(picked[:64], 0, keepdims=True)
    terms = index[...] * jnp.sum(picked[64:], 0, keepdims=True) - base * head[...]
    local = joined(nt(split(jnp.concatenate([high_mark * base, high_mark * terms], 0)), low_mark))
    me = lax.axis_index("col")
    tile = jnp.where(iota((WELLS_DEV, 128), 1) % WELLS_DEV == iota((WELLS_DEV, 128), 0), 1.0, 0.0)
    lines = jnp.concatenate([stiff[...], drive[...], jnp.zeros((6, WELLS_DEV), F32)], 0)
    lines = jnp.dot(lines, tile, precision=EXACT, preferred_element_type=F32)
    mine = (iota((8, 128), 1) // WELLS_DEV == me % 8) & (iota((8, 128), 0) % 4 == me // 8)
    upper = iota((8, 128), 0) < 4
    extra = jnp.where(mine, jnp.where(upper, lines[1:2], lines[0:1]), 0.0)
    corner = (iota((8, 128), 0) == 4) & (iota((8, 128), 1) == 0)
    sums[0:8, :] = jnp.where(corner, jnp.sum(terms, 1, keepdims=True) * -1.0, local[:8])
    sums[8:16, :] = jnp.where(upper, local[8:], 0.0) + extra


def inside_flags():
    row = lax.axis_index("row")
    col = lax.axis_index("col")
    return (
        jnp.where(row > 0, 1.0, 0.0),
        jnp.where(row < ROWS - 1, 1.0, 0.0),
        jnp.where(col > 0, 1.0, 0.0),
        jnp.where(col < COLS - 1, 1.0, 0.0),
    )


def border_body(
    up_x, down_x, up_y, down_y, from_low_x, from_high_x, from_low_y, from_high_y, sums, outgoing
):
    low_x, high_x, low_y, high_y = inside_flags()

    def crossing(lower, upper, inside):
        mobile = read_plane(lower, 0) + read_plane(upper, 0)
        for k in (1, 2):
            mobile = mobile + read_plane(lower, 16 * k) + read_plane(upper, 16 * k)
        rate = read_plane(lower, 64) * 0.5 * mobile
        return rate * (read_plane(lower, 48) - read_plane(upper, 48)) * inside

    net = crossing(up_x, from_high_x, high_x) - crossing(from_low_x, down_x, low_x)
    net = net + crossing(up_y, from_high_y, high_y) - crossing(from_low_y, down_y, low_y)
    corner = (iota((8, 128), 0) == 4) & (iota((8, 128), 1) == 0)
    first = sums[0:8, :] - jnp.where(corner, total_of(net), 0.0)
    second = sums[8:16, :]
    for other in range(COLS):
        outgoing[other, 0:8, :] = first
        outgoing[other, 8:16, :] = second


def neighbours(planes, x, x_low, x_high, y_low, y_high):
    plane = planes[x]
    line = iota((8, 256), 0)
    return (
        planes[x + 1] if x < 7 else x_high,
        planes[x - 1] if x > 0 else x_low,
        jnp.where(line == 7, y_high[x : x + 1], pltpu.roll(plane, 7, 0)),
        jnp.where(line == 0, y_low[x : x + 1], pltpu.roll(plane, 1, 0)),
        pltpu.roll(plane, 255, 1),
    )


def gathered(faces, k, x, plane, around):
    face_x, face_y, face_z = faces
    ahead = face_z[k, x]
    return (
        face_x[k, x + 1] * around[0]
        + face_x[k, x] * around[1]
        + (face_y[0, k, x] * around[2] + face_y[1, k, x] * around[3])
        + (ahead * around[4] + pltpu.roll(ahead * plane, 1, 1))
    )


def coupled(acc_diag, porosity, k, x, terms):
    total = acc_diag[k, x] * terms[k]
    mixed = None
    for j in range(3):
        if COUPLING[k][j] != 0.0:
            part = COUPLING[k][j] * terms[j]
            mixed = part if mixed is None else mixed + part
    return total + porosity[x] * mixed


def invert(slopes, acc_diag, porosity, diagonal, x, inverse):
    m = []
    for k in range(3):
        line = []
        for j in range(3):
            if j == k:
                entry = acc_diag[k, x] * slopes[k]
            else:
                entry = porosity[x] * COUPLING[k][j] * slopes[j]
            if j == 0:
                entry = entry + diagonal[k]
            line.append(entry)
        m.append(line)
    cofactor = [
        [
            m[1][1] * m[2][2] - m[1][2] * m[2][1],
            m[1][2] * m[2][0] - m[1][0] * m[2][2],
            m[1][0] * m[2][1] - m[1][1] * m[2][0],
        ],
        [
            m[0][2] * m[2][1] - m[0][1] * m[2][2],
            m[0][0] * m[2][2] - m[0][2] * m[2][0],
            m[0][1] * m[2][0] - m[0][0] * m[2][1],
        ],
        [
            m[0][1] * m[1][2] - m[0][2] * m[1][1],
            m[0][2] * m[1][0] - m[0][0] * m[1][2],
            m[0][0] * m[1][1] - m[0][1] * m[1][0],
        ],
    ]
    determinant = m[0][0] * cofactor[0][0] + m[0][1] * cofactor[0][1] + m[0][2] * cofactor[0][2]
    reciprocal = 1.0 / determinant
    for k in range(3):
        for j in range(3):
            inverse[k, j, x] = cofactor[j][k] * reciprocal


def total_of(plane):
    return jnp.sum(jnp.sum(plane, 1, keepdims=True), 0, keepdims=True)


def broadcast_rows(outgoing, mean, dots=()):
    lane = iota((1, 128), 1)
    row = jnp.broadcast_to(mean, (1, 128))
    for n, dot in enumerate(dots):
        row = jnp.where(lane == 127 - n, dot, row)
    outgoing[...] = jnp.broadcast_to(row, (DEVS, 128))


def start_body(
    state_in,
    acc_in,
    porosity_in,
    mobility_in,
    trans_x_in,
    trans_y_in,
    trans_z_in,
    from_low_x,
    from_high_x,
    from_low_y,
    from_high_y,
    density,
    pulled,
    hole,
    cell,
    label,
    index,
    face_x,
    face_y,
    face_z,
    inner,
    edges,
    inverse,
    right,
    layer,
    place,
    low_mark,
    high_mark,
    state,
    acc_diag,
    porosity,
    mobility,
    trans_x,
    trans_y,
    trans_z,
    diagonal,
    sems,
):
    copies = fetch(
        (
            (mobility_in, mobility),
            (trans_x_in, trans_x),
            (trans_y_in, trans_y),
            (trans_z_in, trans_z),
            (state_in, state),
            (acc_in, acc_diag),
            (porosity_in, porosity),
        ),
        sems,
    )
    marks = marks_of(cell, label)
    keep(marks, (layer, place, low_mark, high_mark))
    back = to_cells(hole[...], index, marks)
    low_x, high_x, low_y, high_y = inside_flags()
    lane = iota((8, 256), 1)
    line = iota((8, 256), 0)
    t_low_x = read_plane(from_low_x, 64) * low_x
    t_low_y = read_plane(from_low_y, 64) * low_y
    for copy in copies[:4]:
        copy.wait()
    for k in range(3):
        m_low_x = read_plane(from_low_x, 16 * k)
        m_high_x = read_plane(from_high_x, 16 * k)
        m_low_y = read_plane(from_low_y, 16 * k)
        m_high_y = read_plane(from_high_y, 16 * k)
        previous = t_low_x * 0.5 * (m_low_x + mobility[k, 0])
        face_x[k, 0] = previous
        planes = [mobility[k, x] for x in range(8)]
        for x in range(8):
            here = planes[x]
            around = neighbours(planes, x, m_low_x, m_high_x, m_low_y, m_high_y)
            tx = trans_x[x] if x < 7 else trans_x[x] * high_x
            ahead = tx * 0.5 * (here + around[0])
            face_x[k, x + 1] = ahead
            total = ahead + previous
            previous = ahead
            ty = jnp.where(line == 7, trans_y[x] * high_y, trans_y[x])
            ahead_y = ty * 0.5 * (here + around[2])
            entering = t_low_y[x : x + 1] * 0.5 * (m_low_y[x : x + 1] + here[0:1])
            behind_y = jnp.where(line == 0, entering, pltpu.roll(ahead_y, 1, 0))
            face_y[0, k, x] = ahead_y
            face_y[1, k, x] = behind_y
            total = total + (ahead_y + behind_y)
            ahead_z = jnp.where(lane < 255, trans_z[x] * 0.5 * (here + around[4]), 0.0)
            face_z[k, x] = ahead_z
            total = total + (ahead_z + pltpu.roll(ahead_z, 1, 1))
            diagonal[k, x] = total + here * density[x * 8 : x * 8 + 8, :]

    def summed(face, *place):
        return face[0, *place] + face[1, *place] + face[2, *place]

    edges[0] = summed(face_x, 8)
    edges[1] = summed(face_x, 0)
    edges[2] = face_y[0, 0, :, 7, :] + face_y[0, 1, :, 7, :] + face_y[0, 2, :, 7, :]
    edges[3] = face_y[1, 0, :, 0, :] + face_y[1, 1, :, 0, :] + face_y[1, 2, :, 0, :]
    halo = (
        read_plane(from_low_x, 48),
        read_plane(from_high_x, 48),
        read_plane(from_low_y, 48),
        read_plane(from_high_y, 48),
    )
    for copy in copies[4:]:
        copy.wait()
    planes = [state[0, x] for x in range(8)]
    for x in range(8):
        up_z = summed(face_z, x)
        kept = up_z + pltpu.roll(up_z, 1, 1)
        kept = kept + jnp.where(line < 7, summed(face_y.at[0], x), 0.0)
        kept = kept + jnp.where(line > 0, summed(face_y.at[1], x), 0.0)
        if x < 7:
            kept = kept + summed(face_x, x + 1)
        if x > 0:
            kept = kept + summed(face_x, x)
        inner[x] = kept
        around = neighbours(planes, x, *halo)
        source = pulled[x * 8 : x * 8 + 8, :] + back[x * 8 : x * 8 + 8]
        for k in range(3):
            value = (
                gathered((face_x, face_y, face_z), k, x, planes[x], around)
                + mobility[k, x] * source
                - diagonal[k, x] * planes[x]
            )
            right[k, x] = value
        slopes = []
        for k in range(3):
            bent = jnp.tanh(state[k, x])
            slopes.append(1.5 - 0.5 * bent * bent)
        invert(slopes, acc_diag, porosity, [diagonal[k, x] for k in range(3)], x, inverse)


def shares(per_block, hole):
    share = per_block[0] * hole[0:1]
    for a in range(1, 4):
        share = share + per_block[a] * hole[a : a + 1]
    return jnp.sum(share, 1, keepdims=True)


def open_wells_body(arrived, coarse, divisor, per_block, hole, tile):
    totals = jnp.zeros((8, 128), F32)
    others = jnp.zeros((8, 128), F32)
    for other in range(COLS):
        totals = totals + arrived[other, 0:8, :]
        others = others + arrived[other, 8:16, :]
    blocks = [arrived[:, a, :] for a in range(4)]
    for a in range(4):
        per_block[a] = blocks[a]
    upper = iota((8, 128), 0) < 4
    div = jnp.where(upper, totals + pltpu.roll(others, 4, 0), 1.0)
    divisor[...] = div
    found = jnp.where(upper, others, 0.0) / div
    hole[...] = found
    share = shares(blocks, found) + arrived[:, 4, 0:1]
    tile[0:32, :] = jnp.where(iota((COLS, 128), 1) == 0, share * -1.0, 0.0)
    tile[32:64, :] = coarse[...]


def find_direction(stored, coarse_x, *refs):
    (
        vector,
        mobility,
        face_x,
        face_y,
        face_z,
        inner,
        edges,
        inverse,
        divisor,
        per_block,
        *refs,
    ) = refs
    if stored:
        layer, place, low_mark, high_mark, index, *refs = refs
        marks = (layer[...], place[...], low_mark[...], high_mark[...])
    else:
        cell, label, index, *refs = refs
        marks = marks_of(cell, label)
    (
        direction_out,
        to_high,
        to_low,
        outgoing,
        swept,
        level,
        direction,
        for_wells,
        for_sides,
        sems,
    ) = refs
    row = lax.axis_index("row")
    col = lax.axis_index("col")
    faces = (face_x, face_y, face_z)

    def wide(at_row, at_col):
        place = at_col * ROWS + at_row
        value = coarse_x[pl.ds(place, 1), :]
        return jnp.broadcast_to(jnp.concatenate([value, value], 1), (8, 256))

    own = wide(row, col)
    x_high = wide(jnp.minimum(row + 1, ROWS - 1), col)
    x_low = wide(jnp.maximum(row - 1, 0), col)
    y_high = wide(row, jnp.minimum(col + 1, COLS - 1))
    y_low = wide(row, jnp.maximum(col - 1, 0))
    level[...] = own[:, :128]
    weights = coarse_x[pl.ds(row, COLS, stride=ROWS), :]
    sums = [jnp.sum(weights * per_block[a], 0, keepdims=True) for a in range(4)]
    sums = jnp.concatenate([*sums, jnp.zeros((4, 128), F32)], 0)
    back = to_cells(sums / divisor[...], index, marks)
    line = iota((8, 256), 0)
    up_y = jnp.where(line == 7, y_high, own)
    down_y = jnp.where(line == 0, y_low, own)
    weighted = []
    inside = jnp.zeros((8, 256), F32)
    for x in range(8):
        around = (own if x < 7 else x_high, own if x > 0 else x_low, up_y, down_y, own)
        terms = [
            vector[k, x] + gathered(faces, k, x, own, around) + mobility[k, x] * back[x * 8 : x * 8 + 8]
            for k in range(3)
        ]
        for k in range(3):
            value = (
                inverse[k, 0, x] * terms[0]
                + inverse[k, 1, x] * terms[1]
                + inverse[k, 2, x] * terms[2]
            )
            if k == 0:
                kept = value - own
                swept[x] = kept
            else:
                direction[k - 1, x] = value
        inside = inside + kept * inner[x]
        weighted.append(kept * (mobility[0, x] + mobility[1, x] + mobility[2, x]))
    to_high[...] = swept[7]
    to_low[...] = swept[0]
    last = swept[:, 7, :]
    first = swept[:, 0, :]
    for other in range(COLS):
        send = jnp.where(other < col, first, last)
        for_sides[other, 0:8, :] = send[:, :128]
        for_sides[other, 8:16, :] = send[:, 128:]
    side_copy = pltpu.make_async_copy(for_sides, outgoing.at[:, 8:24, :], sems.at[0])
    side_copy.start()
    direction_copy = pltpu.make_async_copy(direction, direction_out, sems.at[2])
    direction_copy.start()
    local = to_wells(jnp.concatenate(weighted, 0), index, marks)
    sides = (swept[7] * edges[0], swept[0] * edges[1], last * edges[2], first * edges[3])
    lane = iota((8, 128), 1)
    for n, term in enumerate((inside, *sides)):
        local = jnp.where((iota((8, 128), 0) == 4) & (lane == n), total_of(term), local)
    for other in range(COLS):
        for_wells[other] = local
    well_copy = pltpu.make_async_copy(for_wells, outgoing.at[:, 0:8, :], sems.at[1])
    well_copy.start()
    direction_copy.wait()
    side_copy.wait()
    well_copy.wait()


def coarse_solve(solve, means, ordered, coarse_x):
    for r in range(ROWS):
        ordered[pl.ds(r, COLS, stride=ROWS), :] = means[r * COLS : (r + 1) * COLS, :]
    coarse_x[...] = jnp.dot(solve[...], ordered[...], precision=EXACT, preferred_element_type=F32)


def direction_body(solve, received, *rest):
    *rest, ordered, coarse_x = rest
    coarse_solve(solve, received, ordered, coarse_x)
    find_direction(False, coarse_x, *rest)


def place_rows(sources, target, base):
    for shift, source in enumerate(sources):
        start = pl.multiple_of(((lax.axis_index("row") - shift + ROWS) % ROWS) * COLS, COLS)
        target[pl.ds(start, COLS), :] = source[base : base + COLS, :]


def from_rows(solve, sources, rest, opening):
    *rest, ordered, coarse_x = rest
    place_rows(sources, coarse_x, 0)
    every = coarse_x[...]
    means = every[:, 0:1]
    if not opening:
        means = means + pltpu.roll(every, COLS, 0)[:, 1:2]
        means = means + pltpu.roll(every, DEVS - COLS, 0)[:, 2:3]
    means = jnp.broadcast_to(means * (-1.0 / CELLS), (DEVS, 128))
    coarse_solve(solve, means, ordered, coarse_x)
    find_direction(True, coarse_x, *rest)


def gathered_direction_body(solve, own, low, far, high, *rest):
    from_rows(solve, (own, low, far, high), rest, False)


def opening_direction_body(own, low, far, high, *rest):
    *rest, solve, direction, for_wells, for_sides, sems, ordered, coarse_x = rest
    place_rows((own, low, far, high), solve, COLS)
    rest = (*rest, direction, for_wells, for_sides, sems, ordered, coarse_x)
    from_rows(solve, (own, low, far, high), rest, True)


def sum_wells_body(came, divisor, per_block, hole, tile):
    sums = jnp.zeros((8, 128), F32)
    for other in range(COLS):
        sums = sums + came[other, 0:8, :]
    found = jnp.where(iota((8, 128), 0) < 4, sums, 0.0) / divisor[...]
    hole[...] = found
    if tile is not None:
        pieces = came[:, 4, :]
        share = shares(per_block, found) + pieces[:, 0:1]
        share = share + pltpu.roll(pieces, 1, 0)[:, 3:4] + pltpu.roll(pieces, COLS - 1, 0)[:, 4:5]
        tile[...] = jnp.where(iota((COLS, 128), 1) == 0, share, pieces)


def close_wells_body(came, divisor, per_block, from_low, from_high, hole, tile):
    sum_wells_body(came, divisor, per_block, hole, tile)


def coupling_planes(
    hole,
    swept,
    from_low,
    from_high,
    came,
    mobility,
    face_x,
    face_y,
    face_z,
    cell,
    label,
    index,
    kept=(),
):
    col = lax.axis_index("col")
    faces = (face_x, face_y, face_z)
    marks = marks_of(cell, label)
    keep(marks, kept)
    back = to_cells(hole[...], index, marks)
    below = jnp.maximum(col - 1, 0)
    above = jnp.minimum(col + 1, COLS - 1)
    y_low = jnp.concatenate([came[below, 8:16, :], came[below, 16:24, :]], 1)
    y_high = jnp.concatenate([came[above, 8:16, :], came[above, 16:24, :]], 1)
    planes = [swept[x] for x in range(8)]
    for x in range(8):
        around = neighbours(planes, x, from_low[...], from_high[...], y_low, y_high)
        for k in range(3):
            value = gathered(faces, k, x, planes[x], around)
            yield k, x, value + mobility[k, x] * back[x * 8 : x * 8 + 8]


def first_image_body(*rest):
    *rest, tied, layer, place, low_mark, high_mark = rest
    for k, x, value in coupling_planes(*rest, kept=(layer, place, low_mark, high_mark)):
        tied[k, x] = -value


def second_image_body(divisor, right, tied, *rest):
    *rest, image, outgoing, hole = rest
    sum_wells_body(rest[3], divisor, None, hole, None)
    totals = [jnp.zeros((8, 256), F32) for _ in range(5)]
    for k, x, value in coupling_planes(hole, *rest):
        value = tied[k, x] - value
        image[k, x] = value
        goal = right[k, x]
        one = goal + tied[k, x]
        for n, term in enumerate((one * one, one * value, value * value, one * goal, value * goal)):
            totals[n] = totals[n] + term
    broadcast_rows(outgoing, jnp.zeros((1, 1), F32), [total_of(t) for t in totals])


def update_body(last, *refs):
    (
        met,
        current,
        acc_diag,
        porosity,
        right,
        tied,
        image,
        first_swept,
        first_level,
        first_direction,
        second_swept,
        second_level,
        second_direction,
        *outs,
    ) = refs
    sums = jnp.sum(met[...], 0, keepdims=True)
    g00, g01, g11, t0, t1 = [sums[:, 127 - n : 128 - n] for n in range(5)]
    l00 = jnp.sqrt(g00)
    l10 = g01 / l00
    l11 = jnp.sqrt(g11 - l10 * l10)
    f0 = t0 / l00
    f1 = (t1 - l10 * f0) / l11
    y1 = f1 / l11
    y0 = (f0 - l10 * y1) / l00
    shift = y0 * first_level[0:1, 0:1] + y1 * second_level[0:1, 0:1]
    if last:
        fresh, residual = outs
    else:
        mobility, face_x, face_y, face_z, density, fresh, residual, inverse, outgoing = outs
    mean = jnp.zeros((8, 256), F32)
    for x in range(8):
        remainder = []
        slopes = []
        for k in range(3):
            old = current[k, x]
            if k == 0:
                step = y0 * first_swept[x] + y1 * second_swept[x] + shift
            else:
                step = y0 * first_direction[k - 1, x] + y1 * second_direction[k - 1, x]
            new = old + step
            fresh[k, x] = new
            before = jnp.tanh(old)
            after = jnp.tanh(new)
            remainder.append(0.5 * ((after - before) - (1.0 - before * before) * step))
            slopes.append(1.5 - 0.5 * after * after)
        for k in range(3):
            goal = right[k, x]
            value = (
                goal
                - y0 * (goal + tied[k, x])
                - y1 * image[k, x]
                - coupled(acc_diag, porosity, k, x, remainder)
            )
            residual[k, x] = -value if last else value
            mean = mean + value
        if not last:
            diagonal = []
            for k in range(3):
                total = face_x[k, x + 1] + face_x[k, x] + (face_y[0, k, x] + face_y[1, k, x])
                total = total + (face_z[k, x] + pltpu.roll(face_z[k, x], 1, 1))
                diagonal.append(total + mobility[k, x] * density[x * 8 : x * 8 + 8, :])
            invert(slopes, acc_diag, porosity, diagonal, x, inverse)
    if not last:
        broadcast_rows(outgoing, total_of(mean) * (1.0 / CELLS))


def per_device(
    state,
    acc_diag,
    porosity,
    mobility,
    trans_x,
    trans_y,
    trans_z,
    perf_cell,
    perf_owner,
    perf_well,
    perf_index,
    perf_head,
    well_stiff,
    well_drive,
    coarse_inverse,
):
    field = (8, 8, 256)
    triple = (3, *field)
    plane = (8, 256)
    count = perf_cell.shape[1]

    def ring(value, axis, count, shift):
        return lax.ppermute(value, axis, [(i, (i + shift) % count) for i in range(count)])

    def swap_cols(value):
        return lax.all_to_all(value, "col", 0, 0, tiled=True)

    def swap_all(value):
        return lax.all_to_all(value, ("row", "col"), 0, 0, tiled=True)

    def exchange(to_high, to_low, outgoing):
        return (
            ring(to_high, "row", ROWS, 1),
            ring(to_low, "row", ROWS, -1),
            swap_cols(outgoing),
        )

    vmem = pl.BlockSpec(memory_space=pltpu.VMEM)
    hbm = pl.BlockSpec(memory_space=pltpu.HBM)

    def run(body, outs, *args, scratch=(), far=(), far_outs=(), room=ROOM):
        specs = [hbm if n in far else vmem for n in range(len(args))]
        return pl.pallas_call(
            body,
            out_shape=[
                pltpu.HBM(s, t) if n in far_outs else jax.ShapeDtypeStruct(s, t)
                for n, (s, t) in enumerate(outs)
            ],
            in_specs=specs,
            out_specs=[hbm if n in far_outs else vmem for n in range(len(outs))],
            scratch_shapes=list(scratch),
            compiler_params=pltpu.CompilerParams(vmem_limit_bytes=room),
        )(
            *(
                pltpu.with_memory_space_constraint(arg, pltpu.HBM) if n in far else arg
                for n, arg in enumerate(args)
            )
        )

    def buffers(*values):
        return [pltpu.VMEM(value.shape, value.dtype) for value in values]

    line = (1, count)
    packs = run(
        pack_body,
        [((80, 128), F32), ((64, 128), F32), ((80, 128), F32), ((64, 128), F32)],
        state,
        mobility,
        trans_x,
        trans_y,
        scratch=[
            pltpu.VMEM(field, F32),
            pltpu.VMEM(triple, F32),
            pltpu.VMEM(plane, F32),
            pltpu.VMEM(field, F32),
            pltpu.SemaphoreType.DMA((4,)),
        ],
        far=range(4),
        room=FIRST_ROOM,
    )
    up_x, down_x, up_y, down_y = packs
    halos = (
        ring(up_x, "row", ROWS, 1),
        ring(down_x, "row", ROWS, -1),
        ring(up_y, "col", COLS, 1),
        ring(down_y, "col", COLS, -1),
    )
    cell, label, index, density, pulled, sums = run(
        prepare_body,
        [
            (line, jnp.int32),
            (line, jnp.int32),
            (line, F32),
            ((64, 256), F32),
            ((64, 256), F32),
            ((16, 128), F32),
        ],
        state,
        mobility,
        perf_cell,
        perf_owner,
        perf_well,
        perf_index,
        perf_head,
        well_stiff,
        well_drive,
        scratch=[
            pltpu.VMEM(field, F32),
            pltpu.VMEM(triple, F32),
            *buffers(perf_owner, perf_well, perf_head, well_stiff, well_drive),
            pltpu.SemaphoreType.DMA((9,)),
        ],
        far=range(9),
    )
    marks = (cell, label, index)
    (outgoing,) = run(border_body, [((COLS, 16, 128), F32)], *packs, *halos, sums)
    well_tile = (8, 128)
    divisor, per_block, hole, tile = run(
        open_wells_body,
        [(well_tile, F32), ((4, COLS, 128), F32), (well_tile, F32), ((2 * COLS, 128), F32)],
        swap_cols(outgoing),
        coarse_inverse,
    )
    one_hots = [((256, count), BF16), ((64, count), F32), ((128, count), BF16), ((8, count), F32)]
    face_x, face_y, face_z, inner, edges, inverse, right, *stored = run(
        start_body,
        [
            ((3, 9, *plane), F32),
            ((2, *triple), F32),
            (triple, F32),
            (field, F32),
            ((4, *plane), F32),
            ((3, *triple), F32),
            (triple, F32),
            *one_hots,
        ],
        state,
        acc_diag,
        porosity,
        mobility,
        trans_x,
        trans_y,
        trans_z,
        *halos,
        density,
        pulled,
        hole,
        *marks,
        scratch=[
            *buffers(state, acc_diag, porosity, mobility, trans_x, trans_y, trans_z),
            pltpu.VMEM(triple, F32),
            pltpu.SemaphoreType.DMA((7,)),
        ],
        far=range(7),
    )
    faces = (face_x, face_y, face_z)
    current = state
    solve = None
    sends = [((2, *field), F32), (plane, F32), (plane, F32), ((COLS, 24, 128), F32)]
    sends += [(field, F32), (well_tile, F32)]
    send_scratch = [
        pltpu.VMEM((2, *field), F32),
        pltpu.VMEM((COLS, 8, 128), F32),
        pltpu.VMEM((COLS, 16, 128), F32),
        pltpu.SemaphoreType.DMA((3,)),
    ]
    coarse_scratch = [pltpu.VMEM((DEVS, 128), F32)] * 2

    def spread_rows(tile):
        return (tile, *(ring(tile, "row", ROWS, shift) for shift in (1, 2, 3)))

    for outer in range(NEWTON):
        static = (mobility, *faces, inner, edges, inverse, divisor, per_block)
        if outer == 0:
            first_direction, to_high, to_low, outgoing, first_swept, first_level, solve = run(
                opening_direction_body,
                [*sends, ((DEVS, DEVS), F32)],
                *spread_rows(tile),
                right,
                *static,
                *stored,
                index,
                scratch=[*send_scratch, *coarse_scratch],
                far_outs=(0, 3),
            )
        else:
            first_direction, to_high, to_low, outgoing, first_swept, first_level = run(
                direction_body,
                sends,
                solve,
                swap_all(outgoing),
                right,
                *static,
                *marks,
                scratch=[*send_scratch, *coarse_scratch],
                far_outs=(0, 3),
            )
        from_low, from_high, came = exchange(to_high, to_low, outgoing)
        hole, tile = run(
            close_wells_body,
            [(well_tile, F32), ((COLS, 128), F32)],
            came,
            divisor,
            per_block,
            from_low,
            from_high,
        )
        tied, *stored = run(
            first_image_body,
            [(triple, F32), *one_hots],
            hole,
            first_swept,
            from_low,
            from_high,
            came,
            mobility,
            *faces,
            *marks,
        )
        second_direction, to_high, to_low, outgoing, second_swept, second_level = run(
            gathered_direction_body,
            sends,
            solve,
            *spread_rows(tile),
            tied,
            *static,
            *stored,
            index,
            scratch=[*send_scratch, *coarse_scratch],
            far_outs=(0, 3),
        )
        image, outgoing = run(
            second_image_body,
            [(triple, F32), ((DEVS, 128), F32)],
            divisor,
            right,
            tied,
            second_swept,
            *exchange(to_high, to_low, outgoing),
            mobility,
            *faces,
            *marks,
            scratch=[pltpu.VMEM(well_tile, F32)],
        )
        met = swap_all(outgoing)
        last = outer == NEWTON - 1
        outs = [(triple, F32), (triple, F32)]
        extra = ()
        if not last:
            outs += [((3, *triple), F32), ((DEVS, 128), F32)]
            extra = (mobility, *faces, density)
        results = run(
            lambda *refs: update_body(last, *refs),
            outs,
            met,
            current,
            acc_diag,
            porosity,
            right,
            tied,
            image,
            first_swept,
            first_level,
            first_direction,
            second_swept,
            second_level,
            second_direction,
            *extra,
        )
        if last:
            return tuple(results)
        current, right, inverse, outgoing = results


def solution(mesh):
    in_specs = (
        P(None, "row", "col", None),
        P(None, "row", "col", None),
        P("row", "col", None),
        P(None, "row", "col", None),
        P("row", "col", None),
        P("row", "col", None),
        P("row", "col", None),
        P("row", "col"),
        P("row", "col"),
        P("row", "col"),
        P("row", "col"),
        P("row", "col"),
        P("row", "col"),
        P("row", "col"),
        P("row", None),
    )
    out_specs = (P(None, "row", "col", None), P(None, "row", "col", None))
    return jax.shard_map(
        per_device, mesh=mesh, in_specs=in_specs, out_specs=out_specs, check_vma=False
    )
```

```python
import jax
import jax.numpy as jnp
from jax import lax
from jax.experimental import pallas as pl
from jax.experimental.pallas import tpu as pltpu
from jax.sharding import PartitionSpec as P

NEWTON = 2
WELLS_DEV = 16
EXACT = lax.Precision.HIGHEST
COUPLING = ((0.0, 0.3, 0.2), (0.25, 0.0, 0.15), (0.2, 0.1, 0.0))
ROWS = 4
COLS = 32
DEVS = ROWS * COLS
CELLS = 8 * 8 * 256
F32 = jnp.float32
BF16 = jnp.bfloat16
ROOM = 24_000_000
FIRST_ROOM = 66_700_000


def iota(shape, dim):
    return lax.broadcasted_iota(jnp.int32, shape, dim)


def split(value):
    high = value.astype(BF16)
    low = (value - high.astype(F32)).astype(BF16)
    return jnp.concatenate([high, low], 0)


def joined(pair):
    half = pair.shape[0] // 2
    return pair[:half] + pair[half:]


def nn(a, b):
    return lax.dot_general(a, b, (((1,), (0,)), ((), ())), preferred_element_type=F32)


def nt(a, b):
    return lax.dot_general(a, b, (((1,), (1,)), ((), ())), preferred_element_type=F32)


def one_hot(rows, key):
    key = key.astype(F32).astype(BF16)
    line = iota((rows, 128), 0).astype(F32).astype(BF16)
    one = jnp.ones((rows, 128), BF16)
    none = jnp.zeros((rows, 128), BF16)
    return jnp.concatenate(
        [
            jnp.where(line == key[:, start : start + 128], one, none)
            for start in range(0, key.shape[1], 128)
        ],
        1,
    )


def marks_of(cell, label):
    count = cell.shape[1]
    layer = one_hot(256, cell[...] & 255)
    place = jnp.where(iota((64, count), 0) == (cell[...] >> 8), 1.0, 0.0)
    low_mark = one_hot(128, label[...] & 127)
    high_mark = jnp.where(iota((8, count), 0) == (label[...] >> 7), 1.0, 0.0)
    return layer, place, low_mark, high_mark


def keep(marks, targets):
    for value, target in zip(marks, targets):
        target[...] = value


def to_wells(field, index, marks):
    layer, place, low_mark, high_mark = marks
    picked = joined(nn(split(field), layer))
    value = index[...] * jnp.sum(picked * place, 0, keepdims=True)
    return joined(nt(split(high_mark * value), low_mark))


def to_cells(per_well, index, marks):
    layer, place, low_mark, high_mark = marks
    spread = joined(nn(split(per_well), low_mark))
    value = index[...] * jnp.sum(spread * high_mark, 0, keepdims=True)
    return joined(nt(split(place * value), layer))


def write_plane(ref, base, plane):
    ref[base : base + 8, :] = plane[:, :128]
    ref[base + 8 : base + 16, :] = plane[:, 128:]


def read_plane(ref, base):
    return jnp.concatenate([ref[base : base + 8, :], ref[base + 8 : base + 16, :]], 1)


def fetch(pairs, sems):
    copies = [
        pltpu.make_async_copy(source, target, sems.at[n]) for n, (source, target) in enumerate(pairs)
    ]
    for copy in copies:
        copy.start()
    return copies


def pack_body(
    state,
    mobility,
    trans_x,
    trans_y,
    up_x,
    down_x,
    up_y,
    down_y,
    pressure,
    carried,
    along_x,
    along_y,
    sems,
):
    copies = fetch(
        (
            (mobility, carried),
            (state.at[0], pressure),
            (trans_x.at[7], along_x),
            (trans_y, along_y),
        ),
        sems,
    )
    for copy in copies:
        copy.wait()
    for k in range(3):
        write_plane(up_x, 16 * k, carried[k, 7])
        write_plane(down_x, 16 * k, carried[k, 0])
        write_plane(up_y, 16 * k, carried[k, :, 7, :])
        write_plane(down_y, 16 * k, carried[k, :, 0, :])
    write_plane(up_x, 48, pressure[7])
    write_plane(down_x, 48, pressure[0])
    write_plane(up_y, 48, pressure[:, 7, :])
    write_plane(down_y, 48, pressure[:, 0, :])
    write_plane(up_x, 64, along_x[...])
    write_plane(up_y, 64, along_y[:, 7, :])


def prepare_body(
    state,
    mobility,
    cell_in,
    owner_in,
    well_in,
    index_in,
    head_in,
    stiff_in,
    drive_in,
    cell,
    label,
    index,
    density,
    pulled,
    sums,
    pressure,
    carried,
    owner,
    well,
    head,
    stiff,
    drive,
    sems,
):
    copies = fetch(
        (
            (cell_in, cell),
            (owner_in, owner),
            (well_in, well),
            (index_in, index),
            (head_in, head),
            (stiff_in, stiff),
            (drive_in, drive),
            (mobility, carried),
            (state.at[0], pressure),
        ),
        sems,
    )
    for copy in copies:
        copy.wait()
    label[...] = owner[...] * WELLS_DEV + well[...]
    layer, place, low_mark, high_mark = marks_of(cell, label)
    both = jnp.concatenate([place * index[...], place * (index[...] * head[...])], 0)
    spread = joined(nt(split(both), layer))
    density[...] = spread[:64]
    pulled[...] = spread[64:]
    total = (carried[0] + carried[1] + carried[2]).reshape(64, 256)
    pair = split(jnp.concatenate([total, total * pressure[...].reshape(64, 256)], 0))
    picked = joined(nn(pair, layer)) * jnp.concatenate([place, place], 0)
    base = index[...] * jnp.sum(picked[:64], 0, keepdims=True)
    terms = index[...] * jnp.sum(picked[64:], 0, keepdims=True) - base * head[...]
    local = joined(nt(split(jnp.concatenate([high_mark * base, high_mark * terms], 0)), low_mark))
    me = lax.axis_index("col")
    tile = jnp.where(iota((WELLS_DEV, 128), 1) % WELLS_DEV == iota((WELLS_DEV, 128), 0), 1.0, 0.0)
    lines = jnp.concatenate([stiff[...], drive[...], jnp.zeros((6, WELLS_DEV), F32)], 0)
    lines = jnp.dot(lines, tile, precision=EXACT, preferred_element_type=F32)
    mine = (iota((8, 128), 1) // WELLS_DEV == me % 8) & (iota((8, 128), 0) % 4 == me // 8)
    upper = iota((8, 128), 0) < 4
    extra = jnp.where(mine, jnp.where(upper, lines[1:2], lines[0:1]), 0.0)
    corner = (iota((8, 128), 0) == 4) & (iota((8, 128), 1) == 0)
    sums[0:8, :] = jnp.where(corner, jnp.sum(terms, 1, keepdims=True) * -1.0, local[:8])
    sums[8:16, :] = jnp.where(upper, local[8:], 0.0) + extra


def inside_flags():
    row = lax.axis_index("row")
    col = lax.axis_index("col")
    return (
        jnp.where(row > 0, 1.0, 0.0),
        jnp.where(row < ROWS - 1, 1.0, 0.0),
        jnp.where(col > 0, 1.0, 0.0),
        jnp.where(col < COLS - 1, 1.0, 0.0),
    )


def border_body(
    up_x, down_x, up_y, down_y, from_low_x, from_high_x, from_low_y, from_high_y, sums, outgoing
):
    low_x, high_x, low_y, high_y = inside_flags()

    def crossing(lower, upper, inside):
        mobile = read_plane(lower, 0) + read_plane(upper, 0)
        for k in (1, 2):
            mobile = mobile + read_plane(lower, 16 * k) + read_plane(upper, 16 * k)
        rate = read_plane(lower, 64) * 0.5 * mobile
        return rate * (read_plane(lower, 48) - read_plane(upper, 48)) * inside

    net = crossing(up_x, from_high_x, high_x) - crossing(from_low_x, down_x, low_x)
    net = net + crossing(up_y, from_high_y, high_y) - crossing(from_low_y, down_y, low_y)
    corner = (iota((8, 128), 0) == 4) & (iota((8, 128), 1) == 0)
    first = sums[0:8, :] - jnp.where(corner, total_of(net), 0.0)
    second = sums[8:16, :]
    for other in range(COLS):
        outgoing[other, 0:8, :] = first
        outgoing[other, 8:16, :] = second


def neighbours(planes, x, x_low, x_high, y_low, y_high):
    plane = planes[x]
    line = iota((8, 256), 0)
    return (
        planes[x + 1] if x < 7 else x_high,
        planes[x - 1] if x > 0 else x_low,
        jnp.where(line == 7, y_high[x : x + 1], pltpu.roll(plane, 7, 0)),
        jnp.where(line == 0, y_low[x : x + 1], pltpu.roll(plane, 1, 0)),
        pltpu.roll(plane, 255, 1),
    )


def gathered(faces, k, x, plane, around):
    face_x, face_y, face_z = faces
    ahead = face_z[k, x]
    return (
        face_x[k, x + 1] * around[0]
        + face_x[k, x] * around[1]
        + (face_y[0, k, x] * around[2] + face_y[1, k, x] * around[3])
        + (ahead * around[4] + pltpu.roll(ahead * plane, 1, 1))
    )


def coupled(acc_diag, porosity, k, x, terms):
    total = acc_diag[k, x] * terms[k]
    mixed = None
    for j in range(3):
        if COUPLING[k][j] != 0.0:
            part = COUPLING[k][j] * terms[j]
            mixed = part if mixed is None else mixed + part
    return total + porosity[x] * mixed


def invert(slopes, acc_diag, porosity, diagonal, x, inverse):
    m = []
    for k in range(3):
        line = []
        for j in range(3):
            if j == k:
                entry = acc_diag[k, x] * slopes[k]
            else:
                entry = porosity[x] * COUPLING[k][j] * slopes[j]
            if j == 0:
                entry = entry + diagonal[k]
            line.append(entry)
        m.append(line)
    cofactor = [
        [
            m[1][1] * m[2][2] - m[1][2] * m[2][1],
            m[1][2] * m[2][0] - m[1][0] * m[2][2],
            m[1][0] * m[2][1] - m[1][1] * m[2][0],
        ],
        [
            m[0][2] * m[2][1] - m[0][1] * m[2][2],
            m[0][0] * m[2][2] - m[0][2] * m[2][0],
            m[0][1] * m[2][0] - m[0][0] * m[2][1],
        ],
        [
            m[0][1] * m[1][2] - m[0][2] * m[1][1],
            m[0][2] * m[1][0] - m[0][0] * m[1][2],
            m[0][0] * m[1][1] - m[0][1] * m[1][0],
        ],
    ]
    determinant = m[0][0] * cofactor[0][0] + m[0][1] * cofactor[0][1] + m[0][2] * cofactor[0][2]
    reciprocal = 1.0 / determinant
    for k in range(3):
        for j in range(3):
            inverse[k, j, x] = cofactor[j][k] * reciprocal


def total_of(plane):
    return jnp.sum(jnp.sum(plane, 1, keepdims=True), 0, keepdims=True)


def broadcast_rows(outgoing, mean, dots=()):
    lane = iota((1, 128), 1)
    row = jnp.broadcast_to(mean, (1, 128))
    for n, dot in enumerate(dots):
        row = jnp.where(lane == 127 - n, dot, row)
    outgoing[...] = jnp.broadcast_to(row, (DEVS, 128))


def start_body(
    state_in,
    acc_in,
    porosity_in,
    mobility_in,
    trans_x_in,
    trans_y_in,
    trans_z_in,
    from_low_x,
    from_high_x,
    from_low_y,
    from_high_y,
    density,
    pulled,
    hole,
    cell,
    label,
    index,
    face_x,
    face_y,
    face_z,
    inner,
    edges,
    inverse,
    right,
    layer,
    place,
    low_mark,
    high_mark,
    state,
    acc_diag,
    porosity,
    mobility,
    trans_x,
    trans_y,
    trans_z,
    diagonal,
    sems,
):
    copies = fetch(
        (
            (mobility_in, mobility),
            (trans_x_in, trans_x),
            (trans_y_in, trans_y),
            (trans_z_in, trans_z),
            (state_in, state),
            (acc_in, acc_diag),
            (porosity_in, porosity),
        ),
        sems,
    )
    marks = marks_of(cell, label)
    keep(marks, (layer, place, low_mark, high_mark))
    back = to_cells(hole[...], index, marks)
    low_x, high_x, low_y, high_y = inside_flags()
    lane = iota((8, 256), 1)
    line = iota((8, 256), 0)
    t_low_x = read_plane(from_low_x, 64) * low_x
    t_low_y = read_plane(from_low_y, 64) * low_y
    for copy in copies[:4]:
        copy.wait()
    for k in range(3):
        m_low_x = read_plane(from_low_x, 16 * k)
        m_high_x = read_plane(from_high_x, 16 * k)
        m_low_y = read_plane(from_low_y, 16 * k)
        m_high_y = read_plane(from_high_y, 16 * k)
        previous = t_low_x * 0.5 * (m_low_x + mobility[k, 0])
        face_x[k, 0] = previous
        planes = [mobility[k, x] for x in range(8)]
        for x in range(8):
            here = planes[x]
            around = neighbours(planes, x, m_low_x, m_high_x, m_low_y, m_high_y)
            tx = trans_x[x] if x < 7 else trans_x[x] * high_x
            ahead = tx * 0.5 * (here + around[0])
            face_x[k, x + 1] = ahead
            total = ahead + previous
            previous = ahead
            ty = jnp.where(line == 7, trans_y[x] * high_y, trans_y[x])
            ahead_y = ty * 0.5 * (here + around[2])
            entering = t_low_y[x : x + 1] * 0.5 * (m_low_y[x : x + 1] + here[0:1])
            behind_y = jnp.where(line == 0, entering, pltpu.roll(ahead_y, 1, 0))
            face_y[0, k, x] = ahead_y
            face_y[1, k, x] = behind_y
            total = total + (ahead_y + behind_y)
            ahead_z = jnp.where(lane < 255, trans_z[x] * 0.5 * (here + around[4]), 0.0)
            face_z[k, x] = ahead_z
            total = total + (ahead_z + pltpu.roll(ahead_z, 1, 1))
            diagonal[k, x] = total + here * density[x * 8 : x * 8 + 8, :]

    def summed(face, *place):
        return face[0, *place] + face[1, *place] + face[2, *place]

    edges[0] = summed(face_x, 8)
    edges[1] = summed(face_x, 0)
    edges[2] = face_y[0, 0, :, 7, :] + face_y[0, 1, :, 7, :] + face_y[0, 2, :, 7, :]
    edges[3] = face_y[1, 0, :, 0, :] + face_y[1, 1, :, 0, :] + face_y[1, 2, :, 0, :]
    halo = (
        read_plane(from_low_x, 48),
        read_plane(from_high_x, 48),
        read_plane(from_low_y, 48),
        read_plane(from_high_y, 48),
    )
    for copy in copies[4:]:
        copy.wait()
    planes = [state[0, x] for x in range(8)]
    for x in range(8):
        up_z = summed(face_z, x)
        kept = up_z + pltpu.roll(up_z, 1, 1)
        kept = kept + jnp.where(line < 7, summed(face_y.at[0], x), 0.0)
        kept = kept + jnp.where(line > 0, summed(face_y.at[1], x), 0.0)
        if x < 7:
            kept = kept + summed(face_x, x + 1)
        if x > 0:
            kept = kept + summed(face_x, x)
        inner[x] = kept
        around = neighbours(planes, x, *halo)
        source = pulled[x * 8 : x * 8 + 8, :] + back[x * 8 : x * 8 + 8]
        for k in range(3):
            value = (
                gathered((face_x, face_y, face_z), k, x, planes[x], around)
                + mobility[k, x] * source
                - diagonal[k, x] * planes[x]
            )
            right[k, x] = value
        slopes = []
        for k in range(3):
            bent = jnp.tanh(state[k, x])
            slopes.append(1.5 - 0.5 * bent * bent)
        invert(slopes, acc_diag, porosity, [diagonal[k, x] for k in range(3)], x, inverse)


def shares(per_block, hole):
    share = per_block[0] * hole[0:1]
    for a in range(1, 4):
        share = share + per_block[a] * hole[a : a + 1]
    return jnp.sum(share, 1, keepdims=True)


def open_wells_body(arrived, coarse, divisor, per_block, hole, tile):
    totals = jnp.zeros((8, 128), F32)
    others = jnp.zeros((8, 128), F32)
    for other in range(COLS):
        totals = totals + arrived[other, 0:8, :]
        others = others + arrived[other, 8:16, :]
    blocks = [arrived[:, a, :] for a in range(4)]
    for a in range(4):
        per_block[a] = blocks[a]
    upper = iota((8, 128), 0) < 4
    div = jnp.where(upper, totals + pltpu.roll(others, 4, 0), 1.0)
    divisor[...] = div
    found = jnp.where(upper, others, 0.0) / div
    hole[...] = found
    share = shares(blocks, found) + arrived[:, 4, 0:1]
    tile[0:32, :] = jnp.where(iota((COLS, 128), 1) == 0, share * -1.0, 0.0)
    tile[32:64, :] = coarse[...]


def find_direction(stored, coarse_x, *refs):
    (
        vector,
        mobility,
        face_x,
        face_y,
        face_z,
        inner,
        edges,
        inverse,
        divisor,
        per_block,
        *refs,
    ) = refs
    if stored:
        layer, place, low_mark, high_mark, index, *refs = refs
        marks = (layer[...], place[...], low_mark[...], high_mark[...])
    else:
        cell, label, index, *refs = refs
        marks = marks_of(cell, label)
    (
        direction_out,
        to_high,
        to_low,
        outgoing,
        swept,
        level,
        direction,
        for_wells,
        for_sides,
        sems,
    ) = refs
    row = lax.axis_index("row")
    col = lax.axis_index("col")
    faces = (face_x, face_y, face_z)

    def wide(at_row, at_col):
        place = at_col * ROWS + at_row
        value = coarse_x[pl.ds(place, 1), :]
        return jnp.broadcast_to(jnp.concatenate([value, value], 1), (8, 256))

    own = wide(row, col)
    x_high = wide(jnp.minimum(row + 1, ROWS - 1), col)
    x_low = wide(jnp.maximum(row - 1, 0), col)
    y_high = wide(row, jnp.minimum(col + 1, COLS - 1))
    y_low = wide(row, jnp.maximum(col - 1, 0))
    level[...] = own[:, :128]
    weights = coarse_x[pl.ds(row, COLS, stride=ROWS), :]
    sums = [jnp.sum(weights * per_block[a], 0, keepdims=True) for a in range(4)]
    sums = jnp.concatenate([*sums, jnp.zeros((4, 128), F32)], 0)
    back = to_cells(sums / divisor[...], index, marks)
    line = iota((8, 256), 0)
    up_y = jnp.where(line == 7, y_high, own)
    down_y = jnp.where(line == 0, y_low, own)
    weighted = []
    inside = jnp.zeros((8, 256), F32)
    for x in range(8):
        around = (own if x < 7 else x_high, own if x > 0 else x_low, up_y, down_y, own)
        terms = [
            vector[k, x] + gathered(faces, k, x, own, around) + mobility[k, x] * back[x * 8 : x * 8 + 8]
            for k in range(3)
        ]
        for k in range(3):
            value = (
                inverse[k, 0, x] * terms[0]
                + inverse[k, 1, x] * terms[1]
                + inverse[k, 2, x] * terms[2]
            )
            if k == 0:
                kept = value - own
                swept[x] = kept
            else:
                direction[k - 1, x] = value
        inside = inside + kept * inner[x]
        weighted.append(kept * (mobility[0, x] + mobility[1, x] + mobility[2, x]))
    to_high[...] = swept[7]
    to_low[...] = swept[0]
    last = swept[:, 7, :]
    first = swept[:, 0, :]
    for other in range(COLS):
        send = jnp.where(other < col, first, last)
        for_sides[other, 0:8, :] = send[:, :128]
        for_sides[other, 8:16, :] = send[:, 128:]
    side_copy = pltpu.make_async_copy(for_sides, outgoing.at[:, 8:24, :], sems.at[0])
    side_copy.start()
    direction_copy = pltpu.make_async_copy(direction, direction_out, sems.at[2])
    direction_copy.start()
    local = to_wells(jnp.concatenate(weighted, 0), index, marks)
    sides = (swept[7] * edges[0], swept[0] * edges[1], last * edges[2], first * edges[3])
    lane = iota((8, 128), 1)
    for n, term in enumerate((inside, *sides)):
        local = jnp.where((iota((8, 128), 0) == 4) & (lane == n), total_of(term), local)
    for other in range(COLS):
        for_wells[other] = local
    well_copy = pltpu.make_async_copy(for_wells, outgoing.at[:, 0:8, :], sems.at[1])
    well_copy.start()
    direction_copy.wait()
    side_copy.wait()
    well_copy.wait()


def coarse_solve(solve, means, ordered, coarse_x):
    for r in range(ROWS):
        ordered[pl.ds(r, COLS, stride=ROWS), :] = means[r * COLS : (r + 1) * COLS, :]
    coarse_x[...] = jnp.dot(solve[...], ordered[...], precision=EXACT, preferred_element_type=F32)


def direction_body(solve, received, *rest):
    *rest, coarse_x = rest
    coarse_x[...] = jnp.dot(
        solve[...], received[...], precision=EXACT, preferred_element_type=F32
    )
    find_direction(False, coarse_x, *rest)


def place_rows(sources, target, base):
    for shift, source in enumerate(sources):
        start = pl.multiple_of(((lax.axis_index("row") - shift + ROWS) % ROWS) * COLS, COLS)
        target[pl.ds(start, COLS), :] = source[base : base + COLS, :]


def from_rows(solve, sources, rest, opening):
    *rest, ordered, coarse_x = rest
    place_rows(sources, coarse_x, 0)
    every = coarse_x[...]
    means = every[:, 0:1]
    if not opening:
        means = means + pltpu.roll(every, COLS, 0)[:, 1:2]
        means = means + pltpu.roll(every, DEVS - COLS, 0)[:, 2:3]
    means = jnp.broadcast_to(means * (-1.0 / CELLS), (DEVS, 128))
    coarse_solve(solve, means, ordered, coarse_x)
    find_direction(True, coarse_x, *rest)


def gathered_direction_body(solve, own, low, far, high, *rest):
    from_rows(solve, (own, low, far, high), rest, False)


def opening_direction_body(own, low, far, high, *rest):
    *rest, solve, direction, for_wells, for_sides, sems, ordered, coarse_x = rest
    place_rows((own, low, far, high), solve, COLS)
    rest = (*rest, direction, for_wells, for_sides, sems, ordered, coarse_x)
    from_rows(solve, (own, low, far, high), rest, True)


def sum_wells_body(came, divisor, per_block, hole, tile):
    sums = jnp.zeros((8, 128), F32)
    for other in range(COLS):
        sums = sums + came[other, 0:8, :]
    found = jnp.where(iota((8, 128), 0) < 4, sums, 0.0) / divisor[...]
    hole[...] = found
    if tile is not None:
        pieces = came[:, 4, :]
        share = shares(per_block, found) + pieces[:, 0:1]
        share = share + pltpu.roll(pieces, 1, 0)[:, 3:4] + pltpu.roll(pieces, COLS - 1, 0)[:, 4:5]
        tile[...] = jnp.where(iota((COLS, 128), 1) == 0, share, pieces)


def close_wells_body(came, divisor, per_block, from_low, from_high, hole, tile):
    sum_wells_body(came, divisor, per_block, hole, tile)


def coupling_planes(
    hole,
    swept,
    from_low,
    from_high,
    came,
    mobility,
    face_x,
    face_y,
    face_z,
    cell,
    label,
    index,
    kept=(),
):
    col = lax.axis_index("col")
    faces = (face_x, face_y, face_z)
    marks = marks_of(cell, label)
    keep(marks, kept)
    back = to_cells(hole[...], index, marks)
    below = jnp.maximum(col - 1, 0)
    above = jnp.minimum(col + 1, COLS - 1)
    y_low = jnp.concatenate([came[below, 8:16, :], came[below, 16:24, :]], 1)
    y_high = jnp.concatenate([came[above, 8:16, :], came[above, 16:24, :]], 1)
    planes = [swept[x] for x in range(8)]
    for x in range(8):
        around = neighbours(planes, x, from_low[...], from_high[...], y_low, y_high)
        for k in range(3):
            value = gathered(faces, k, x, planes[x], around)
            yield k, x, value + mobility[k, x] * back[x * 8 : x * 8 + 8]


def first_image_body(*rest):
    *rest, tied, layer, place, low_mark, high_mark = rest
    for k, x, value in coupling_planes(*rest, kept=(layer, place, low_mark, high_mark)):
        tied[k, x] = -value


def second_image_body(divisor, right, tied, *rest):
    *rest, image, outgoing, hole = rest
    sum_wells_body(rest[3], divisor, None, hole, None)
    totals = [jnp.zeros((8, 256), F32) for _ in range(5)]
    for k, x, value in coupling_planes(hole, *rest):
        value = tied[k, x] - value
        image[k, x] = value
        goal = right[k, x]
        one = goal + tied[k, x]
        for n, term in enumerate((one * one, one * value, value * value, one * goal, value * goal)):
            totals[n] = totals[n] + term
    broadcast_rows(outgoing, jnp.zeros((1, 1), F32), [total_of(t) for t in totals])


def update_body(last, *refs):
    (
        met,
        current,
        acc_diag,
        porosity,
        right,
        tied,
        image,
        first_swept,
        first_level,
        first_direction,
        second_swept,
        second_level,
        second_direction,
        *outs,
    ) = refs
    sums = jnp.sum(met[...], 0, keepdims=True)
    g00, g01, g11, t0, t1 = [sums[:, 127 - n : 128 - n] for n in range(5)]
    l00 = jnp.sqrt(g00)
    l10 = g01 / l00
    l11 = jnp.sqrt(g11 - l10 * l10)
    f0 = t0 / l00
    f1 = (t1 - l10 * f0) / l11
    y1 = f1 / l11
    y0 = (f0 - l10 * y1) / l00
    shift = y0 * first_level[0:1, 0:1] + y1 * second_level[0:1, 0:1]
    if last:
        fresh, residual = outs
    else:
        mobility, face_x, face_y, face_z, density, fresh, residual, inverse, outgoing = outs
    mean = jnp.zeros((8, 256), F32)
    for x in range(8):
        remainder = []
        slopes = []
        for k in range(3):
            old = current[k, x]
            if k == 0:
                step = y0 * first_swept[x] + y1 * second_swept[x] + shift
            else:
                step = y0 * first_direction[k - 1, x] + y1 * second_direction[k - 1, x]
            new = old + step
            fresh[k, x] = new
            before = jnp.tanh(old)
            after = jnp.tanh(new)
            remainder.append(0.5 * ((after - before) - (1.0 - before * before) * step))
            slopes.append(1.5 - 0.5 * after * after)
        for k in range(3):
            goal = right[k, x]
            value = (
                goal
                - y0 * (goal + tied[k, x])
                - y1 * image[k, x]
                - coupled(acc_diag, porosity, k, x, remainder)
            )
            residual[k, x] = -value if last else value
            mean = mean + value
        if not last:
            diagonal = []
            for k in range(3):
                total = face_x[k, x + 1] + face_x[k, x] + (face_y[0, k, x] + face_y[1, k, x])
                total = total + (face_z[k, x] + pltpu.roll(face_z[k, x], 1, 1))
                diagonal.append(total + mobility[k, x] * density[x * 8 : x * 8 + 8, :])
            invert(slopes, acc_diag, porosity, diagonal, x, inverse)
    if not last:
        broadcast_rows(outgoing, total_of(mean) * (1.0 / CELLS))


def per_device(
    state,
    acc_diag,
    porosity,
    mobility,
    trans_x,
    trans_y,
    trans_z,
    perf_cell,
    perf_owner,
    perf_well,
    perf_index,
    perf_head,
    well_stiff,
    well_drive,
    coarse_inverse,
):
    field = (8, 8, 256)
    triple = (3, *field)
    plane = (8, 256)
    count = perf_cell.shape[1]

    def ring(value, axis, count, shift):
        return lax.ppermute(value, axis, [(i, (i + shift) % count) for i in range(count)])

    def swap_cols(value):
        return lax.all_to_all(value, "col", 0, 0, tiled=True)

    def swap_all(value):
        return lax.all_to_all(value, ("col", "row"), 0, 0, tiled=True)

    def exchange(to_high, to_low, outgoing):
        return (
            ring(to_high, "row", ROWS, 1),
            ring(to_low, "row", ROWS, -1),
            swap_cols(outgoing),
        )

    vmem = pl.BlockSpec(memory_space=pltpu.VMEM)
    hbm = pl.BlockSpec(memory_space=pltpu.HBM)

    def run(body, outs, *args, scratch=(), far=(), far_outs=(), room=ROOM):
        specs = [hbm if n in far else vmem for n in range(len(args))]
        return pl.pallas_call(
            body,
            out_shape=[
                pltpu.HBM(s, t) if n in far_outs else jax.ShapeDtypeStruct(s, t)
                for n, (s, t) in enumerate(outs)
            ],
            in_specs=specs,
            out_specs=[hbm if n in far_outs else vmem for n in range(len(outs))],
            scratch_shapes=list(scratch),
            compiler_params=pltpu.CompilerParams(vmem_limit_bytes=room),
        )(
            *(
                pltpu.with_memory_space_constraint(arg, pltpu.HBM) if n in far else arg
                for n, arg in enumerate(args)
            )
        )

    def buffers(*values):
        return [pltpu.VMEM(value.shape, value.dtype) for value in values]

    line = (1, count)
    packs = run(
        pack_body,
        [((80, 128), F32), ((64, 128), F32), ((80, 128), F32), ((64, 128), F32)],
        state,
        mobility,
        trans_x,
        trans_y,
        scratch=[
            pltpu.VMEM(field, F32),
            pltpu.VMEM(triple, F32),
            pltpu.VMEM(plane, F32),
            pltpu.VMEM(field, F32),
            pltpu.SemaphoreType.DMA((4,)),
        ],
        far=range(4),
        room=FIRST_ROOM,
    )
    up_x, down_x, up_y, down_y = packs
    halos = (
        ring(up_x, "row", ROWS, 1),
        ring(down_x, "row", ROWS, -1),
        ring(up_y, "col", COLS, 1),
        ring(down_y, "col", COLS, -1),
    )
    cell, label, index, density, pulled, sums = run(
        prepare_body,
        [
            (line, jnp.int32),
            (line, jnp.int32),
            (line, F32),
            ((64, 256), F32),
            ((64, 256), F32),
            ((16, 128), F32),
        ],
        state,
        mobility,
        perf_cell,
        perf_owner,
        perf_well,
        perf_index,
        perf_head,
        well_stiff,
        well_drive,
        scratch=[
            pltpu.VMEM(field, F32),
            pltpu.VMEM(triple, F32),
            *buffers(perf_owner, perf_well, perf_head, well_stiff, well_drive),
            pltpu.SemaphoreType.DMA((9,)),
        ],
        far=range(9),
    )
    marks = (cell, label, index)
    (outgoing,) = run(border_body, [((COLS, 16, 128), F32)], *packs, *halos, sums)
    well_tile = (8, 128)
    divisor, per_block, hole, tile = run(
        open_wells_body,
        [(well_tile, F32), ((4, COLS, 128), F32), (well_tile, F32), ((2 * COLS, 128), F32)],
        swap_cols(outgoing),
        coarse_inverse,
    )
    one_hots = [((256, count), BF16), ((64, count), F32), ((128, count), BF16), ((8, count), F32)]
    face_x, face_y, face_z, inner, edges, inverse, right, *stored = run(
        start_body,
        [
            ((3, 9, *plane), F32),
            ((2, *triple), F32),
            (triple, F32),
            (field, F32),
            ((4, *plane), F32),
            ((3, *triple), F32),
            (triple, F32),
            *one_hots,
        ],
        state,
        acc_diag,
        porosity,
        mobility,
        trans_x,
        trans_y,
        trans_z,
        *halos,
        density,
        pulled,
        hole,
        *marks,
        scratch=[
            *buffers(state, acc_diag, porosity, mobility, trans_x, trans_y, trans_z),
            pltpu.VMEM(triple, F32),
            pltpu.SemaphoreType.DMA((7,)),
        ],
        far=range(7),
    )
    faces = (face_x, face_y, face_z)
    current = state
    solve = None
    sends = [((2, *field), F32), (plane, F32), (plane, F32), ((COLS, 24, 128), F32)]
    sends += [(field, F32), (well_tile, F32)]
    send_scratch = [
        pltpu.VMEM((2, *field), F32),
        pltpu.VMEM((COLS, 8, 128), F32),
        pltpu.VMEM((COLS, 16, 128), F32),
        pltpu.SemaphoreType.DMA((3,)),
    ]
    coarse_scratch = [pltpu.VMEM((DEVS, 128), F32)] * 2

    def spread_rows(tile):
        return (tile, *(ring(tile, "row", ROWS, shift) for shift in (1, 2, 3)))

    for outer in range(NEWTON):
        static = (mobility, *faces, inner, edges, inverse, divisor, per_block)
        if outer == 0:
            first_direction, to_high, to_low, outgoing, first_swept, first_level, solve = run(
                opening_direction_body,
                [*sends, ((DEVS, DEVS), F32)],
                *spread_rows(tile),
                right,
                *static,
                *stored,
                index,
                scratch=[*send_scratch, *coarse_scratch],
                far_outs=(0, 3),
            )
        else:
            first_direction, to_high, to_low, outgoing, first_swept, first_level = run(
                direction_body,
                sends,
                solve,
                swap_all(outgoing),
                right,
                *static,
                *marks,
                scratch=[*send_scratch, coarse_scratch[0]],
                far_outs=(0, 3),
            )
        from_low, from_high, came = exchange(to_high, to_low, outgoing)
        hole, tile = run(
            close_wells_body,
            [(well_tile, F32), ((COLS, 128), F32)],
            came,
            divisor,
            per_block,
            from_low,
            from_high,
        )
        tied, *stored = run(
            first_image_body,
            [(triple, F32), *one_hots],
            hole,
            first_swept,
            from_low,
            from_high,
            came,
            mobility,
            *faces,
            *marks,
        )
        second_direction, to_high, to_low, outgoing, second_swept, second_level = run(
            gathered_direction_body,
            sends,
            solve,
            *spread_rows(tile),
            tied,
            *static,
            *stored,
            index,
            scratch=[*send_scratch, *coarse_scratch],
            far_outs=(0, 3),
        )
        image, outgoing = run(
            second_image_body,
            [(triple, F32), ((DEVS, 128), F32)],
            divisor,
            right,
            tied,
            second_swept,
            *exchange(to_high, to_low, outgoing),
            mobility,
            *faces,
            *marks,
            scratch=[pltpu.VMEM(well_tile, F32)],
        )
        met = swap_all(outgoing)
        last = outer == NEWTON - 1
        outs = [(triple, F32), (triple, F32)]
        extra = ()
        if not last:
            outs += [((3, *triple), F32), ((DEVS, 128), F32)]
            extra = (mobility, *faces, density)
        results = run(
            lambda *refs: update_body(last, *refs),
            outs,
            met,
            current,
            acc_diag,
            porosity,
            right,
            tied,
            image,
            first_swept,
            first_level,
            first_direction,
            second_swept,
            second_level,
            second_direction,
            *extra,
        )
        if last:
            return tuple(results)
        current, right, inverse, outgoing = results


def solution(mesh):
    in_specs = (
        P(None, "row", "col", None),
        P(None, "row", "col", None),
        P("row", "col", None),
        P(None, "row", "col", None),
        P("row", "col", None),
        P("row", "col", None),
        P("row", "col", None),
        P("row", "col"),
        P("row", "col"),
        P("row", "col"),
        P("row", "col"),
        P("row", "col"),
        P("row", "col"),
        P("row", "col"),
        P("row", None),
    )
    out_specs = (P(None, "row", "col", None), P(None, "row", "col", None))
    return jax.shard_map(
        per_device, mesh=mesh, in_specs=in_specs, out_specs=out_specs, check_vma=False
    )
```

```python
import jax
import jax.numpy as jnp
from jax import lax
from jax.experimental import pallas as pl
from jax.experimental.pallas import tpu as pltpu
from jax.sharding import PartitionSpec as P

NEWTON = 2
WELLS_DEV = 16
EXACT = lax.Precision.HIGHEST
COUPLING = ((0.0, 0.3, 0.2), (0.25, 0.0, 0.15), (0.2, 0.1, 0.0))
ROWS = 4
COLS = 32
DEVS = ROWS * COLS
CELLS = 8 * 8 * 256
F32 = jnp.float32
BF16 = jnp.bfloat16
ROOM = 24_000_000
FIRST_ROOM = 66_700_000


def iota(shape, dim):
    return lax.broadcasted_iota(jnp.int32, shape, dim)


def split(value):
    high = value.astype(BF16)
    low = (value - high.astype(F32)).astype(BF16)
    return jnp.concatenate([high, low], 0)


def joined(pair):
    half = pair.shape[0] // 2
    return pair[:half] + pair[half:]


def nn(a, b):
    return lax.dot_general(a, b, (((1,), (0,)), ((), ())), preferred_element_type=F32)


def nt(a, b):
    return lax.dot_general(a, b, (((1,), (1,)), ((), ())), preferred_element_type=F32)


def one_hot(rows, key):
    key = key.astype(F32).astype(BF16)
    line = iota((rows, 128), 0).astype(F32).astype(BF16)
    one = jnp.ones((rows, 128), BF16)
    none = jnp.zeros((rows, 128), BF16)
    return jnp.concatenate(
        [
            jnp.where(line == key[:, start : start + 128], one, none)
            for start in range(0, key.shape[1], 128)
        ],
        1,
    )


def marks_of(cell, label):
    count = cell.shape[1]
    layer = one_hot(256, cell[...] & 255)
    place = jnp.where(iota((64, count), 0) == (cell[...] >> 8), 1.0, 0.0)
    low_mark = one_hot(128, label[...] & 127)
    high_mark = jnp.where(iota((8, count), 0) == (label[...] >> 7), 1.0, 0.0)
    return layer, place, low_mark, high_mark


def keep(marks, targets):
    for value, target in zip(marks, targets):
        target[...] = value


def to_wells(field, index, marks):
    layer, place, low_mark, high_mark = marks
    picked = joined(nn(split(field), layer))
    value = index[...] * jnp.sum(picked * place, 0, keepdims=True)
    return joined(nt(split(high_mark * value), low_mark))


def to_cells(per_well, index, marks):
    layer, place, low_mark, high_mark = marks
    spread = joined(nn(split(per_well), low_mark))
    value = index[...] * jnp.sum(spread * high_mark, 0, keepdims=True)
    return joined(nt(split(place * value), layer))


def write_plane(ref, base, plane):
    ref[base : base + 8, :] = plane[:, :128]
    ref[base + 8 : base + 16, :] = plane[:, 128:]


def read_plane(ref, base):
    return jnp.concatenate([ref[base : base + 8, :], ref[base + 8 : base + 16, :]], 1)


def fetch(pairs, sems):
    copies = [
        pltpu.make_async_copy(source, target, sems.at[n]) for n, (source, target) in enumerate(pairs)
    ]
    for copy in copies:
        copy.start()
    return copies


def pack_body(
    state,
    mobility,
    trans_x,
    trans_y,
    up_x,
    down_x,
    up_y,
    down_y,
    pressure,
    carried,
    along_x,
    along_y,
    sems,
):
    copies = fetch(
        (
            (mobility, carried),
            (state.at[0], pressure),
            (trans_x.at[7], along_x),
            (trans_y, along_y),
        ),
        sems,
    )
    for copy in copies:
        copy.wait()
    for k in range(3):
        write_plane(up_x, 16 * k, carried[k, 7])
        write_plane(down_x, 16 * k, carried[k, 0])
        write_plane(up_y, 16 * k, carried[k, :, 7, :])
        write_plane(down_y, 16 * k, carried[k, :, 0, :])
    write_plane(up_x, 48, pressure[7])
    write_plane(down_x, 48, pressure[0])
    write_plane(up_y, 48, pressure[:, 7, :])
    write_plane(down_y, 48, pressure[:, 0, :])
    write_plane(up_x, 64, along_x[...])
    write_plane(up_y, 64, along_y[:, 7, :])


def prepare_body(
    state,
    mobility,
    cell_in,
    owner_in,
    well_in,
    index_in,
    head_in,
    stiff_in,
    drive_in,
    cell,
    label,
    index,
    density,
    pulled,
    sums,
    pressure,
    carried,
    owner,
    well,
    head,
    stiff,
    drive,
    sems,
):
    copies = fetch(
        (
            (cell_in, cell),
            (owner_in, owner),
            (well_in, well),
            (index_in, index),
            (head_in, head),
            (stiff_in, stiff),
            (drive_in, drive),
            (mobility, carried),
            (state.at[0], pressure),
        ),
        sems,
    )
    for copy in copies:
        copy.wait()
    label[...] = owner[...] * WELLS_DEV + well[...]
    layer, place, low_mark, high_mark = marks_of(cell, label)
    both = jnp.concatenate([place * index[...], place * (index[...] * head[...])], 0)
    spread = joined(nt(split(both), layer))
    density[...] = spread[:64]
    pulled[...] = spread[64:]
    total = (carried[0] + carried[1] + carried[2]).reshape(64, 256)
    pair = split(jnp.concatenate([total, total * pressure[...].reshape(64, 256)], 0))
    picked = joined(nn(pair, layer)) * jnp.concatenate([place, place], 0)
    base = index[...] * jnp.sum(picked[:64], 0, keepdims=True)
    terms = index[...] * jnp.sum(picked[64:], 0, keepdims=True) - base * head[...]
    local = joined(nt(split(jnp.concatenate([high_mark * base, high_mark * terms], 0)), low_mark))
    me = lax.axis_index("col")
    tile = jnp.where(iota((WELLS_DEV, 128), 1) % WELLS_DEV == iota((WELLS_DEV, 128), 0), 1.0, 0.0)
    lines = jnp.concatenate([stiff[...], drive[...], jnp.zeros((6, WELLS_DEV), F32)], 0)
    lines = jnp.dot(lines, tile, precision=EXACT, preferred_element_type=F32)
    mine = (iota((8, 128), 1) // WELLS_DEV == me % 8) & (iota((8, 128), 0) % 4 == me // 8)
    upper = iota((8, 128), 0) < 4
    extra = jnp.where(mine, jnp.where(upper, lines[1:2], lines[0:1]), 0.0)
    corner = (iota((8, 128), 0) == 4) & (iota((8, 128), 1) == 0)
    sums[0:8, :] = jnp.where(corner, jnp.sum(terms, 1, keepdims=True) * -1.0, local[:8])
    sums[8:16, :] = jnp.where(upper, local[8:], 0.0) + extra


def inside_flags():
    row = lax.axis_index("row")
    col = lax.axis_index("col")
    return (
        jnp.where(row > 0, 1.0, 0.0),
        jnp.where(row < ROWS - 1, 1.0, 0.0),
        jnp.where(col > 0, 1.0, 0.0),
        jnp.where(col < COLS - 1, 1.0, 0.0),
    )


def border_body(
    up_x, down_x, up_y, down_y, from_low_x, from_high_x, from_low_y, from_high_y, sums, outgoing
):
    low_x, high_x, low_y, high_y = inside_flags()

    def crossing(lower, upper, inside):
        mobile = read_plane(lower, 0) + read_plane(upper, 0)
        for k in (1, 2):
            mobile = mobile + read_plane(lower, 16 * k) + read_plane(upper, 16 * k)
        rate = read_plane(lower, 64) * 0.5 * mobile
        return rate * (read_plane(lower, 48) - read_plane(upper, 48)) * inside

    net = crossing(up_x, from_high_x, high_x) - crossing(from_low_x, down_x, low_x)
    net = net + crossing(up_y, from_high_y, high_y) - crossing(from_low_y, down_y, low_y)
    corner = (iota((8, 128), 0) == 4) & (iota((8, 128), 1) == 0)
    first = sums[0:8, :] - jnp.where(corner, total_of(net), 0.0)
    second = sums[8:16, :]
    for other in range(COLS):
        outgoing[other, 0:8, :] = first
        outgoing[other, 8:16, :] = second


def neighbours(planes, x, x_low, x_high, y_low, y_high):
    plane = planes[x]
    line = iota((8, 256), 0)
    return (
        planes[x + 1] if x < 7 else x_high,
        planes[x - 1] if x > 0 else x_low,
        jnp.where(line == 7, y_high[x : x + 1], pltpu.roll(plane, 7, 0)),
        jnp.where(line == 0, y_low[x : x + 1], pltpu.roll(plane, 1, 0)),
        pltpu.roll(plane, 255, 1),
    )


def gathered(faces, k, x, plane, around):
    face_x, face_y, face_z = faces
    ahead = face_z[k, x]
    return (
        face_x[k, x + 1] * around[0]
        + face_x[k, x] * around[1]
        + (face_y[0, k, x] * around[2] + face_y[1, k, x] * around[3])
        + (ahead * around[4] + pltpu.roll(ahead * plane, 1, 1))
    )


def coupled(acc_diag, porosity, k, x, terms):
    total = acc_diag[k, x] * terms[k]
    mixed = None
    for j in range(3):
        if COUPLING[k][j] != 0.0:
            part = COUPLING[k][j] * terms[j]
            mixed = part if mixed is None else mixed + part
    return total + porosity[x] * mixed


def invert(slopes, acc_diag, porosity, diagonal, x, inverse):
    m = []
    for k in range(3):
        line = []
        for j in range(3):
            if j == k:
                entry = acc_diag[k, x] * slopes[k]
            else:
                entry = porosity[x] * COUPLING[k][j] * slopes[j]
            if j == 0:
                entry = entry + diagonal[k]
            line.append(entry)
        m.append(line)
    cofactor = [
        [
            m[1][1] * m[2][2] - m[1][2] * m[2][1],
            m[1][2] * m[2][0] - m[1][0] * m[2][2],
            m[1][0] * m[2][1] - m[1][1] * m[2][0],
        ],
        [
            m[0][2] * m[2][1] - m[0][1] * m[2][2],
            m[0][0] * m[2][2] - m[0][2] * m[2][0],
            m[0][1] * m[2][0] - m[0][0] * m[2][1],
        ],
        [
            m[0][1] * m[1][2] - m[0][2] * m[1][1],
            m[0][2] * m[1][0] - m[0][0] * m[1][2],
            m[0][0] * m[1][1] - m[0][1] * m[1][0],
        ],
    ]
    determinant = m[0][0] * cofactor[0][0] + m[0][1] * cofactor[0][1] + m[0][2] * cofactor[0][2]
    reciprocal = 1.0 / determinant
    for k in range(3):
        for j in range(3):
            inverse[k, j, x] = cofactor[j][k] * reciprocal


def total_of(plane):
    return jnp.sum(jnp.sum(plane, 1, keepdims=True), 0, keepdims=True)


def broadcast_rows(outgoing, mean, dots=()):
    lane = iota((1, 128), 1)
    row = jnp.broadcast_to(mean, (1, 128))
    for n, dot in enumerate(dots):
        row = jnp.where(lane == 127 - n, dot, row)
    outgoing[...] = jnp.broadcast_to(row, (DEVS, 128))


def start_body(
    state_in,
    acc_in,
    porosity_in,
    mobility_in,
    trans_x_in,
    trans_y_in,
    trans_z_in,
    from_low_x,
    from_high_x,
    from_low_y,
    from_high_y,
    density,
    pulled,
    hole,
    cell,
    label,
    index,
    face_x,
    face_y,
    face_z,
    inner,
    edges,
    inverse,
    right,
    layer,
    place,
    low_mark,
    high_mark,
    state,
    acc_diag,
    porosity,
    mobility,
    trans_x,
    trans_y,
    trans_z,
    diagonal,
    sems,
):
    copies = fetch(
        (
            (mobility_in, mobility),
            (trans_x_in, trans_x),
            (trans_y_in, trans_y),
            (trans_z_in, trans_z),
            (state_in, state),
            (acc_in, acc_diag),
            (porosity_in, porosity),
        ),
        sems,
    )
    marks = marks_of(cell, label)
    keep(marks, (layer, place, low_mark, high_mark))
    back = to_cells(hole[...], index, marks)
    low_x, high_x, low_y, high_y = inside_flags()
    lane = iota((8, 256), 1)
    line = iota((8, 256), 0)
    t_low_x = read_plane(from_low_x, 64) * low_x
    t_low_y = read_plane(from_low_y, 64) * low_y
    for copy in copies[:4]:
        copy.wait()
    for k in range(3):
        m_low_x = read_plane(from_low_x, 16 * k)
        m_high_x = read_plane(from_high_x, 16 * k)
        m_low_y = read_plane(from_low_y, 16 * k)
        m_high_y = read_plane(from_high_y, 16 * k)
        previous = t_low_x * 0.5 * (m_low_x + mobility[k, 0])
        face_x[k, 0] = previous
        planes = [mobility[k, x] for x in range(8)]
        for x in range(8):
            here = planes[x]
            around = neighbours(planes, x, m_low_x, m_high_x, m_low_y, m_high_y)
            tx = trans_x[x] if x < 7 else trans_x[x] * high_x
            ahead = tx * 0.5 * (here + around[0])
            face_x[k, x + 1] = ahead
            total = ahead + previous
            previous = ahead
            ty = jnp.where(line == 7, trans_y[x] * high_y, trans_y[x])
            ahead_y = ty * 0.5 * (here + around[2])
            entering = t_low_y[x : x + 1] * 0.5 * (m_low_y[x : x + 1] + here[0:1])
            behind_y = jnp.where(line == 0, entering, pltpu.roll(ahead_y, 1, 0))
            face_y[0, k, x] = ahead_y
            face_y[1, k, x] = behind_y
            total = total + (ahead_y + behind_y)
            ahead_z = jnp.where(lane < 255, trans_z[x] * 0.5 * (here + around[4]), 0.0)
            face_z[k, x] = ahead_z
            total = total + (ahead_z + pltpu.roll(ahead_z, 1, 1))
            diagonal[k, x] = total + here * density[x * 8 : x * 8 + 8, :]

    def summed(face, *place):
        return face[0, *place] + face[1, *place] + face[2, *place]

    edges[0] = summed(face_x, 8)
    edges[1] = summed(face_x, 0)
    edges[2] = face_y[0, 0, :, 7, :] + face_y[0, 1, :, 7, :] + face_y[0, 2, :, 7, :]
    edges[3] = face_y[1, 0, :, 0, :] + face_y[1, 1, :, 0, :] + face_y[1, 2, :, 0, :]
    halo = (
        read_plane(from_low_x, 48),
        read_plane(from_high_x, 48),
        read_plane(from_low_y, 48),
        read_plane(from_high_y, 48),
    )
    for copy in copies[4:]:
        copy.wait()
    planes = [state[0, x] for x in range(8)]
    for x in range(8):
        up_z = summed(face_z, x)
        kept = up_z + pltpu.roll(up_z, 1, 1)
        kept = kept + jnp.where(line < 7, summed(face_y.at[0], x), 0.0)
        kept = kept + jnp.where(line > 0, summed(face_y.at[1], x), 0.0)
        if x < 7:
            kept = kept + summed(face_x, x + 1)
        if x > 0:
            kept = kept + summed(face_x, x)
        inner[x] = kept
        around = neighbours(planes, x, *halo)
        source = pulled[x * 8 : x * 8 + 8, :] + back[x * 8 : x * 8 + 8]
        for k in range(3):
            value = (
                gathered((face_x, face_y, face_z), k, x, planes[x], around)
                + mobility[k, x] * source
                - diagonal[k, x] * planes[x]
            )
            right[k, x] = value
        slopes = []
        for k in range(3):
            bent = jnp.tanh(state[k, x])
            slopes.append(1.5 - 0.5 * bent * bent)
        invert(slopes, acc_diag, porosity, [diagonal[k, x] for k in range(3)], x, inverse)


def shares(per_block, hole):
    share = per_block[0] * hole[0:1]
    for a in range(1, 4):
        share = share + per_block[a] * hole[a : a + 1]
    return jnp.sum(share, 1, keepdims=True)


def open_wells_body(arrived, coarse, divisor, per_block, hole, tile):
    totals = jnp.zeros((8, 128), F32)
    others = jnp.zeros((8, 128), F32)
    for other in range(COLS):
        totals = totals + arrived[other, 0:8, :]
        others = others + arrived[other, 8:16, :]
    blocks = [arrived[:, a, :] for a in range(4)]
    for a in range(4):
        per_block[a] = blocks[a]
    upper = iota((8, 128), 0) < 4
    div = jnp.where(upper, totals + pltpu.roll(others, 4, 0), 1.0)
    divisor[...] = div
    found = jnp.where(upper, others, 0.0) / div
    hole[...] = found
    share = shares(blocks, found) + arrived[:, 4, 0:1]
    tile[0:32, :] = jnp.where(iota((COLS, 128), 1) == 0, share * -1.0, 0.0)
    tile[32:64, :] = coarse[...]


def find_direction(stored, coarse_x, *refs):
    (
        vector,
        mobility,
        face_x,
        face_y,
        face_z,
        inner,
        edges,
        inverse,
        divisor,
        per_block,
        *refs,
    ) = refs
    if stored:
        layer, place, low_mark, high_mark, index, *refs = refs
        marks = (layer[...], place[...], low_mark[...], high_mark[...])
    else:
        cell, label, index, *refs = refs
        marks = marks_of(cell, label)
    (
        direction_out,
        to_high,
        to_low,
        outgoing,
        swept,
        level,
        direction,
        for_wells,
        for_sides,
        sems,
    ) = refs
    row = lax.axis_index("row")
    col = lax.axis_index("col")
    faces = (face_x, face_y, face_z)

    def wide(at_row, at_col):
        place = at_col * ROWS + at_row
        value = coarse_x[pl.ds(place, 1), :]
        return jnp.broadcast_to(jnp.concatenate([value, value], 1), (8, 256))

    own = wide(row, col)
    x_high = wide(jnp.minimum(row + 1, ROWS - 1), col)
    x_low = wide(jnp.maximum(row - 1, 0), col)
    y_high = wide(row, jnp.minimum(col + 1, COLS - 1))
    y_low = wide(row, jnp.maximum(col - 1, 0))
    level[...] = own[:, :128]
    weights = coarse_x[pl.ds(row, COLS, stride=ROWS), :]
    sums = [jnp.sum(weights * per_block[a], 0, keepdims=True) for a in range(4)]
    sums = jnp.concatenate([*sums, jnp.zeros((4, 128), F32)], 0)
    back = to_cells(sums / divisor[...], index, marks)
    line = iota((8, 256), 0)
    up_y = jnp.where(line == 7, y_high, own)
    down_y = jnp.where(line == 0, y_low, own)
    weighted = []
    inside = jnp.zeros((8, 256), F32)
    for x in range(8):
        around = (own if x < 7 else x_high, own if x > 0 else x_low, up_y, down_y, own)
        terms = [
            vector[k, x] + gathered(faces, k, x, own, around) + mobility[k, x] * back[x * 8 : x * 8 + 8]
            for k in range(3)
        ]
        for k in range(3):
            value = (
                inverse[k, 0, x] * terms[0]
                + inverse[k, 1, x] * terms[1]
                + inverse[k, 2, x] * terms[2]
            )
            if k == 0:
                kept = value - own
                swept[x] = kept
            else:
                direction[k - 1, x] = value
        inside = inside + kept * inner[x]
        weighted.append(kept * (mobility[0, x] + mobility[1, x] + mobility[2, x]))
    to_high[...] = swept[7]
    to_low[...] = swept[0]
    last = swept[:, 7, :]
    first = swept[:, 0, :]
    for other in range(COLS):
        send = jnp.where(other < col, first, last)
        for_sides[other, 0:8, :] = send[:, :128]
        for_sides[other, 8:16, :] = send[:, 128:]
    side_copy = pltpu.make_async_copy(for_sides, outgoing.at[:, 8:24, :], sems.at[0])
    side_copy.start()
    direction_copy = pltpu.make_async_copy(direction, direction_out, sems.at[2])
    direction_copy.start()
    local = to_wells(jnp.concatenate(weighted, 0), index, marks)
    sides = (swept[7] * edges[0], swept[0] * edges[1], last * edges[2], first * edges[3])
    lane = iota((8, 128), 1)
    for n, term in enumerate((inside, *sides)):
        local = jnp.where((iota((8, 128), 0) == 4) & (lane == n), total_of(term), local)
    for other in range(COLS):
        for_wells[other] = local
    well_copy = pltpu.make_async_copy(for_wells, outgoing.at[:, 0:8, :], sems.at[1])
    well_copy.start()
    direction_copy.wait()
    side_copy.wait()
    well_copy.wait()


def coarse_product(solve, means):
    parts = split(solve)
    high = means.astype(BF16)
    low = (means - high.astype(F32)).astype(BF16)
    return joined(nn(parts, high)) + nn(parts[:DEVS], low)


def coarse_solve(solve, means, ordered, coarse_x):
    for r in range(ROWS):
        ordered[pl.ds(r, COLS, stride=ROWS), :] = means[r * COLS : (r + 1) * COLS, :]
    coarse_x[...] = coarse_product(solve[...], ordered[...])


def direction_body(solve, received, *rest):
    *rest, coarse_x = rest
    coarse_x[...] = coarse_product(solve[...], received[...])
    find_direction(False, coarse_x, *rest)


def place_rows(sources, target, base):
    for shift, source in enumerate(sources):
        start = pl.multiple_of(((lax.axis_index("row") - shift + ROWS) % ROWS) * COLS, COLS)
        target[pl.ds(start, COLS), :] = source[base : base + COLS, :]


def from_rows(solve, sources, rest, opening):
    *rest, ordered, coarse_x = rest
    place_rows(sources, coarse_x, 0)
    every = coarse_x[...]
    means = every[:, 0:1]
    if not opening:
        means = means + pltpu.roll(every, COLS, 0)[:, 1:2]
        means = means + pltpu.roll(every, DEVS - COLS, 0)[:, 2:3]
    means = jnp.broadcast_to(means * (-1.0 / CELLS), (DEVS, 128))
    coarse_solve(solve, means, ordered, coarse_x)
    find_direction(True, coarse_x, *rest)


def gathered_direction_body(solve, own, low, far, high, *rest):
    from_rows(solve, (own, low, far, high), rest, False)


def opening_direction_body(own, low, far, high, *rest):
    *rest, solve, direction, for_wells, for_sides, sems, ordered, coarse_x = rest
    place_rows((own, low, far, high), solve, COLS)
    rest = (*rest, direction, for_wells, for_sides, sems, ordered, coarse_x)
    from_rows(solve, (own, low, far, high), rest, True)


def sum_wells_body(came, divisor, per_block, hole, tile):
    sums = jnp.zeros((8, 128), F32)
    for other in range(COLS):
        sums = sums + came[other, 0:8, :]
    found = jnp.where(iota((8, 128), 0) < 4, sums, 0.0) / divisor[...]
    hole[...] = found
    if tile is not None:
        pieces = came[:, 4, :]
        share = shares(per_block, found) + pieces[:, 0:1]
        share = share + pltpu.roll(pieces, 1, 0)[:, 3:4] + pltpu.roll(pieces, COLS - 1, 0)[:, 4:5]
        tile[...] = jnp.where(iota((COLS, 128), 1) == 0, share, pieces)


def close_wells_body(came, divisor, per_block, from_low, from_high, hole, tile):
    sum_wells_body(came, divisor, per_block, hole, tile)


def coupling_planes(
    hole,
    swept,
    from_low,
    from_high,
    came,
    mobility,
    face_x,
    face_y,
    face_z,
    cell,
    label,
    index,
    kept=(),
):
    col = lax.axis_index("col")
    faces = (face_x, face_y, face_z)
    marks = marks_of(cell, label)
    keep(marks, kept)
    back = to_cells(hole[...], index, marks)
    below = jnp.maximum(col - 1, 0)
    above = jnp.minimum(col + 1, COLS - 1)
    y_low = jnp.concatenate([came[below, 8:16, :], came[below, 16:24, :]], 1)
    y_high = jnp.concatenate([came[above, 8:16, :], came[above, 16:24, :]], 1)
    planes = [swept[x] for x in range(8)]
    for x in range(8):
        around = neighbours(planes, x, from_low[...], from_high[...], y_low, y_high)
        for k in range(3):
            value = gathered(faces, k, x, planes[x], around)
            yield k, x, value + mobility[k, x] * back[x * 8 : x * 8 + 8]


def first_image_body(*rest):
    *rest, tied, layer, place, low_mark, high_mark = rest
    for k, x, value in coupling_planes(*rest, kept=(layer, place, low_mark, high_mark)):
        tied[k, x] = -value


def second_image_body(divisor, right, tied, *rest):
    *rest, image, outgoing, hole = rest
    sum_wells_body(rest[3], divisor, None, hole, None)
    totals = [jnp.zeros((8, 256), F32) for _ in range(5)]
    for k, x, value in coupling_planes(hole, *rest):
        value = tied[k, x] - value
        image[k, x] = value
        goal = right[k, x]
        one = goal + tied[k, x]
        for n, term in enumerate((one * one, one * value, value * value, one * goal, value * goal)):
            totals[n] = totals[n] + term
    broadcast_rows(outgoing, jnp.zeros((1, 1), F32), [total_of(t) for t in totals])


def update_body(last, *refs):
    (
        met,
        current,
        acc_diag,
        porosity,
        right,
        tied,
        image,
        first_swept,
        first_level,
        first_direction,
        second_swept,
        second_level,
        second_direction,
        *outs,
    ) = refs
    sums = jnp.sum(met[...], 0, keepdims=True)
    g00, g01, g11, t0, t1 = [sums[:, 127 - n : 128 - n] for n in range(5)]
    l00 = jnp.sqrt(g00)
    l10 = g01 / l00
    l11 = jnp.sqrt(g11 - l10 * l10)
    f0 = t0 / l00
    f1 = (t1 - l10 * f0) / l11
    y1 = f1 / l11
    y0 = (f0 - l10 * y1) / l00
    shift = y0 * first_level[0:1, 0:1] + y1 * second_level[0:1, 0:1]
    if last:
        fresh, residual = outs
    else:
        mobility, face_x, face_y, face_z, density, fresh, residual, inverse, outgoing = outs
    mean = jnp.zeros((8, 256), F32)
    for x in range(8):
        remainder = []
        slopes = []
        for k in range(3):
            old = current[k, x]
            if k == 0:
                step = y0 * first_swept[x] + y1 * second_swept[x] + shift
            else:
                step = y0 * first_direction[k - 1, x] + y1 * second_direction[k - 1, x]
            new = old + step
            fresh[k, x] = new
            before = jnp.tanh(old)
            after = jnp.tanh(new)
            remainder.append(0.5 * ((after - before) - (1.0 - before * before) * step))
            slopes.append(1.5 - 0.5 * after * after)
        for k in range(3):
            goal = right[k, x]
            value = (
                goal
                - y0 * (goal + tied[k, x])
                - y1 * image[k, x]
                - coupled(acc_diag, porosity, k, x, remainder)
            )
            residual[k, x] = -value if last else value
            mean = mean + value
        if not last:
            diagonal = []
            for k in range(3):
                total = face_x[k, x + 1] + face_x[k, x] + (face_y[0, k, x] + face_y[1, k, x])
                total = total + (face_z[k, x] + pltpu.roll(face_z[k, x], 1, 1))
                diagonal.append(total + mobility[k, x] * density[x * 8 : x * 8 + 8, :])
            invert(slopes, acc_diag, porosity, diagonal, x, inverse)
    if not last:
        broadcast_rows(outgoing, total_of(mean) * (1.0 / CELLS))


def per_device(
    state,
    acc_diag,
    porosity,
    mobility,
    trans_x,
    trans_y,
    trans_z,
    perf_cell,
    perf_owner,
    perf_well,
    perf_index,
    perf_head,
    well_stiff,
    well_drive,
    coarse_inverse,
):
    field = (8, 8, 256)
    triple = (3, *field)
    plane = (8, 256)
    count = perf_cell.shape[1]

    def ring(value, axis, count, shift):
        return lax.ppermute(value, axis, [(i, (i + shift) % count) for i in range(count)])

    def swap_cols(value):
        return lax.all_to_all(value, "col", 0, 0, tiled=True)

    def swap_all(value):
        return lax.all_to_all(value, ("col", "row"), 0, 0, tiled=True)

    def exchange(to_high, to_low, outgoing):
        return (
            ring(to_high, "row", ROWS, 1),
            ring(to_low, "row", ROWS, -1),
            swap_cols(outgoing),
        )

    vmem = pl.BlockSpec(memory_space=pltpu.VMEM)
    hbm = pl.BlockSpec(memory_space=pltpu.HBM)

    def run(body, outs, *args, scratch=(), far=(), far_outs=(), room=ROOM):
        specs = [hbm if n in far else vmem for n in range(len(args))]
        return pl.pallas_call(
            body,
            out_shape=[
                pltpu.HBM(s, t) if n in far_outs else jax.ShapeDtypeStruct(s, t)
                for n, (s, t) in enumerate(outs)
            ],
            in_specs=specs,
            out_specs=[hbm if n in far_outs else vmem for n in range(len(outs))],
            scratch_shapes=list(scratch),
            compiler_params=pltpu.CompilerParams(vmem_limit_bytes=room),
        )(
            *(
                pltpu.with_memory_space_constraint(arg, pltpu.HBM) if n in far else arg
                for n, arg in enumerate(args)
            )
        )

    def buffers(*values):
        return [pltpu.VMEM(value.shape, value.dtype) for value in values]

    line = (1, count)
    packs = run(
        pack_body,
        [((80, 128), F32), ((64, 128), F32), ((80, 128), F32), ((64, 128), F32)],
        state,
        mobility,
        trans_x,
        trans_y,
        scratch=[
            pltpu.VMEM(field, F32),
            pltpu.VMEM(triple, F32),
            pltpu.VMEM(plane, F32),
            pltpu.VMEM(field, F32),
            pltpu.SemaphoreType.DMA((4,)),
        ],
        far=range(4),
        room=FIRST_ROOM,
    )
    up_x, down_x, up_y, down_y = packs
    halos = (
        ring(up_x, "row", ROWS, 1),
        ring(down_x, "row", ROWS, -1),
        ring(up_y, "col", COLS, 1),
        ring(down_y, "col", COLS, -1),
    )
    cell, label, index, density, pulled, sums = run(
        prepare_body,
        [
            (line, jnp.int32),
            (line, jnp.int32),
            (line, F32),
            ((64, 256), F32),
            ((64, 256), F32),
            ((16, 128), F32),
        ],
        state,
        mobility,
        perf_cell,
        perf_owner,
        perf_well,
        perf_index,
        perf_head,
        well_stiff,
        well_drive,
        scratch=[
            pltpu.VMEM(field, F32),
            pltpu.VMEM(triple, F32),
            *buffers(perf_owner, perf_well, perf_head, well_stiff, well_drive),
            pltpu.SemaphoreType.DMA((9,)),
        ],
        far=range(9),
    )
    marks = (cell, label, index)
    (outgoing,) = run(border_body, [((COLS, 16, 128), F32)], *packs, *halos, sums)
    well_tile = (8, 128)
    divisor, per_block, hole, tile = run(
        open_wells_body,
        [(well_tile, F32), ((4, COLS, 128), F32), (well_tile, F32), ((2 * COLS, 128), F32)],
        swap_cols(outgoing),
        coarse_inverse,
    )
    one_hots = [((256, count), BF16), ((64, count), F32), ((128, count), BF16), ((8, count), F32)]
    face_x, face_y, face_z, inner, edges, inverse, right, *stored = run(
        start_body,
        [
            ((3, 9, *plane), F32),
            ((2, *triple), F32),
            (triple, F32),
            (field, F32),
            ((4, *plane), F32),
            ((3, *triple), F32),
            (triple, F32),
            *one_hots,
        ],
        state,
        acc_diag,
        porosity,
        mobility,
        trans_x,
        trans_y,
        trans_z,
        *halos,
        density,
        pulled,
        hole,
        *marks,
        scratch=[
            *buffers(state, acc_diag, porosity, mobility, trans_x, trans_y, trans_z),
            pltpu.VMEM(triple, F32),
            pltpu.SemaphoreType.DMA((7,)),
        ],
        far=range(7),
    )
    faces = (face_x, face_y, face_z)
    current = state
    solve = None
    sends = [((2, *field), F32), (plane, F32), (plane, F32), ((COLS, 24, 128), F32)]
    sends += [(field, F32), (well_tile, F32)]
    send_scratch = [
        pltpu.VMEM((2, *field), F32),
        pltpu.VMEM((COLS, 8, 128), F32),
        pltpu.VMEM((COLS, 16, 128), F32),
        pltpu.SemaphoreType.DMA((3,)),
    ]
    coarse_scratch = [pltpu.VMEM((DEVS, 128), F32)] * 2

    def spread_rows(tile):
        return (tile, *(ring(tile, "row", ROWS, shift) for shift in (1, 2, 3)))

    for outer in range(NEWTON):
        static = (mobility, *faces, inner, edges, inverse, divisor, per_block)
        if outer == 0:
            first_direction, to_high, to_low, outgoing, first_swept, first_level, solve = run(
                opening_direction_body,
                [*sends, ((DEVS, DEVS), F32)],
                *spread_rows(tile),
                right,
                *static,
                *stored,
                index,
                scratch=[*send_scratch, *coarse_scratch],
                far_outs=(0, 3),
            )
        else:
            first_direction, to_high, to_low, outgoing, first_swept, first_level = run(
                direction_body,
                sends,
                solve,
                swap_all(outgoing),
                right,
                *static,
                *marks,
                scratch=[*send_scratch, coarse_scratch[0]],
                far_outs=(0, 3),
            )
        from_low, from_high, came = exchange(to_high, to_low, outgoing)
        hole, tile = run(
            close_wells_body,
            [(well_tile, F32), ((COLS, 128), F32)],
            came,
            divisor,
            per_block,
            from_low,
            from_high,
        )
        tied, *stored = run(
            first_image_body,
            [(triple, F32), *one_hots],
            hole,
            first_swept,
            from_low,
            from_high,
            came,
            mobility,
            *faces,
            *marks,
        )
        second_direction, to_high, to_low, outgoing, second_swept, second_level = run(
            gathered_direction_body,
            sends,
            solve,
            *spread_rows(tile),
            tied,
            *static,
            *stored,
            index,
            scratch=[*send_scratch, *coarse_scratch],
            far_outs=(0, 3),
        )
        image, outgoing = run(
            second_image_body,
            [(triple, F32), ((DEVS, 128), F32)],
            divisor,
            right,
            tied,
            second_swept,
            *exchange(to_high, to_low, outgoing),
            mobility,
            *faces,
            *marks,
            scratch=[pltpu.VMEM(well_tile, F32)],
        )
        met = swap_all(outgoing)
        last = outer == NEWTON - 1
        outs = [(triple, F32), (triple, F32)]
        extra = ()
        if not last:
            outs += [((3, *triple), F32), ((DEVS, 128), F32)]
            extra = (mobility, *faces, density)
        results = run(
            lambda *refs: update_body(last, *refs),
            outs,
            met,
            current,
            acc_diag,
            porosity,
            right,
            tied,
            image,
            first_swept,
            first_level,
            first_direction,
            second_swept,
            second_level,
            second_direction,
            *extra,
        )
        if last:
            return tuple(results)
        current, right, inverse, outgoing = results


def solution(mesh):
    in_specs = (
        P(None, "row", "col", None),
        P(None, "row", "col", None),
        P("row", "col", None),
        P(None, "row", "col", None),
        P("row", "col", None),
        P("row", "col", None),
        P("row", "col", None),
        P("row", "col"),
        P("row", "col"),
        P("row", "col"),
        P("row", "col"),
        P("row", "col"),
        P("row", "col"),
        P("row", "col"),
        P("row", None),
    )
    out_specs = (P(None, "row", "col", None), P(None, "row", "col", None))
    return jax.shard_map(
        per_device, mesh=mesh, in_specs=in_specs, out_specs=out_specs, check_vma=False
    )
```
